32 devices in a mesh: tile: 8 (over z, x), trace: 4 (over y, core).
Axes of the slice: x: 2, y: 2, z: 4, core: 2. Of those that a mesh axis runs over, the one named last changes fastest.
Arguments:
- traces: bfloat16 [4, 128, 32, 256], P('trace', 'tile'), may hold values from -6 to 6
- taps: bfloat16 [2, 65], replicated, may hold values from -0.75 to 0.75
- aperture: int32 [4, 8, 128], P('trace'), may hold values from 0 to 127, as said below
- counts: int32 [4, 8], P('trace'), may hold values from 32 to 128, as said below
- time_weights: bfloat16 [4, 8, 128, 128, 256], P('trace', 'tile'), may hold values from -0.375 to 0.375
- amplitudes: bfloat16 [4, 8, 128, 2, 32, 256], P('trace', 'tile'), may hold values from -0.0625 to 0.0625
Outputs:
- image: float32 [8, 128, 256], P('tile', 'trace')
The draws below stay inside these ranges and needn't reach their ends.
Inputs may be any that keep to these rules, and one draw needn't show every extreme that they name: `aperture`: entries of one list are distinct ids of the subset's blocks; they come in runs of 16 consecutive entries whose ids share the owner index id // 16, and no owner index appears in more than one run of a list. `counts`: some list uses all 128 entries and some uses 128 // 4.
All inputs are finite; a program needn't handle non-finite values.
Results may differ from the reference program's by a relative error of at most 0.0041.
Values may be sent and summed in bfloat16 or wider, within the bound.
A program may use at most 64 MiB of HBM per device.

```python
import jax
import jax.numpy as jnp
from jax import lax

NS = 256
NTAU = 128
TAPS = 65
TRACE_BLK = 32
BLK_DEV = 16
SLOTS = 128
COLS = 256
HALF = 32
TILES = 8
SUBSETS = 4
BLOCKS = 128
CAP = 16


def draw_counts(key, part):
    key_values, key_upper, key_lower = jax.random.split(key, 3)
    entries = SUBSETS * TILES
    values = jax.random.randint(key_values, (entries,), SLOTS // 4, SLOTS + 1)
    upper = jax.random.randint(key_upper, (), 0, entries)
    lower = (upper + 1 + jax.random.randint(key_lower, (), 0, entries - 1)) % entries
    values = values.at[upper].set(SLOTS).at[lower].set(SLOTS // 4)
    return values.reshape(SUBSETS, TILES).astype(jnp.int32)


def permute_tiles(subkey):
    return jax.random.permutation(subkey, TILES)


def permute_blocks(subkey):
    return jax.random.permutation(subkey, BLK_DEV)


def draw_aperture(key, part):
    list_count = SUBSETS * TILES
    run_count = SLOTS // CAP
    owner_keys = jax.random.split(jax.random.fold_in(key, 11), list_count)
    owners = jax.vmap(permute_tiles)(owner_keys)[:, :run_count]
    within_keys = jax.random.split(jax.random.fold_in(key, 23), list_count * run_count)
    within = jax.vmap(permute_blocks)(within_keys)[:, :CAP].reshape(list_count, SLOTS)
    slot_owner = jnp.repeat(owners, CAP, axis=1)
    return (slot_owner * BLK_DEV + within).reshape(SUBSETS, TILES, SLOTS).astype(jnp.int32)


def shard_levels(rng, extent, shards, smallest, top_value):
    def one(axis_at, shards_of):
        steps = jax.random.uniform(jax.random.fold_in(jax.random.fold_in(rng, 6), axis_at), (shards_of,), jnp.float32, smallest / len(shards), top_value / len(shards))
        return jnp.repeat(jnp.exp(steps), extent[axis_at] // shards_of).reshape((-1,) + (1,) * (len(extent) - axis_at - 1))

    factor_of = one(*shards[0])
    for cut in shards[1:]:
        factor_of = factor_of * one(*cut)
    return factor_of


def normal_values(rng, dims, scale, bound, shards=(), dtype=jnp.bfloat16):
    drawn = jax.random.normal(rng, dims, jnp.float32) * scale
    if len(shards) > 0:
        drawn = shard_levels(rng, dims, shards, -0.22, 0.18) * drawn
    return jnp.clip(drawn, min=-bound, max=bound).astype(dtype)


def setup_inputs(seed: int = 0) -> dict:
    streams_of = jax.random.split(jax.random.key(seed), 7)
    return {
        "traces": normal_values(streams_of[0], (SUBSETS, BLOCKS, TRACE_BLK, NS), 1.0, 6.0, ((0, 4), (1, 8))),
        "taps": normal_values(streams_of[1], (2, TAPS), TAPS ** -0.5, 0.75),
        "aperture": draw_aperture(jax.random.fold_in(streams_of[6], 71), 0),
        "counts": draw_counts(jax.random.fold_in(streams_of[6], 71), 0),
        "time_weights": normal_values(streams_of[4], (SUBSETS, TILES, SLOTS, NTAU, NS), NS ** -0.5, 0.375, ((0, 4), (1, 8))),
        "amplitudes": normal_values(streams_of[5], (SUBSETS, TILES, SLOTS, 2, TRACE_BLK, COLS), (2 * TRACE_BLK * SLOTS) ** -0.5, 0.0625, ((0, 4), (1, 8))),
    }


def filter_matrix(taps):
    offset = jnp.arange(NS)[:, None] - jnp.arange(NS)[None, :] + HALF
    inside = (offset >= 0) & (offset < TAPS)
    picked = jnp.take(taps, jnp.clip(offset, 0, TAPS - 1).astype(jnp.int32), axis=1)
    return jnp.where(inside[None], picked, jnp.zeros_like(picked))


def reference(traces, taps, aperture, counts, time_weights, amplitudes):
    operator = filter_matrix(taps).astype(jnp.float32)
    image = jnp.zeros((TILES, NTAU, COLS), jnp.float32)
    for subset in range(SUBSETS):
        filtered = jnp.einsum('cnm,kbm->kcbn', operator, traces[subset].astype(jnp.float32)).astype(jnp.bfloat16)

        def one_tile(packed):
            listing, filled, weights, spread = packed
            blocks = jnp.take(filtered, listing, axis=0).astype(jnp.float32)
            alive = (jnp.arange(SLOTS) < filled).astype(jnp.float32)
            interp = jnp.einsum('stn,scbn->scbt', weights.astype(jnp.float32), blocks) * alive[:, None, None, None]
            interp = lax.optimization_barrier(interp.astype(jnp.bfloat16)).astype(jnp.float32)
            return jnp.einsum('scbt,scbp->tp', interp, spread.astype(jnp.float32))

        image = image + lax.map(one_tile, (aperture[subset], counts[subset], time_weights[subset], amplitudes[subset]))
    return image
```

```python
import jax
import jax.numpy as jnp
from jax import lax
from jax.experimental import pallas as pl
from jax.experimental.pallas import tpu as pltpu
from jax.sharding import PartitionSpec as P

group_slots = 8
quarters = 4
rows_z = 4
events = 14
MESH = pl.DeviceIdType.MESH


def migrate_kernel(
    counts_hbm,
    aperture_hbm,
    taps_hbm,
    traces_ref,
    weights_ref,
    spread_ref,
    out_ref,
    gathered,
    weights,
    spread,
    operator,
    total,
    outgoing,
    parts,
    counts_ref,
    aperture_ref,
    taps_ref,
    band,
    lookup,
    slot_of,
    recv_sem,
    send_sem,
    load_sem,
    part_send_sem,
    part_recv_sem,
):
    tile = lax.axis_index("tile")
    subset = lax.axis_index("trace")
    z = tile // 2
    x = tile % 2
    other = 1 - x
    low = z < rows_z // 2
    inward = jnp.where(low, 1, -1)
    place = jnp.where(low, z, rows_z - 1 - z)
    end = place == 0
    middle = place == 1
    samples = operator.shape[1]
    taus = weights.shape[1]
    block_rows = spread.shape[2]
    chunk_rows = gathered.shape[2]
    chunk_blocks = chunk_rows // block_rows
    block_count = chunk_blocks * quarters
    share = out_ref.shape[0]

    load_small = [
        pltpu.make_async_copy(src, dst, load_sem.at[4 + at])
        for at, (src, dst) in enumerate(
            ((counts_hbm, counts_ref), (aperture_hbm, aperture_ref), (taps_hbm, taps_ref))
        )
    ]
    load_own = pltpu.make_async_copy(traces_ref, gathered.at[tile], load_sem.at[0])
    load_weights = pltpu.make_async_copy(weights_ref, weights, load_sem.at[1])
    load_spread = pltpu.make_async_copy(spread_ref, spread, load_sem.at[2])

    row_y = subset // 2
    core = subset % 2
    across_y = (1 - row_y) * 2
    peers = (across_y + core, across_y + 1 - core, row_y * 2 + 1 - core)

    barrier = pltpu.get_barrier_semaphore()
    neighbours = {
        "x": z * 2 + other,
        "in": tile + 2 * inward,
        "out": tile - 2 * inward,
    }

    def greet(to_tile, to_subset):
        pl.semaphore_signal(barrier, inc=1, device_id=(to_tile, to_subset), device_id_type=MESH)

    greet(neighbours["in"], subset)
    greet(neighbours["x"], subset)

    @pl.when(middle)
    def _():
        greet(neighbours["out"], subset)

    for peer in peers:
        greet(tile, peer)
    for load in load_small:
        load.start()
    load_own.start()
    pl.semaphore_wait(barrier, 5 + jnp.where(middle, 1, 0))

    def send(way, origin, quarter, own=False):
        return pltpu.make_async_remote_copy(
            src_ref=traces_ref.at[quarter] if own else gathered.at[origin, quarter],
            dst_ref=gathered.at[origin, quarter],
            send_sem=send_sem.at[("x", "in", "out").index(way), origin, quarter],
            recv_sem=recv_sem.at[origin, quarter],
            device_id=(neighbours[way], subset),
            device_id_type=MESH,
        )

    def wait_arrival(origin, quarter):
        pltpu.make_async_remote_copy(
            src_ref=gathered.at[origin, quarter],
            dst_ref=gathered.at[origin, quarter],
            send_sem=send_sem.at[0, 0, 0],
            recv_sem=recv_sem.at[origin, quarter],
            device_id=(neighbours["x"], subset),
            device_id_type=MESH,
        ).wait_recv()

    for quarter in range(quarters):
        send("in", tile, quarter, True).start()

        @pl.when(middle)
        def _():
            send("out", tile, quarter, True).start()

        send("x", tile, quarter, True).start()

    load_weights.start()
    load_spread.start()
    for load in load_small:
        load.wait()
    slots = weights.shape[0]
    listing = aperture_ref[0, pl.ds(tile, 1), :]
    slot = lax.broadcasted_iota(jnp.int32, (slots, slots), 0)
    block = lax.broadcasted_iota(jnp.int32, (slots, slots), 1)
    named = jnp.broadcast_to(listing, (slots, slots)).T
    match = (named == block) & (slot < counts_ref[0, tile])
    lookup[...] = jnp.broadcast_to(
        jnp.sum(jnp.where(match, slot + 1, 0), axis=0, keepdims=True) - 1, lookup.shape
    )
    publish = pltpu.make_async_copy(lookup, slot_of, load_sem.at[3])
    publish.start()

    half_taps = (taps_ref.shape[1] - 1) // 2
    band[...] = jnp.zeros_like(band)
    band[0:2, 0 : taps_ref.shape[1]] = taps_ref[...].astype(jnp.float32)
    row = lax.broadcasted_iota(jnp.int32, (samples, samples), 0)
    gap = lax.broadcasted_iota(jnp.int32, (samples, samples), 1) - row
    inside = (gap <= half_taps) & (gap >= -half_taps)
    for channel in range(2):
        centred = pltpu.roll(band[...], samples - half_taps, 1)[channel : channel + 1, :]
        shifted = jnp.broadcast_to(centred, (samples, samples))
        shift = 1
        while shift < samples:
            shifted = jnp.where((row // shift) % 2 == 1, pltpu.roll(shifted, shift, 1), shifted)
            shift *= 2
        operator[channel * samples : (channel + 1) * samples, :] = (
            jnp.where(inside, shifted, 0.0).T
        ).astype(operator.dtype)
    total[...] = jnp.zeros_like(total)

    def tile_at(position, column):
        return jnp.where(low, position, rows_z - 1 - position) * 2 + jnp.where(
            column == 0, x, other
        )

    def arrival(event, side):
        if side == 0:
            late = event >= 12
            end_column = jnp.where(late, 1, 0)
            end_position = jnp.where(late, 3, 1 + event // 4)
            end_quarter = jnp.where(late, event - 10, event % 4)
            end_x = event < 10
            end_in = event < 0
        else:
            end_column = 1
            end_position = event // 4
            end_quarter = event % 4
            end_x = event < 0
            end_in = event < 4
        number = 2 * event + side
        turn = number < 24
        stream = jnp.where(turn, number % 3, 2)
        index = jnp.where(turn, number // 3, number - 16)
        from_end = stream == 0
        from_middle = stream == 1
        from_x = stream == 2
        column = jnp.where(from_x | (from_end & (index >= 4)), 1, 0)
        position = jnp.where(from_end, 0, jnp.where(from_middle, 2, 1) + index // 4)
        quarter = jnp.where(from_x & (index >= 9), 1 + (index - 8) % 3, index % 4)
        mid_x = from_middle & (index != 5)
        mid_in = from_end & (index < 4)
        mid_out = from_middle | (from_x & ((index == 9) | (index == 10)))
        origin = tile_at(
            jnp.where(end, end_position, position), jnp.where(end, end_column, column)
        )
        ways = {
            "x": (end & end_x) | (middle & mid_x),
            "in": (end & end_in) | (middle & mid_in),
            "out": middle & mid_out,
        }
        postponed = middle & from_middle & (index == 7)
        return origin, jnp.where(end, end_quarter, quarter), ways, postponed

    def each_way(event, side, act):
        origin, quarter, ways, postponed = arrival(event, side)
        for way in ("out", "in", "x"):

            @pl.when(ways[way])
            def _():
                act(send(way, origin, quarter))

        @pl.when(postponed)
        def _():
            act(send("x", origin, 1))

    def take(event):
        for side in range(2):
            origin, quarter, _, _ = arrival(event, side)
            wait_arrival(origin, quarter)
            each_way(event, side, lambda copy: copy.start())

    lanes = lax.broadcasted_iota(jnp.int32, (1, 2 * chunk_rows), 1)
    member = (lanes // block_rows) % chunk_blocks

    def compute(chunks):
        rows = jnp.concatenate([gathered[origin, quarter] for origin, quarter in chunks], axis=0)
        filtered = lax.dot_general(
            operator[...], rows, (((1,), (1,)), ((), ())), preferred_element_type=jnp.float32
        ).astype(jnp.bfloat16)
        image = None
        for at, (origin, quarter) in enumerate(chunks):
            first = at * chunk_rows
            blocks = jnp.concatenate(
                [
                    filtered[0:samples, first : first + chunk_rows],
                    filtered[samples : 2 * samples, first : first + chunk_rows],
                ],
                axis=1,
            )
            base = origin * block_count + quarter * chunk_blocks
            found = [slot_of[0, base + index] for index in range(chunk_blocks)]
            picks = [jnp.maximum(value, 0) for value in found]
            gains = [jnp.where(value >= 0, 1.0, 0.0) for value in found]
            stacked = jnp.concatenate([weights[pick] for pick in picks], axis=0)
            product = jnp.dot(stacked, blocks, preferred_element_type=jnp.float32)
            interp = product[0:taus]
            alive = jnp.full((1, 2 * chunk_rows), gains[0], jnp.float32)
            for index in range(1, chunk_blocks):
                here = member == index
                interp = jnp.where(here, product[index * taus : (index + 1) * taus], interp)
                alive = jnp.where(here, gains[index], alive)
            interp = (interp * alive).astype(jnp.bfloat16)
            columns = jnp.concatenate(
                [spread[pick, channel] for channel in range(2) for pick in picks], axis=0
            )
            part = jnp.dot(interp, columns, preferred_element_type=jnp.float32)
            image = part if image is None else image + part
        total[...] += image

    take(0)
    take(1)
    load_own.wait()
    load_weights.wait()
    load_spread.wait()
    publish.wait()

    def step(number, carry):
        caught_up = number >= 6

        @pl.when((number == 2) | (number == 4) | caught_up)
        def _():
            take(jnp.where(caught_up, number - 2, number // 2 + 1))

        chunks = []
        for side in range(2):
            origin, quarter, _, _ = arrival(jnp.maximum(number - 2, 0), side)
            own = number < 2
            chunks.append(
                (jnp.where(own, tile, origin), jnp.where(own, 2 * number + side, quarter))
            )
        compute(chunks)
        return carry

    lax.fori_loop(0, events + 2, step, 0)

    exchanges = []
    for at, peer in enumerate(peers):
        outgoing[at] = total[pl.ds(pl.multiple_of(peer * share, share), share), :].astype(
            outgoing.dtype
        )
        copy = pltpu.make_async_remote_copy(
            src_ref=outgoing.at[at],
            dst_ref=parts.at[at],
            send_sem=part_send_sem.at[at],
            recv_sem=part_recv_sem.at[at],
            device_id=(tile, peer),
            device_id_type=MESH,
        )
        copy.start()
        exchanges.append(copy)

    for quarter in range(quarters):
        send("in", tile, quarter, True).wait_send()

        @pl.when(middle)
        def _():
            send("out", tile, quarter, True).wait_send()

        send("x", tile, quarter, True).wait_send()

    def sent(event, carry):
        for side in range(2):
            each_way(event, side, lambda copy: copy.wait_send())
        return carry

    lax.fori_loop(0, events, sent, 0)

    result = total[pl.ds(pl.multiple_of(subset * share, share), share), :]
    for at, copy in enumerate(exchanges):
        copy.wait_recv()
        result = result + parts[at].astype(jnp.float32)
    out_ref[...] = result
    for copy in exchanges:
        copy.wait_send()


def keep(array):
    return pltpu.with_memory_space_constraint(array, pltpu.HBM)


def gather_per_device(traces, taps, aperture, counts, time_weights, amplitudes):
    tiles = lax.axis_size("tile")
    subsets = lax.axis_size("trace")
    _, block_count, block_rows, samples = traces.shape
    slots, taus = time_weights.shape[2:4]
    columns = amplitudes.shape[-1]
    chunk_rows = block_count * block_rows // quarters
    share = taus // subsets
    vmem = pl.BlockSpec(memory_space=pltpu.VMEM)
    hbm = pl.BlockSpec(memory_space=pl.ANY)
    image = pl.pallas_call(
        migrate_kernel,
        out_shape=jax.ShapeDtypeStruct((share, columns), jnp.float32),
        in_specs=[hbm] * 6,
        out_specs=vmem,
        scratch_shapes=[
            pltpu.VMEM((tiles, quarters, chunk_rows, samples), jnp.bfloat16),
            pltpu.VMEM((slots, taus, samples), jnp.bfloat16),
            pltpu.VMEM((slots, 2, block_rows, columns), jnp.bfloat16),
            pltpu.VMEM((2 * samples, samples), jnp.bfloat16),
            pltpu.VMEM((taus, columns), jnp.float32),
            pltpu.VMEM((subsets - 1, share, columns), jnp.bfloat16),
            pltpu.VMEM((subsets - 1, share, columns), jnp.bfloat16),
            pltpu.SMEM(counts.shape, jnp.int32),
            pltpu.VMEM(aperture.shape, jnp.int32),
            pltpu.VMEM(taps.shape, taps.dtype),
            pltpu.VMEM((8, samples), jnp.float32),
            pltpu.VMEM((8, slots), jnp.int32),
            pltpu.SMEM((8, slots), jnp.int32),
            pltpu.SemaphoreType.DMA((tiles, quarters)),
            pltpu.SemaphoreType.DMA((3, tiles, quarters)),
            pltpu.SemaphoreType.DMA((7,)),
            pltpu.SemaphoreType.DMA((subsets - 1,)),
            pltpu.SemaphoreType.DMA((subsets - 1,)),
        ],
        compiler_params=pltpu.CompilerParams(
            collective_id=0, has_side_effects=True, vmem_limit_bytes=48 * 1024 * 1024
        ),
    )(
        keep(counts),
        keep(aperture),
        keep(taps),
        keep(traces.reshape(quarters, chunk_rows, samples)),
        keep(time_weights[0, 0]),
        keep(amplitudes[0, 0]),
    )
    return image[None]


def filter_matrix(taps, samples):
    width = taps.shape[1]
    center = (width - 1) // 2
    offset = jnp.arange(samples)[:, None] - jnp.arange(samples)[None, :] + center
    table = (offset[:, :, None] == jnp.arange(width)[None, None, :]).astype(jnp.bfloat16)
    return jnp.einsum("ct,nmt->cnm", taps, table, preferred_element_type=jnp.float32).astype(
        jnp.bfloat16
    )


def exchange_per_device(traces, taps, aperture, counts, time_weights, amplitudes):
    tiles = lax.axis_size("tile")
    myself = lax.axis_index("tile")
    block_count = traces.shape[1]
    samples = traces.shape[3]
    slots = aperture.shape[2]
    capacity = max(2, slots // tiles)
    listing = aperture[0]
    filled = counts[0]
    owners = listing // block_count
    within = listing - owners * block_count
    order = jnp.arange(slots)
    earlier = order[None, :] < order[:, None]
    rank = jnp.sum((owners[:, :, None] == owners[:, None, :]) & earlier[None], axis=2)
    alive_slots = order[None, :] < filled[:, None]
    mine = (owners == myself) & alive_slots
    rank_onehot = (
        (rank[:, :, None] == jnp.arange(capacity)[None, None, :]) & mine[:, :, None]
    ).astype(jnp.bfloat16)
    local_onehot = (within[:, :, None] == jnp.arange(block_count)[None, None, :]).astype(
        jnp.bfloat16
    )
    select = jnp.einsum(
        "ksc,ksl->kcl", rank_onehot, local_onehot, preferred_element_type=jnp.float32
    ).astype(jnp.bfloat16)
    operator = filter_matrix(taps, samples)
    own_owner = lax.dynamic_index_in_dim(owners, myself, 0, keepdims=False)
    own_rank = lax.dynamic_index_in_dim(rank, myself, 0, keepdims=False)
    own_fill = lax.dynamic_index_in_dim(filled, myself, 0, keepdims=False)
    source_slot = own_owner * capacity + own_rank
    arrived_rows = tiles * capacity

    def pick_rows(positions):
        return (positions[:, None] == jnp.arange(arrived_rows)[None, :]).astype(jnp.bfloat16)

    filtered = jnp.einsum(
        "cnm,kbm->kcbn", operator, traces[0], preferred_element_type=jnp.float32
    ).astype(jnp.bfloat16)
    outgoing = jnp.einsum(
        "kcl,lqbn->kcqbn", select, filtered, preferred_element_type=jnp.float32
    ).astype(jnp.bfloat16)
    arrived = lax.all_to_all(outgoing, "tile", split_axis=0, concat_axis=0, tiled=True)
    arrived = arrived.reshape((arrived_rows,) + arrived.shape[2:])

    def fetch(positions):
        return jnp.einsum(
            "gq,qcbn->gcbn", pick_rows(positions), arrived, preferred_element_type=jnp.float32
        ).astype(jnp.bfloat16)

    weights = time_weights[0, 0]
    spread = amplitudes[0, 0]

    def add_group(index, total):
        start = index * group_slots
        positions = lax.dynamic_slice_in_dim(source_slot, start, group_slots, 0)
        blocks = fetch(positions)
        part_weights = lax.dynamic_slice_in_dim(weights, start, group_slots, 0)
        part_spread = lax.dynamic_slice_in_dim(spread, start, group_slots, 0)
        alive = (start + jnp.arange(group_slots) < own_fill).astype(jnp.float32)
        interp = jnp.einsum(
            "gtn,gcbn->gcbt", part_weights, blocks, preferred_element_type=jnp.float32
        )
        interp = (interp * alive[:, None, None, None]).astype(jnp.bfloat16)
        return total + jnp.einsum(
            "gcbt,gcbp->tp", interp, part_spread, preferred_element_type=jnp.float32
        )

    rounds = (own_fill + group_slots - 1) // group_slots
    partial_value = lax.fori_loop(
        0, rounds, add_group, jnp.zeros((weights.shape[1], spread.shape[-1]), jnp.float32)
    )
    image = lax.psum_scatter(partial_value, "trace", scatter_dimension=0, tiled=True)
    return image[None]


def per_device(traces, taps, aperture, counts, time_weights, amplitudes):
    tiles = lax.axis_size("tile")
    every_block = traces.shape[1] * tiles
    quarter = traces.shape[1] // quarters
    gathers = (
        every_block == aperture.shape[2]
        and tiles == 2 * rows_z
        and lax.axis_size("trace") == 4
        and quarter * quarters == traces.shape[1]
    )
    form = gather_per_device if gathers else exchange_per_device
    return form(traces, taps, aperture, counts, time_weights, amplitudes)


def solution(mesh):
    placed = (
        P("trace", "tile", None, None),
        P(),
        P("trace", None, None),
        P("trace", None),
        P("trace", "tile", None, None, None),
        P("trace", "tile", None, None, None, None),
    )
    return jax.shard_map(
        per_device, mesh=mesh, in_specs=placed, out_specs=P("tile", "trace", None), check_vma=False
    )
```

```python
import jax
import jax.numpy as jnp
from jax import lax
from jax.experimental import pallas as pl
from jax.experimental.pallas import tpu as pltpu
from jax.sharding import PartitionSpec as P

group_slots = 8
quarters = 4
rows_z = 4
events = 14
MESH = pl.DeviceIdType.MESH


def migrate_kernel(
    counts_hbm,
    aperture_hbm,
    taps_hbm,
    traces_ref,
    weights_ref,
    spread_ref,
    out_ref,
    gathered,
    weights,
    spread,
    operator,
    total,
    outgoing,
    parts,
    counts_ref,
    aperture_ref,
    taps_ref,
    band,
    lookup,
    slot_of,
    recv_sem,
    send_sem,
    load_sem,
    part_send_sem,
    part_recv_sem,
):
    tile = lax.axis_index("tile")
    subset = lax.axis_index("trace")
    z = tile // 2
    x = tile % 2
    other = 1 - x
    low = z < rows_z // 2
    inward = jnp.where(low, 1, -1)
    place = jnp.where(low, z, rows_z - 1 - z)
    end = place == 0
    middle = place == 1
    samples = operator.shape[0]
    taus = weights.shape[1]
    block_rows = spread.shape[2]
    chunk_rows = gathered.shape[2]
    chunk_blocks = chunk_rows // block_rows
    block_count = chunk_blocks * quarters
    share = out_ref.shape[0]

    load_small = [
        pltpu.make_async_copy(src, dst, load_sem.at[4 + at])
        for at, (src, dst) in enumerate(
            ((counts_hbm, counts_ref), (aperture_hbm, aperture_ref), (taps_hbm, taps_ref))
        )
    ]
    load_own = pltpu.make_async_copy(traces_ref, gathered.at[tile], load_sem.at[0])
    load_weights = pltpu.make_async_copy(weights_ref, weights, load_sem.at[1])
    load_spread = pltpu.make_async_copy(spread_ref, spread, load_sem.at[2])

    row_y = subset // 2
    core = subset % 2
    across_y = (1 - row_y) * 2
    peers = (across_y + core, across_y + 1 - core, row_y * 2 + 1 - core)

    barrier = pltpu.get_barrier_semaphore()
    neighbours = {
        "x": z * 2 + other,
        "in": tile + 2 * inward,
        "out": tile - 2 * inward,
    }

    def greet(to_tile, to_subset):
        pl.semaphore_signal(barrier, inc=1, device_id=(to_tile, to_subset), device_id_type=MESH)

    greet(neighbours["in"], subset)
    greet(neighbours["x"], subset)

    @pl.when(middle)
    def _():
        greet(neighbours["out"], subset)

    for peer in peers:
        greet(tile, peer)
    for load in load_small:
        load.start()
    load_own.start()
    pl.semaphore_wait(barrier, 5 + jnp.where(middle, 1, 0))

    def send(way, origin, quarter, own=False):
        return pltpu.make_async_remote_copy(
            src_ref=traces_ref.at[quarter] if own else gathered.at[origin, quarter],
            dst_ref=gathered.at[origin, quarter],
            send_sem=send_sem.at[("x", "in", "out").index(way), origin, quarter],
            recv_sem=recv_sem.at[origin, quarter],
            device_id=(neighbours[way], subset),
            device_id_type=MESH,
        )

    def wait_arrival(origin, quarter):
        pltpu.make_async_remote_copy(
            src_ref=gathered.at[origin, quarter],
            dst_ref=gathered.at[origin, quarter],
            send_sem=send_sem.at[0, 0, 0],
            recv_sem=recv_sem.at[origin, quarter],
            device_id=(neighbours["x"], subset),
            device_id_type=MESH,
        ).wait_recv()

    for quarter in range(quarters):
        send("in", tile, quarter, True).start()

        @pl.when(middle)
        def _():
            send("out", tile, quarter, True).start()

        send("x", tile, quarter, True).start()

    load_weights.start()
    load_spread.start()
    for load in load_small:
        load.wait()
    slots = weights.shape[0]
    listing = aperture_ref[0, pl.ds(tile, 1), :]
    slot = lax.broadcasted_iota(jnp.int32, (slots, slots), 0)
    block = lax.broadcasted_iota(jnp.int32, (slots, slots), 1)
    named = jnp.broadcast_to(listing, (slots, slots)).T
    match = (named == block) & (slot < counts_ref[0, tile])
    lookup[...] = jnp.broadcast_to(
        jnp.sum(jnp.where(match, slot + 1, 0), axis=0, keepdims=True) - 1, lookup.shape
    )
    publish = pltpu.make_async_copy(lookup, slot_of, load_sem.at[3])
    publish.start()

    half_taps = (taps_ref.shape[1] - 1) // 2
    band[...] = jnp.zeros_like(band)
    band[0:2, 0 : taps_ref.shape[1]] = taps_ref[...].astype(jnp.float32)
    row = lax.broadcasted_iota(jnp.int32, (samples, samples), 0)
    gap = lax.broadcasted_iota(jnp.int32, (samples, samples), 1) - row
    inside = (gap <= half_taps) & (gap >= -half_taps)
    for channel in range(2):
        centred = pltpu.roll(band[...], samples - half_taps, 1)[channel : channel + 1, :]
        shifted = jnp.broadcast_to(centred, (samples, samples))
        shift = 1
        while shift < samples:
            shifted = jnp.where((row // shift) % 2 == 1, pltpu.roll(shifted, shift, 1), shifted)
            shift *= 2
        operator[:, channel * samples : (channel + 1) * samples] = jnp.where(
            inside, shifted, 0.0
        ).astype(operator.dtype)
    total[...] = jnp.zeros_like(total)

    def tile_at(position, column):
        return jnp.where(low, position, rows_z - 1 - position) * 2 + jnp.where(
            column == 0, x, other
        )

    def arrival(event, side):
        if side == 0:
            late = event >= 12
            end_column = jnp.where(late, 1, 0)
            end_position = jnp.where(late, 3, 1 + event // 4)
            end_quarter = jnp.where(late, event - 10, event % 4)
            end_x = event < 10
            end_in = event < 0
        else:
            end_column = 1
            end_position = event // 4
            end_quarter = event % 4
            end_x = event < 0
            end_in = event < 4
        number = 2 * event + side
        turn = number < 24
        stream = jnp.where(turn, number % 3, 2)
        index = jnp.where(turn, number // 3, number - 16)
        from_end = stream == 0
        from_middle = stream == 1
        from_x = stream == 2
        column = jnp.where(from_x | (from_end & (index >= 4)), 1, 0)
        position = jnp.where(from_end, 0, jnp.where(from_middle, 2, 1) + index // 4)
        quarter = jnp.where(from_x & (index >= 9), 1 + (index - 8) % 3, index % 4)
        mid_x = from_middle & (index != 5)
        mid_in = from_end & (index < 4)
        mid_out = from_middle | (from_x & ((index == 9) | (index == 10)))
        origin = tile_at(
            jnp.where(end, end_position, position), jnp.where(end, end_column, column)
        )
        ways = {
            "x": (end & end_x) | (middle & mid_x),
            "in": (end & end_in) | (middle & mid_in),
            "out": middle & mid_out,
        }
        postponed = middle & from_middle & (index == 7)
        return origin, jnp.where(end, end_quarter, quarter), ways, postponed

    def each_way(event, side, act):
        origin, quarter, ways, postponed = arrival(event, side)
        for way in ("out", "in", "x"):

            @pl.when(ways[way])
            def _():
                act(send(way, origin, quarter))

        @pl.when(postponed)
        def _():
            act(send("x", origin, 1))

    def take(event):
        for side in range(2):
            origin, quarter, _, _ = arrival(event, side)
            wait_arrival(origin, quarter)
            each_way(event, side, lambda copy: copy.start())

    lanes = lax.broadcasted_iota(jnp.int32, (1, 2 * chunk_rows), 1)
    member = (lanes // block_rows) % chunk_blocks

    def compute(chunks):
        rows = jnp.concatenate([gathered[origin, quarter] for origin, quarter in chunks], axis=0)
        filtered = jnp.dot(rows, operator[...], preferred_element_type=jnp.float32).astype(
            jnp.bfloat16
        )
        image = None
        for at, (origin, quarter) in enumerate(chunks):
            first = at * chunk_rows
            blocks = jnp.concatenate(
                [
                    filtered[first : first + chunk_rows, 0:samples],
                    filtered[first : first + chunk_rows, samples : 2 * samples],
                ],
                axis=0,
            )
            base = origin * block_count + quarter * chunk_blocks
            found = [slot_of[0, base + index] for index in range(chunk_blocks)]
            picks = [jnp.maximum(value, 0) for value in found]
            gains = [jnp.where(value >= 0, 1.0, 0.0) for value in found]
            stacked = jnp.concatenate([weights[pick] for pick in picks], axis=0)
            product = lax.dot_general(
                stacked, blocks, (((1,), (1,)), ((), ())), preferred_element_type=jnp.float32
            )
            interp = product[0:taus]
            alive = jnp.full((1, 2 * chunk_rows), gains[0], jnp.float32)
            for index in range(1, chunk_blocks):
                here = member == index
                interp = jnp.where(here, product[index * taus : (index + 1) * taus], interp)
                alive = jnp.where(here, gains[index], alive)
            interp = (interp * alive).astype(jnp.bfloat16)
            columns = jnp.concatenate(
                [spread[pick, channel] for channel in range(2) for pick in picks], axis=0
            )
            part = jnp.dot(interp, columns, preferred_element_type=jnp.float32)
            image = part if image is None else image + part
        total[...] += image

    take(0)
    load_own.wait()
    load_weights.wait()
    load_spread.wait()
    publish.wait()

    def step(number, carry):
        caught_up = number >= 6

        @pl.when((number == 1) | (number == 3) | (number == 5) | caught_up)
        def _():
            take(jnp.where(caught_up, number - 2, (number + 1) // 2))

        chunks = []
        for side in range(2):
            origin, quarter, _, _ = arrival(jnp.maximum(number - 2, 0), side)
            own = number < 2
            chunks.append(
                (jnp.where(own, tile, origin), jnp.where(own, 2 * number + side, quarter))
            )
        compute(chunks)
        return carry

    lax.fori_loop(0, events + 2, step, 0)

    exchanges = []
    for at, peer in enumerate(peers):
        outgoing[at] = total[pl.ds(pl.multiple_of(peer * share, share), share), :].astype(
            outgoing.dtype
        )
        copy = pltpu.make_async_remote_copy(
            src_ref=outgoing.at[at],
            dst_ref=parts.at[at],
            send_sem=part_send_sem.at[at],
            recv_sem=part_recv_sem.at[at],
            device_id=(tile, peer),
            device_id_type=MESH,
        )
        copy.start()
        exchanges.append(copy)

    for quarter in range(quarters):
        send("in", tile, quarter, True).wait_send()

        @pl.when(middle)
        def _():
            send("out", tile, quarter, True).wait_send()

        send("x", tile, quarter, True).wait_send()

    def sent(event, carry):
        for side in range(2):
            each_way(event, side, lambda copy: copy.wait_send())
        return carry

    lax.fori_loop(0, events, sent, 0)

    result = total[pl.ds(pl.multiple_of(subset * share, share), share), :]
    for at, copy in enumerate(exchanges):
        copy.wait_recv()
        result = result + parts[at].astype(jnp.float32)
    out_ref[...] = result
    for copy in exchanges:
        copy.wait_send()


def keep(array):
    return pltpu.with_memory_space_constraint(array, pltpu.HBM)


def gather_per_device(traces, taps, aperture, counts, time_weights, amplitudes):
    tiles = lax.axis_size("tile")
    subsets = lax.axis_size("trace")
    _, block_count, block_rows, samples = traces.shape
    slots, taus = time_weights.shape[2:4]
    columns = amplitudes.shape[-1]
    chunk_rows = block_count * block_rows // quarters
    share = taus // subsets
    vmem = pl.BlockSpec(memory_space=pltpu.VMEM)
    hbm = pl.BlockSpec(memory_space=pl.ANY)
    image = pl.pallas_call(
        migrate_kernel,
        out_shape=jax.ShapeDtypeStruct((share, columns), jnp.float32),
        in_specs=[hbm] * 6,
        out_specs=vmem,
        scratch_shapes=[
            pltpu.VMEM((tiles, quarters, chunk_rows, samples), jnp.bfloat16),
            pltpu.VMEM((slots, taus, samples), jnp.bfloat16),
            pltpu.VMEM((slots, 2, block_rows, columns), jnp.bfloat16),
            pltpu.VMEM((samples, 2 * samples), jnp.bfloat16),
            pltpu.VMEM((taus, columns), jnp.float32),
            pltpu.VMEM((subsets - 1, share, columns), jnp.bfloat16),
            pltpu.VMEM((subsets - 1, share, columns), jnp.bfloat16),
            pltpu.SMEM(counts.shape, jnp.int32),
            pltpu.VMEM(aperture.shape, jnp.int32),
            pltpu.VMEM(taps.shape, taps.dtype),
            pltpu.VMEM((8, samples), jnp.float32),
            pltpu.VMEM((8, slots), jnp.int32),
            pltpu.SMEM((8, slots), jnp.int32),
            pltpu.SemaphoreType.DMA((tiles, quarters)),
            pltpu.SemaphoreType.DMA((3, tiles, quarters)),
            pltpu.SemaphoreType.DMA((7,)),
            pltpu.SemaphoreType.DMA((subsets - 1,)),
            pltpu.SemaphoreType.DMA((subsets - 1,)),
        ],
        compiler_params=pltpu.CompilerParams(
            collective_id=0, has_side_effects=True, vmem_limit_bytes=48 * 1024 * 1024
        ),
    )(
        keep(counts),
        keep(aperture),
        keep(taps),
        keep(traces.reshape(quarters, chunk_rows, samples)),
        keep(time_weights[0, 0]),
        keep(amplitudes[0, 0]),
    )
    return image[None]


def filter_matrix(taps, samples):
    width = taps.shape[1]
    center = (width - 1) // 2
    offset = jnp.arange(samples)[:, None] - jnp.arange(samples)[None, :] + center
    table = (offset[:, :, None] == jnp.arange(width)[None, None, :]).astype(jnp.bfloat16)
    return jnp.einsum("ct,nmt->cnm", taps, table, preferred_element_type=jnp.float32).astype(
        jnp.bfloat16
    )


def exchange_per_device(traces, taps, aperture, counts, time_weights, amplitudes):
    tiles = lax.axis_size("tile")
    myself = lax.axis_index("tile")
    block_count = traces.shape[1]
    samples = traces.shape[3]
    slots = aperture.shape[2]
    capacity = max(2, slots // tiles)
    listing = aperture[0]
    filled = counts[0]
    owners = listing // block_count
    within = listing - owners * block_count
    order = jnp.arange(slots)
    earlier = order[None, :] < order[:, None]
    rank = jnp.sum((owners[:, :, None] == owners[:, None, :]) & earlier[None], axis=2)
    alive_slots = order[None, :] < filled[:, None]
    mine = (owners == myself) & alive_slots
    rank_onehot = (
        (rank[:, :, None] == jnp.arange(capacity)[None, None, :]) & mine[:, :, None]
    ).astype(jnp.bfloat16)
    local_onehot = (within[:, :, None] == jnp.arange(block_count)[None, None, :]).astype(
        jnp.bfloat16
    )
    select = jnp.einsum(
        "ksc,ksl->kcl", rank_onehot, local_onehot, preferred_element_type=jnp.float32
    ).astype(jnp.bfloat16)
    operator = filter_matrix(taps, samples)
    own_owner = lax.dynamic_index_in_dim(owners, myself, 0, keepdims=False)
    own_rank = lax.dynamic_index_in_dim(rank, myself, 0, keepdims=False)
    own_fill = lax.dynamic_index_in_dim(filled, myself, 0, keepdims=False)
    source_slot = own_owner * capacity + own_rank
    arrived_rows = tiles * capacity

    def pick_rows(positions):
        return (positions[:, None] == jnp.arange(arrived_rows)[None, :]).astype(jnp.bfloat16)

    filtered = jnp.einsum(
        "cnm,kbm->kcbn", operator, traces[0], preferred_element_type=jnp.float32
    ).astype(jnp.bfloat16)
    outgoing = jnp.einsum(
        "kcl,lqbn->kcqbn", select, filtered, preferred_element_type=jnp.float32
    ).astype(jnp.bfloat16)
    arrived = lax.all_to_all(outgoing, "tile", split_axis=0, concat_axis=0, tiled=True)
    arrived = arrived.reshape((arrived_rows,) + arrived.shape[2:])

    def fetch(positions):
        return jnp.einsum(
            "gq,qcbn->gcbn", pick_rows(positions), arrived, preferred_element_type=jnp.float32
        ).astype(jnp.bfloat16)

    weights = time_weights[0, 0]
    spread = amplitudes[0, 0]

    def add_group(index, total):
        start = index * group_slots
        positions = lax.dynamic_slice_in_dim(source_slot, start, group_slots, 0)
        blocks = fetch(positions)
        part_weights = lax.dynamic_slice_in_dim(weights, start, group_slots, 0)
        part_spread = lax.dynamic_slice_in_dim(spread, start, group_slots, 0)
        alive = (start + jnp.arange(group_slots) < own_fill).astype(jnp.float32)
        interp = jnp.einsum(
            "gtn,gcbn->gcbt", part_weights, blocks, preferred_element_type=jnp.float32
        )
        interp = (interp * alive[:, None, None, None]).astype(jnp.bfloat16)
        return total + jnp.einsum(
            "gcbt,gcbp->tp", interp, part_spread, preferred_element_type=jnp.float32
        )

    rounds = (own_fill + group_slots - 1) // group_slots
    partial_value = lax.fori_loop(
        0, rounds, add_group, jnp.zeros((weights.shape[1], spread.shape[-1]), jnp.float32)
    )
    image = lax.psum_scatter(partial_value, "trace", scatter_dimension=0, tiled=True)
    return image[None]


def per_device(traces, taps, aperture, counts, time_weights, amplitudes):
    tiles = lax.axis_size("tile")
    every_block = traces.shape[1] * tiles
    quarter = traces.shape[1] // quarters
    gathers = (
        every_block == aperture.shape[2]
        and tiles == 2 * rows_z
        and lax.axis_size("trace") == 4
        and quarter * quarters == traces.shape[1]
    )
    form = gather_per_device if gathers else exchange_per_device
    return form(traces, taps, aperture, counts, time_weights, amplitudes)


def solution(mesh):
    placed = (
        P("trace", "tile", None, None),
        P(),
        P("trace", None, None),
        P("trace", None),
        P("trace", "tile", None, None, None),
        P("trace", "tile", None, None, None, None),
    )
    return jax.shard_map(
        per_device, mesh=mesh, in_specs=placed, out_specs=P("tile", "trace", None), check_vma=False
    )
```

```python
import jax
import jax.numpy as jnp
from jax import lax
from jax.experimental import pallas as pl
from jax.experimental.pallas import tpu as pltpu
from jax.sharding import PartitionSpec as P

group_slots = 8
quarters = 4
rows_z = 4
events = 14
MESH = pl.DeviceIdType.MESH


def migrate_kernel(
    counts_hbm,
    aperture_hbm,
    taps_hbm,
    traces_ref,
    weights_ref,
    spread_ref,
    out_ref,
    gathered,
    weights,
    spread,
    operator,
    total,
    outgoing,
    parts,
    counts_ref,
    aperture_ref,
    taps_ref,
    band,
    lookup,
    slot_of,
    recv_sem,
    send_sem,
    load_sem,
    part_send_sem,
    part_recv_sem,
    far_sem,
):
    tile = lax.axis_index("tile")
    subset = lax.axis_index("trace")
    z = tile // 2
    x = tile % 2
    other = 1 - x
    low = z < rows_z // 2
    inward = jnp.where(low, 1, -1)
    place = jnp.where(low, z, rows_z - 1 - z)
    end = place == 0
    middle = place == 1
    samples = operator.shape[0]
    taus = weights.shape[1]
    block_rows = spread.shape[2]
    chunk_rows = gathered.shape[2]
    chunk_blocks = chunk_rows // block_rows
    block_count = chunk_blocks * quarters
    share = out_ref.shape[0]

    load_small = [
        pltpu.make_async_copy(src, dst, load_sem.at[4 + at])
        for at, (src, dst) in enumerate(
            ((counts_hbm, counts_ref), (aperture_hbm, aperture_ref), (taps_hbm, taps_ref))
        )
    ]
    load_own = pltpu.make_async_copy(traces_ref, gathered.at[tile], load_sem.at[0])
    load_weights = pltpu.make_async_copy(weights_ref, weights, load_sem.at[1])
    load_spread = pltpu.make_async_copy(spread_ref, spread, load_sem.at[2])

    row_y = subset // 2
    core = subset % 2
    across_y = (1 - row_y) * 2
    peers = (across_y + core, across_y + 1 - core, row_y * 2 + 1 - core)

    barrier = pltpu.get_barrier_semaphore()
    neighbours = {
        "x": z * 2 + other,
        "in": tile + 2 * inward,
        "out": tile - 2 * inward,
    }

    def greet(to_tile, to_subset):
        pl.semaphore_signal(barrier, inc=1, device_id=(to_tile, to_subset), device_id_type=MESH)

    greet(neighbours["in"], subset)
    greet(neighbours["x"], subset)

    @pl.when(middle)
    def _():
        greet(neighbours["out"], subset)

    for peer in (peers[0], peers[2]):
        greet(tile, peer)
    load_own.start()
    for load in load_small:
        load.start()
    load_own.wait()
    load_weights.start()
    load_spread.start()
    pl.semaphore_wait(barrier, 4 + jnp.where(middle, 1, 0))

    def send(way, origin, quarter):
        return pltpu.make_async_remote_copy(
            src_ref=gathered.at[origin, quarter],
            dst_ref=gathered.at[origin, quarter],
            send_sem=send_sem.at[("x", "in", "out").index(way), origin, quarter],
            recv_sem=recv_sem.at[origin, quarter],
            device_id=(neighbours[way], subset),
            device_id_type=MESH,
        )

    def wait_arrival(origin, quarter):
        pltpu.make_async_remote_copy(
            src_ref=gathered.at[origin, quarter],
            dst_ref=gathered.at[origin, quarter],
            send_sem=send_sem.at[0, 0, 0],
            recv_sem=recv_sem.at[origin, quarter],
            device_id=(neighbours["x"], subset),
            device_id_type=MESH,
        ).wait_recv()

    for quarter in range(quarters):
        send("in", tile, quarter).start()

        @pl.when(middle)
        def _():
            send("out", tile, quarter).start()

        send("x", tile, (quarter + jnp.where(end, 2, 0)) % quarters).start()

    pl.semaphore_signal(far_sem, inc=1, device_id=(tile, peers[0]), device_id_type=MESH)
    for load in load_small:
        load.wait()
    slots = weights.shape[0]
    listing = aperture_ref[0, pl.ds(tile, 1), :]
    slot = lax.broadcasted_iota(jnp.int32, (slots, slots), 0)
    block = lax.broadcasted_iota(jnp.int32, (slots, slots), 1)
    named = jnp.broadcast_to(listing, (slots, slots)).T
    match = (named == block) & (slot < counts_ref[0, tile])
    lookup[...] = jnp.broadcast_to(
        jnp.sum(jnp.where(match, slot + 1, 0), axis=0, keepdims=True) - 1, lookup.shape
    )
    publish = pltpu.make_async_copy(lookup, slot_of, load_sem.at[3])
    publish.start()

    half_taps = (taps_ref.shape[1] - 1) // 2
    band[...] = jnp.zeros_like(band)
    band[0:2, 0 : taps_ref.shape[1]] = taps_ref[...].astype(jnp.float32)
    row = lax.broadcasted_iota(jnp.int32, (samples, samples), 0)
    gap = lax.broadcasted_iota(jnp.int32, (samples, samples), 1) - row
    inside = (gap <= half_taps) & (gap >= -half_taps)
    for channel in range(2):
        centred = pltpu.roll(band[...], samples - half_taps, 1)[channel : channel + 1, :]
        shifted = jnp.broadcast_to(centred, (samples, samples))
        shift = 1
        while shift < samples:
            shifted = jnp.where((row // shift) % 2 == 1, pltpu.roll(shifted, shift, 1), shifted)
            shift *= 2
        operator[:, channel * samples : (channel + 1) * samples] = jnp.where(
            inside, shifted, 0.0
        ).astype(operator.dtype)
    total[...] = jnp.zeros_like(total)

    def tile_at(position, column):
        return jnp.where(low, position, rows_z - 1 - position) * 2 + jnp.where(
            column == 0, x, other
        )

    def arrival(event, side):
        if side == 0:
            late = event >= 12
            end_column = jnp.where(late, 1, 0)
            end_position = jnp.where(late, 3, 1 + event // 4)
            end_quarter = jnp.where(late, event - 10, event % 4)
            end_x = event < 10
            end_in = event < 0
        else:
            end_column = 1
            end_position = event // 4
            end_quarter = jnp.where(event < 4, (event + 2) % 4, event % 4)
            end_x = event < 0
            end_in = event < 4
        number = 2 * event + side
        turn = number < 24
        stream = jnp.where(turn, number % 3, 1 + number % 2)
        index = jnp.where(turn, number // 3, number // 2 - 4)
        from_end = stream == 0
        from_middle = stream == 1
        from_x = stream == 2
        relayed = (from_end & (index >= 4)) | (from_middle & (index >= 8))
        column = jnp.where(from_x | relayed, 1, 0)
        position = jnp.where(
            from_end, 0, jnp.where(from_middle, jnp.where(relayed, 3, 2 + index // 4), 1 + index // 4)
        )
        quarter = jnp.where(relayed, (index + 2) % 4, index % 4)
        mid_x = from_middle & (index < 6)
        mid_in = from_end & (index < 6)
        mid_out = from_middle
        origin = tile_at(
            jnp.where(end, end_position, position), jnp.where(end, end_column, column)
        )
        ways = {
            "x": (end & end_x) | (middle & mid_x),
            "in": (end & end_in) | (middle & mid_in),
            "out": middle & mid_out,
        }
        return origin, jnp.where(end, end_quarter, quarter), ways

    def each_way(event, side, act):
        origin, quarter, ways = arrival(event, side)
        for way in ("out", "in", "x"):

            @pl.when(ways[way])
            def _():
                act(send(way, origin, quarter))

    def take(event):
        for side in range(2):
            origin, quarter, _ = arrival(event, side)
            wait_arrival(origin, quarter)
            each_way(event, side, lambda copy: copy.start())

    lanes = lax.broadcasted_iota(jnp.int32, (1, 2 * chunk_rows), 1)
    member = (lanes // block_rows) % chunk_blocks

    def compute(chunks):
        rows = jnp.concatenate([gathered[origin, quarter] for origin, quarter in chunks], axis=0)
        filtered = jnp.dot(rows, operator[...], preferred_element_type=jnp.float32).astype(
            jnp.bfloat16
        )
        image = None
        for at, (origin, quarter) in enumerate(chunks):
            first = at * chunk_rows
            blocks = jnp.concatenate(
                [
                    filtered[first : first + chunk_rows, 0:samples],
                    filtered[first : first + chunk_rows, samples : 2 * samples],
                ],
                axis=0,
            )
            base = origin * block_count + quarter * chunk_blocks
            found = [slot_of[0, base + index] for index in range(chunk_blocks)]
            picks = [jnp.maximum(value, 0) for value in found]
            gains = [jnp.where(value >= 0, 1.0, 0.0) for value in found]
            stacked = jnp.concatenate([weights[pick] for pick in picks], axis=0)
            product = lax.dot_general(
                stacked, blocks, (((1,), (1,)), ((), ())), preferred_element_type=jnp.float32
            )
            interp = product[0:taus]
            alive = jnp.full((1, 2 * chunk_rows), gains[0], jnp.float32)
            for index in range(1, chunk_blocks):
                here = member == index
                interp = jnp.where(here, product[index * taus : (index + 1) * taus], interp)
                alive = jnp.where(here, gains[index], alive)
            interp = (interp * alive).astype(jnp.bfloat16)
            columns = jnp.concatenate(
                [spread[pick, channel] for channel in range(2) for pick in picks], axis=0
            )
            part = jnp.dot(interp, columns, preferred_element_type=jnp.float32)
            image = part if image is None else image + part
        total[...] += image

    take(0)
    load_weights.wait()
    load_spread.wait()
    publish.wait()

    def step(number, carry):
        caught_up = number >= 6

        @pl.when((number == 1) | (number == 3) | (number == 5) | caught_up)
        def _():
            take(jnp.where(caught_up, number - 2, (number + 1) // 2))

        chunks = []
        for side in range(2):
            origin, quarter, _ = arrival(jnp.maximum(number - 2, 0), side)
            own = number < 2
            chunks.append(
                (jnp.where(own, tile, origin), jnp.where(own, 2 * number + side, quarter))
            )
        compute(chunks)
        return carry

    lax.fori_loop(0, events + 2, step, 0)

    pl.semaphore_wait(far_sem, 1)
    exchanges = []
    for at, peer in enumerate(peers):
        outgoing[at] = total[pl.ds(pl.multiple_of(peer * share, share), share), :].astype(
            outgoing.dtype
        )
        copy = pltpu.make_async_remote_copy(
            src_ref=outgoing.at[at],
            dst_ref=parts.at[at],
            send_sem=part_send_sem.at[at],
            recv_sem=part_recv_sem.at[at],
            device_id=(tile, peer),
            device_id_type=MESH,
        )
        copy.start()
        exchanges.append(copy)

    for quarter in range(quarters):
        send("in", tile, quarter).wait_send()

        @pl.when(middle)
        def _():
            send("out", tile, quarter).wait_send()

        send("x", tile, quarter).wait_send()

    def sent(event, carry):
        for side in range(2):
            each_way(event, side, lambda copy: copy.wait_send())
        return carry

    lax.fori_loop(0, events, sent, 0)

    result = total[pl.ds(pl.multiple_of(subset * share, share), share), :]
    for at, copy in enumerate(exchanges):
        copy.wait_recv()
        result = result + parts[at].astype(jnp.float32)
    out_ref[...] = result
    for copy in exchanges:
        copy.wait_send()


def keep(array):
    return pltpu.with_memory_space_constraint(array, pltpu.HBM)


def gather_per_device(traces, taps, aperture, counts, time_weights, amplitudes):
    tiles = lax.axis_size("tile")
    subsets = lax.axis_size("trace")
    _, block_count, block_rows, samples = traces.shape
    slots, taus = time_weights.shape[2:4]
    columns = amplitudes.shape[-1]
    chunk_rows = block_count * block_rows // quarters
    share = taus // subsets
    vmem = pl.BlockSpec(memory_space=pltpu.VMEM)
    hbm = pl.BlockSpec(memory_space=pl.ANY)
    image = pl.pallas_call(
        migrate_kernel,
        out_shape=jax.ShapeDtypeStruct((share, columns), jnp.float32),
        in_specs=[hbm] * 6,
        out_specs=vmem,
        scratch_shapes=[
            pltpu.VMEM((tiles, quarters, chunk_rows, samples), jnp.bfloat16),
            pltpu.VMEM((slots, taus, samples), jnp.bfloat16),
            pltpu.VMEM((slots, 2, block_rows, columns), jnp.bfloat16),
            pltpu.VMEM((samples, 2 * samples), jnp.bfloat16),
            pltpu.VMEM((taus, columns), jnp.float32),
            pltpu.VMEM((subsets - 1, share, columns), jnp.bfloat16),
            pltpu.VMEM((subsets - 1, share, columns), jnp.bfloat16),
            pltpu.SMEM(counts.shape, jnp.int32),
            pltpu.VMEM(aperture.shape, jnp.int32),
            pltpu.VMEM(taps.shape, taps.dtype),
            pltpu.VMEM((8, samples), jnp.float32),
            pltpu.VMEM((8, slots), jnp.int32),
            pltpu.SMEM((8, slots), jnp.int32),
            pltpu.SemaphoreType.DMA((tiles, quarters)),
            pltpu.SemaphoreType.DMA((3, tiles, quarters)),
            pltpu.SemaphoreType.DMA((7,)),
            pltpu.SemaphoreType.DMA((subsets - 1,)),
            pltpu.SemaphoreType.DMA((subsets - 1,)),
            pltpu.SemaphoreType.REGULAR,
        ],
        compiler_params=pltpu.CompilerParams(
            collective_id=0, has_side_effects=True, vmem_limit_bytes=48 * 1024 * 1024
        ),
    )(
        keep(counts),
        keep(aperture),
        keep(taps),
        keep(traces.reshape(quarters, chunk_rows, samples)),
        keep(time_weights[0, 0]),
        keep(amplitudes[0, 0]),
    )
    return image[None]


def filter_matrix(taps, samples):
    width = taps.shape[1]
    center = (width - 1) // 2
    offset = jnp.arange(samples)[:, None] - jnp.arange(samples)[None, :] + center
    table = (offset[:, :, None] == jnp.arange(width)[None, None, :]).astype(jnp.bfloat16)
    return jnp.einsum("ct,nmt->cnm", taps, table, preferred_element_type=jnp.float32).astype(
        jnp.bfloat16
    )


def exchange_per_device(traces, taps, aperture, counts, time_weights, amplitudes):
    tiles = lax.axis_size("tile")
    myself = lax.axis_index("tile")
    block_count = traces.shape[1]
    samples = traces.shape[3]
    slots = aperture.shape[2]
    capacity = max(2, slots // tiles)
    listing = aperture[0]
    filled = counts[0]
    owners = listing // block_count
    within = listing - owners * block_count
    order = jnp.arange(slots)
    earlier = order[None, :] < order[:, None]
    rank = jnp.sum((owners[:, :, None] == owners[:, None, :]) & earlier[None], axis=2)
    alive_slots = order[None, :] < filled[:, None]
    mine = (owners == myself) & alive_slots
    rank_onehot = (
        (rank[:, :, None] == jnp.arange(capacity)[None, None, :]) & mine[:, :, None]
    ).astype(jnp.bfloat16)
    local_onehot = (within[:, :, None] == jnp.arange(block_count)[None, None, :]).astype(
        jnp.bfloat16
    )
    select = jnp.einsum(
        "ksc,ksl->kcl", rank_onehot, local_onehot, preferred_element_type=jnp.float32
    ).astype(jnp.bfloat16)
    operator = filter_matrix(taps, samples)
    own_owner = lax.dynamic_index_in_dim(owners, myself, 0, keepdims=False)
    own_rank = lax.dynamic_index_in_dim(rank, myself, 0, keepdims=False)
    own_fill = lax.dynamic_index_in_dim(filled, myself, 0, keepdims=False)
    source_slot = own_owner * capacity + own_rank
    arrived_rows = tiles * capacity

    def pick_rows(positions):
        return (positions[:, None] == jnp.arange(arrived_rows)[None, :]).astype(jnp.bfloat16)

    filtered = jnp.einsum(
        "cnm,kbm->kcbn", operator, traces[0], preferred_element_type=jnp.float32
    ).astype(jnp.bfloat16)
    outgoing = jnp.einsum(
        "kcl,lqbn->kcqbn", select, filtered, preferred_element_type=jnp.float32
    ).astype(jnp.bfloat16)
    arrived = lax.all_to_all(outgoing, "tile", split_axis=0, concat_axis=0, tiled=True)
    arrived = arrived.reshape((arrived_rows,) + arrived.shape[2:])

    def fetch(positions):
        return jnp.einsum(
            "gq,qcbn->gcbn", pick_rows(positions), arrived, preferred_element_type=jnp.float32
        ).astype(jnp.bfloat16)

    weights = time_weights[0, 0]
    spread = amplitudes[0, 0]

    def add_group(index, total):
        start = index * group_slots
        positions = lax.dynamic_slice_in_dim(source_slot, start, group_slots, 0)
        blocks = fetch(positions)
        part_weights = lax.dynamic_slice_in_dim(weights, start, group_slots, 0)
        part_spread = lax.dynamic_slice_in_dim(spread, start, group_slots, 0)
        alive = (start + jnp.arange(group_slots) < own_fill).astype(jnp.float32)
        interp = jnp.einsum(
            "gtn,gcbn->gcbt", part_weights, blocks, preferred_element_type=jnp.float32
        )
        interp = (interp * alive[:, None, None, None]).astype(jnp.bfloat16)
        return total + jnp.einsum(
            "gcbt,gcbp->tp", interp, part_spread, preferred_element_type=jnp.float32
        )

    rounds = (own_fill + group_slots - 1) // group_slots
    partial_value = lax.fori_loop(
        0, rounds, add_group, jnp.zeros((weights.shape[1], spread.shape[-1]), jnp.float32)
    )
    image = lax.psum_scatter(partial_value, "trace", scatter_dimension=0, tiled=True)
    return image[None]


def per_device(traces, taps, aperture, counts, time_weights, amplitudes):
    tiles = lax.axis_size("tile")
    every_block = traces.shape[1] * tiles
    quarter = traces.shape[1] // quarters
    gathers = (
        every_block == aperture.shape[2]
        and tiles == 2 * rows_z
        and lax.axis_size("trace") == 4
        and quarter * quarters == traces.shape[1]
    )
    form = gather_per_device if gathers else exchange_per_device
    return form(traces, taps, aperture, counts, time_weights, amplitudes)


def solution(mesh):
    placed = (
        P("trace", "tile", None, None),
        P(),
        P("trace", None, None),
        P("trace", None),
        P("trace", "tile", None, None, None),
        P("trace", "tile", None, None, None, None),
    )
    return jax.shard_map(
        per_device, mesh=mesh, in_specs=placed, out_specs=P("tile", "trace", None), check_vma=False
    )
```

```python
import jax
import jax.numpy as jnp
from jax import lax
from jax.experimental import pallas as pl
from jax.experimental.pallas import tpu as pltpu
from jax.sharding import PartitionSpec as P

group_slots = 8
quarters = 4
rows_z = 4
events = 14
MESH = pl.DeviceIdType.MESH


def migrate_kernel(
    counts_hbm,
    aperture_hbm,
    taps_hbm,
    traces_ref,
    weights_ref,
    spread_ref,
    out_ref,
    gathered,
    weights,
    spread,
    operator,
    total,
    outgoing,
    parts,
    counts_ref,
    aperture_ref,
    taps_ref,
    band,
    lookup,
    slot_of,
    recv_sem,
    send_sem,
    load_sem,
    part_send_sem,
    part_recv_sem,
    far_sem,
    turn_sem,
):
    tile = lax.axis_index("tile")
    subset = lax.axis_index("trace")
    z = tile // 2
    x = tile % 2
    other = 1 - x
    low = z < rows_z // 2
    inward = jnp.where(low, 1, -1)
    place = jnp.where(low, z, rows_z - 1 - z)
    end = place == 0
    middle = place == 1
    samples = operator.shape[0]
    taus = weights.shape[1]
    block_rows = spread.shape[2]
    chunk_rows = gathered.shape[2]
    chunk_blocks = chunk_rows // block_rows
    block_count = chunk_blocks * quarters
    share = out_ref.shape[0]

    load_small = [
        pltpu.make_async_copy(src, dst, load_sem.at[4 + at])
        for at, (src, dst) in enumerate(
            ((counts_hbm, counts_ref), (aperture_hbm, aperture_ref), (taps_hbm, taps_ref))
        )
    ]
    load_own = pltpu.make_async_copy(traces_ref, gathered.at[tile], load_sem.at[0])
    load_weights = pltpu.make_async_copy(weights_ref, weights, load_sem.at[1])
    load_spread = pltpu.make_async_copy(spread_ref, spread, load_sem.at[2])

    row_y = subset // 2
    core = subset % 2
    across_y = (1 - row_y) * 2
    peers = (across_y + core, across_y + 1 - core, row_y * 2 + 1 - core)

    barrier = pltpu.get_barrier_semaphore()
    neighbours = {
        "x": z * 2 + other,
        "in": tile + 2 * inward,
        "out": tile - 2 * inward,
    }

    def greet(to_tile, to_subset):
        pl.semaphore_signal(barrier, inc=1, device_id=(to_tile, to_subset), device_id_type=MESH)

    greet(neighbours["in"], subset)
    greet(neighbours["x"], subset)

    @pl.when(middle)
    def _():
        greet(neighbours["out"], subset)

    for peer in (peers[0], peers[2]):
        greet(tile, peer)
    load_own.start()
    for load in load_small:
        load.start()
    load_own.wait()
    load_weights.start()
    load_spread.start()
    pl.semaphore_wait(barrier, 4 + jnp.where(middle, 1, 0))

    def send(way, origin, quarter):
        return pltpu.make_async_remote_copy(
            src_ref=gathered.at[origin, quarter],
            dst_ref=gathered.at[origin, quarter],
            send_sem=send_sem.at[("x", "in", "out").index(way), origin, quarter],
            recv_sem=recv_sem.at[origin, quarter],
            device_id=(neighbours[way], subset),
            device_id_type=MESH,
        )

    def wait_arrival(origin, quarter):
        pltpu.make_async_remote_copy(
            src_ref=gathered.at[origin, quarter],
            dst_ref=gathered.at[origin, quarter],
            send_sem=send_sem.at[0, 0, 0],
            recv_sem=recv_sem.at[origin, quarter],
            device_id=(neighbours["x"], subset),
            device_id_type=MESH,
        ).wait_recv()

    def send_own(quarters_now):
        for quarter in quarters_now:
            send("in", tile, quarter).start()

            @pl.when(middle)
            def _():
                send("out", tile, quarter).start()

            send("x", tile, (quarter + jnp.where(end, 2, 0)) % quarters).start()

    send_own(range(2))

    @pl.when(core == 0)
    def _():
        send_own(range(2, quarters))
        send("in", tile, 0).wait_send()
        pl.semaphore_signal(turn_sem, inc=1, device_id=(tile, peers[2]), device_id_type=MESH)

    @pl.when(core == 1)
    def _():
        pl.semaphore_wait(turn_sem, 1)
        send_own(range(2, quarters))

    pl.semaphore_signal(far_sem, inc=1, device_id=(tile, peers[0]), device_id_type=MESH)
    for load in load_small:
        load.wait()
    slots = weights.shape[0]
    listing = aperture_ref[0, pl.ds(tile, 1), :]
    slot = lax.broadcasted_iota(jnp.int32, (slots, slots), 0)
    block = lax.broadcasted_iota(jnp.int32, (slots, slots), 1)
    named = jnp.broadcast_to(listing, (slots, slots)).T
    match = (named == block) & (slot < counts_ref[0, tile])
    lookup[...] = jnp.broadcast_to(
        jnp.sum(jnp.where(match, slot + 1, 0), axis=0, keepdims=True) - 1, lookup.shape
    )
    publish = pltpu.make_async_copy(lookup, slot_of, load_sem.at[3])
    publish.start()

    half_taps = (taps_ref.shape[1] - 1) // 2
    band[...] = jnp.zeros_like(band)
    band[0:2, 0 : taps_ref.shape[1]] = taps_ref[...].astype(jnp.float32)
    row = lax.broadcasted_iota(jnp.int32, (samples, samples), 0)
    gap = lax.broadcasted_iota(jnp.int32, (samples, samples), 1) - row
    inside = (gap <= half_taps) & (gap >= -half_taps)
    for channel in range(2):
        centred = pltpu.roll(band[...], samples - half_taps, 1)[channel : channel + 1, :]
        shifted = jnp.broadcast_to(centred, (samples, samples))
        shift = 1
        while shift < samples:
            shifted = jnp.where((row // shift) % 2 == 1, pltpu.roll(shifted, shift, 1), shifted)
            shift *= 2
        operator[:, channel * samples : (channel + 1) * samples] = jnp.where(
            inside, shifted, 0.0
        ).astype(operator.dtype)
    total[...] = jnp.zeros_like(total)

    def tile_at(position, column):
        return jnp.where(low, position, rows_z - 1 - position) * 2 + jnp.where(
            column == 0, x, other
        )

    def arrival(event, side):
        if side == 0:
            late = event >= 12
            end_column = jnp.where(late, 1, 0)
            end_position = jnp.where(late, 3, 1 + event // 4)
            end_quarter = jnp.where(late, event - 10, event % 4)
            end_x = event < 10
            end_in = event < 0
        else:
            end_column = 1
            end_position = event // 4
            end_quarter = jnp.where(event < 4, (event + 2) % 4, event % 4)
            end_x = event < 0
            end_in = event < 4
        number = 2 * event + side
        turn = number < 24
        stream = jnp.where(turn, number % 3, 1 + number % 2)
        index = jnp.where(turn, number // 3, number // 2 - 4)
        from_end = stream == 0
        from_middle = stream == 1
        from_x = stream == 2
        relayed = (from_end & (index >= 4)) | (from_middle & (index >= 8))
        column = jnp.where(from_x | relayed, 1, 0)
        position = jnp.where(
            from_end, 0, jnp.where(from_middle, jnp.where(relayed, 3, 2 + index // 4), 1 + index // 4)
        )
        quarter = jnp.where(relayed, (index + 2) % 4, index % 4)
        mid_x = from_middle & (index < 6)
        mid_in = from_end & (index < 6)
        mid_out = from_middle
        origin = tile_at(
            jnp.where(end, end_position, position), jnp.where(end, end_column, column)
        )
        ways = {
            "x": (end & end_x) | (middle & mid_x),
            "in": (end & end_in) | (middle & mid_in),
            "out": middle & mid_out,
        }
        return origin, jnp.where(end, end_quarter, quarter), ways

    def each_way(event, side, act):
        origin, quarter, ways = arrival(event, side)
        for way in ("out", "in", "x"):

            @pl.when(ways[way])
            def _():
                act(send(way, origin, quarter))

    def take(event):
        for side in range(2):
            origin, quarter, _ = arrival(event, side)
            wait_arrival(origin, quarter)
            each_way(event, side, lambda copy: copy.start())

    lanes = lax.broadcasted_iota(jnp.int32, (1, 2 * chunk_rows), 1)
    member = (lanes // block_rows) % chunk_blocks

    def compute(chunks):
        rows = jnp.concatenate([gathered[origin, quarter] for origin, quarter in chunks], axis=0)
        filtered = jnp.dot(rows, operator[...], preferred_element_type=jnp.float32).astype(
            jnp.bfloat16
        )
        image = None
        for at, (origin, quarter) in enumerate(chunks):
            first = at * chunk_rows
            blocks = jnp.concatenate(
                [
                    filtered[first : first + chunk_rows, 0:samples],
                    filtered[first : first + chunk_rows, samples : 2 * samples],
                ],
                axis=0,
            )
            base = origin * block_count + quarter * chunk_blocks
            found = [slot_of[0, base + index] for index in range(chunk_blocks)]
            picks = [jnp.maximum(value, 0) for value in found]
            gains = [jnp.where(value >= 0, 1.0, 0.0) for value in found]
            stacked = jnp.concatenate([weights[pick] for pick in picks], axis=0)
            product = lax.dot_general(
                stacked, blocks, (((1,), (1,)), ((), ())), preferred_element_type=jnp.float32
            )
            interp = product[0:taus]
            alive = jnp.full((1, 2 * chunk_rows), gains[0], jnp.float32)
            for index in range(1, chunk_blocks):
                here = member == index
                interp = jnp.where(here, product[index * taus : (index + 1) * taus], interp)
                alive = jnp.where(here, gains[index], alive)
            interp = (interp * alive).astype(jnp.bfloat16)
            columns = jnp.concatenate(
                [spread[pick, channel] for channel in range(2) for pick in picks], axis=0
            )
            part = jnp.dot(interp, columns, preferred_element_type=jnp.float32)
            image = part if image is None else image + part
        total[...] += image

    take(0)
    load_weights.wait()
    load_spread.wait()
    publish.wait()

    def step(number, carry):
        caught_up = number >= 6

        @pl.when((number == 1) | (number == 3) | (number == 5) | caught_up)
        def _():
            take(jnp.where(caught_up, number - 2, (number + 1) // 2))

        chunks = []
        for side in range(2):
            origin, quarter, _ = arrival(jnp.maximum(number - 2, 0), side)
            own = number < 2
            chunks.append(
                (jnp.where(own, tile, origin), jnp.where(own, 2 * number + side, quarter))
            )
        compute(chunks)
        return carry

    lax.fori_loop(0, events + 2, step, 0)

    pl.semaphore_wait(far_sem, 1)
    exchanges = []
    for at, peer in enumerate(peers):
        outgoing[at] = total[pl.ds(pl.multiple_of(peer * share, share), share), :].astype(
            outgoing.dtype
        )
        copy = pltpu.make_async_remote_copy(
            src_ref=outgoing.at[at],
            dst_ref=parts.at[at],
            send_sem=part_send_sem.at[at],
            recv_sem=part_recv_sem.at[at],
            device_id=(tile, peer),
            device_id_type=MESH,
        )
        copy.start()
        exchanges.append(copy)

    for quarter in range(quarters):

        @pl.when((core == 1) | (quarter >= 1))
        def _():
            send("in", tile, quarter).wait_send()

        @pl.when(middle)
        def _():
            send("out", tile, quarter).wait_send()

        send("x", tile, quarter).wait_send()

    def sent(event, carry):
        for side in range(2):
            each_way(event, side, lambda copy: copy.wait_send())
        return carry

    lax.fori_loop(0, events, sent, 0)

    result = total[pl.ds(pl.multiple_of(subset * share, share), share), :]
    for at, copy in enumerate(exchanges):
        copy.wait_recv()
        result = result + parts[at].astype(jnp.float32)
    out_ref[...] = result
    for copy in exchanges:
        copy.wait_send()


def keep(array):
    return pltpu.with_memory_space_constraint(array, pltpu.HBM)


def gather_per_device(traces, taps, aperture, counts, time_weights, amplitudes):
    tiles = lax.axis_size("tile")
    subsets = lax.axis_size("trace")
    _, block_count, block_rows, samples = traces.shape
    slots, taus = time_weights.shape[2:4]
    columns = amplitudes.shape[-1]
    chunk_rows = block_count * block_rows // quarters
    share = taus // subsets
    vmem = pl.BlockSpec(memory_space=pltpu.VMEM)
    hbm = pl.BlockSpec(memory_space=pl.ANY)
    image = pl.pallas_call(
        migrate_kernel,
        out_shape=jax.ShapeDtypeStruct((share, columns), jnp.float32),
        in_specs=[hbm] * 6,
        out_specs=vmem,
        scratch_shapes=[
            pltpu.VMEM((tiles, quarters, chunk_rows, samples), jnp.bfloat16),
            pltpu.VMEM((slots, taus, samples), jnp.bfloat16),
            pltpu.VMEM((slots, 2, block_rows, columns), jnp.bfloat16),
            pltpu.VMEM((samples, 2 * samples), jnp.bfloat16),
            pltpu.VMEM((taus, columns), jnp.float32),
            pltpu.VMEM((subsets - 1, share, columns), jnp.bfloat16),
            pltpu.VMEM((subsets - 1, share, columns), jnp.bfloat16),
            pltpu.SMEM(counts.shape, jnp.int32),
            pltpu.VMEM(aperture.shape, jnp.int32),
            pltpu.VMEM(taps.shape, taps.dtype),
            pltpu.VMEM((8, samples), jnp.float32),
            pltpu.VMEM((8, slots), jnp.int32),
            pltpu.SMEM((8, slots), jnp.int32),
            pltpu.SemaphoreType.DMA((tiles, quarters)),
            pltpu.SemaphoreType.DMA((3, tiles, quarters)),
            pltpu.SemaphoreType.DMA((7,)),
            pltpu.SemaphoreType.DMA((subsets - 1,)),
            pltpu.SemaphoreType.DMA((subsets - 1,)),
            pltpu.SemaphoreType.REGULAR,
            pltpu.SemaphoreType.REGULAR,
        ],
        compiler_params=pltpu.CompilerParams(
            collective_id=0, has_side_effects=True, vmem_limit_bytes=48 * 1024 * 1024
        ),
    )(
        keep(counts),
        keep(aperture),
        keep(taps),
        keep(traces.reshape(quarters, chunk_rows, samples)),
        keep(time_weights[0, 0]),
        keep(amplitudes[0, 0]),
    )
    return image[None]


def filter_matrix(taps, samples):
    width = taps.shape[1]
    center = (width - 1) // 2
    offset = jnp.arange(samples)[:, None] - jnp.arange(samples)[None, :] + center
    table = (offset[:, :, None] == jnp.arange(width)[None, None, :]).astype(jnp.bfloat16)
    return jnp.einsum("ct,nmt->cnm", taps, table, preferred_element_type=jnp.float32).astype(
        jnp.bfloat16
    )


def exchange_per_device(traces, taps, aperture, counts, time_weights, amplitudes):
    tiles = lax.axis_size("tile")
    myself = lax.axis_index("tile")
    block_count = traces.shape[1]
    samples = traces.shape[3]
    slots = aperture.shape[2]
    capacity = max(2, slots // tiles)
    listing = aperture[0]
    filled = counts[0]
    owners = listing // block_count
    within = listing - owners * block_count
    order = jnp.arange(slots)
    earlier = order[None, :] < order[:, None]
    rank = jnp.sum((owners[:, :, None] == owners[:, None, :]) & earlier[None], axis=2)
    alive_slots = order[None, :] < filled[:, None]
    mine = (owners == myself) & alive_slots
    rank_onehot = (
        (rank[:, :, None] == jnp.arange(capacity)[None, None, :]) & mine[:, :, None]
    ).astype(jnp.bfloat16)
    local_onehot = (within[:, :, None] == jnp.arange(block_count)[None, None, :]).astype(
        jnp.bfloat16
    )
    select = jnp.einsum(
        "ksc,ksl->kcl", rank_onehot, local_onehot, preferred_element_type=jnp.float32
    ).astype(jnp.bfloat16)
    operator = filter_matrix(taps, samples)
    own_owner = lax.dynamic_index_in_dim(owners, myself, 0, keepdims=False)
    own_rank = lax.dynamic_index_in_dim(rank, myself, 0, keepdims=False)
    own_fill = lax.dynamic_index_in_dim(filled, myself, 0, keepdims=False)
    source_slot = own_owner * capacity + own_rank
    arrived_rows = tiles * capacity

    def pick_rows(positions):
        return (positions[:, None] == jnp.arange(arrived_rows)[None, :]).astype(jnp.bfloat16)

    filtered = jnp.einsum(
        "cnm,kbm->kcbn", operator, traces[0], preferred_element_type=jnp.float32
    ).astype(jnp.bfloat16)
    outgoing = jnp.einsum(
        "kcl,lqbn->kcqbn", select, filtered, preferred_element_type=jnp.float32
    ).astype(jnp.bfloat16)
    arrived = lax.all_to_all(outgoing, "tile", split_axis=0, concat_axis=0, tiled=True)
    arrived = arrived.reshape((arrived_rows,) + arrived.shape[2:])

    def fetch(positions):
        return jnp.einsum(
            "gq,qcbn->gcbn", pick_rows(positions), arrived, preferred_element_type=jnp.float32
        ).astype(jnp.bfloat16)

    weights = time_weights[0, 0]
    spread = amplitudes[0, 0]

    def add_group(index, total):
        start = index * group_slots
        positions = lax.dynamic_slice_in_dim(source_slot, start, group_slots, 0)
        blocks = fetch(positions)
        part_weights = lax.dynamic_slice_in_dim(weights, start, group_slots, 0)
        part_spread = lax.dynamic_slice_in_dim(spread, start, group_slots, 0)
        alive = (start + jnp.arange(group_slots) < own_fill).astype(jnp.float32)
        interp = jnp.einsum(
            "gtn,gcbn->gcbt", part_weights, blocks, preferred_element_type=jnp.float32
        )
        interp = (interp * alive[:, None, None, None]).astype(jnp.bfloat16)
        return total + jnp.einsum(
            "gcbt,gcbp->tp", interp, part_spread, preferred_element_type=jnp.float32
        )

    rounds = (own_fill + group_slots - 1) // group_slots
    partial_value = lax.fori_loop(
        0, rounds, add_group, jnp.zeros((weights.shape[1], spread.shape[-1]), jnp.float32)
    )
    image = lax.psum_scatter(partial_value, "trace", scatter_dimension=0, tiled=True)
    return image[None]


def per_device(traces, taps, aperture, counts, time_weights, amplitudes):
    tiles = lax.axis_size("tile")
    every_block = traces.shape[1] * tiles
    quarter = traces.shape[1] // quarters
    gathers = (
        every_block == aperture.shape[2]
        and tiles == 2 * rows_z
        and lax.axis_size("trace") == 4
        and quarter * quarters == traces.shape[1]
    )
    form = gather_per_device if gathers else exchange_per_device
    return form(traces, taps, aperture, counts, time_weights, amplitudes)


def solution(mesh):
    placed = (
        P("trace", "tile", None, None),
        P(),
        P("trace", None, None),
        P("trace", None),
        P("trace", "tile", None, None, None),
        P("trace", "tile", None, None, None, None),
    )
    return jax.shard_map(
        per_device, mesh=mesh, in_specs=placed, out_specs=P("tile", "trace", None), check_vma=False
    )
```

```python
import jax
import jax.numpy as jnp
from jax import lax
from jax.experimental import pallas as pl
from jax.experimental.pallas import tpu as pltpu
from jax.sharding import PartitionSpec as P

group_slots = 8
quarters = 4
rows_z = 4
events = 14
MESH = pl.DeviceIdType.MESH


def migrate_kernel(
    counts_hbm,
    aperture_hbm,
    taps_hbm,
    traces_ref,
    weights_ref,
    spread_ref,
    out_ref,
    gathered,
    weights,
    spread,
    operator,
    total,
    outgoing,
    parts,
    counts_ref,
    aperture_ref,
    taps_ref,
    band,
    lookup,
    slot_of,
    recv_sem,
    send_sem,
    load_sem,
    part_send_sem,
    part_recv_sem,
    far_sem,
    near_sem,
    gift,
    gift_recv_sem,
    staged_weights,
    staged_spread,
    lent_weights,
    lent_spread,
    lend_sem,
    lent_sem,
):
    tile = lax.axis_index("tile")
    subset = lax.axis_index("trace")
    z = tile // 2
    x = tile % 2
    other = 1 - x
    low = z < rows_z // 2
    inward = jnp.where(low, 1, -1)
    place = jnp.where(low, z, rows_z - 1 - z)
    end = place == 0
    middle = place == 1
    samples = operator.shape[0]
    taus = weights.shape[1]
    block_rows = spread.shape[2]
    chunk_rows = gathered.shape[2]
    chunk_blocks = chunk_rows // block_rows
    block_count = chunk_blocks * quarters
    share = out_ref.shape[0]

    load_small = [
        pltpu.make_async_copy(src, dst, load_sem.at[4 + at])
        for at, (src, dst) in enumerate(
            ((counts_hbm, counts_ref), (aperture_hbm, aperture_ref), (taps_hbm, taps_ref))
        )
    ]
    load_own = pltpu.make_async_copy(traces_ref, gathered.at[tile], load_sem.at[0])
    load_weights = pltpu.make_async_copy(weights_ref, weights, load_sem.at[1])
    load_spread = pltpu.make_async_copy(spread_ref, spread, load_sem.at[2])

    row_y = subset // 2
    core = subset % 2
    across_y = (1 - row_y) * 2
    giver = end & (core == 0)
    taker = end & (core == 1)
    peers = (across_y + core, across_y + 1 - core, row_y * 2 + 1 - core)

    barrier = pltpu.get_barrier_semaphore()
    neighbours = {
        "x": z * 2 + other,
        "in": tile + 2 * inward,
        "out": tile - 2 * inward,
    }

    def greet(to_tile, to_subset):
        pl.semaphore_signal(barrier, inc=1, device_id=(to_tile, to_subset), device_id_type=MESH)

    greet(neighbours["in"], subset)
    greet(neighbours["x"], subset)

    @pl.when(middle)
    def _():
        greet(neighbours["out"], subset)

    for peer in (peers[0], peers[2]):
        greet(tile, peer)
    load_own.start()
    for load in load_small:
        load.start()
    load_own.wait()
    load_weights.start()
    load_spread.start()
    pl.semaphore_wait(barrier, 4 + jnp.where(middle, 1, 0))

    def send(way, origin, quarter):
        return pltpu.make_async_remote_copy(
            src_ref=gathered.at[origin, quarter],
            dst_ref=gathered.at[origin, quarter],
            send_sem=send_sem.at[("x", "in", "out").index(way), origin, quarter],
            recv_sem=recv_sem.at[origin, quarter],
            device_id=(neighbours[way], subset),
            device_id_type=MESH,
        )

    def wait_arrival(origin, quarter):
        pltpu.make_async_remote_copy(
            src_ref=gathered.at[origin, quarter],
            dst_ref=gathered.at[origin, quarter],
            send_sem=send_sem.at[0, 0, 0],
            recv_sem=recv_sem.at[origin, quarter],
            device_id=(neighbours["x"], subset),
            device_id_type=MESH,
        ).wait_recv()

    for quarter in range(quarters):
        send("in", tile, quarter).start()

        @pl.when(middle)
        def _():
            send("out", tile, quarter).start()

        send("x", tile, (quarter + jnp.where(end, 2, 0)) % quarters).start()

    @pl.when(giver)
    def _():
        for neighbour in ("in", "x"):
            pl.semaphore_signal(
                near_sem,
                inc=1,
                device_id=(neighbours[neighbour], subset),
                device_id_type=MESH,
            )

    pl.semaphore_signal(far_sem, inc=1, device_id=(tile, peers[0]), device_id_type=MESH)
    for load in load_small:
        load.wait()
    slots = weights.shape[0]
    listing = aperture_ref[0, pl.ds(tile, 1), :]
    slot = lax.broadcasted_iota(jnp.int32, (slots, slots), 0)
    block = lax.broadcasted_iota(jnp.int32, (slots, slots), 1)
    named = jnp.broadcast_to(listing, (slots, slots)).T
    match = (named == block) & (slot < counts_ref[0, tile])
    lookup[...] = jnp.broadcast_to(
        jnp.sum(jnp.where(match, slot + 1, 0), axis=0, keepdims=True) - 1, lookup.shape
    )
    publish = pltpu.make_async_copy(lookup, slot_of, load_sem.at[3])
    publish.start()

    half_taps = (taps_ref.shape[1] - 1) // 2
    band[...] = jnp.zeros_like(band)
    band[0:2, 0 : taps_ref.shape[1]] = taps_ref[...].astype(jnp.float32)
    row = lax.broadcasted_iota(jnp.int32, (samples, samples), 0)
    gap = lax.broadcasted_iota(jnp.int32, (samples, samples), 1) - row
    inside = (gap <= half_taps) & (gap >= -half_taps)
    for channel in range(2):
        centred = pltpu.roll(band[...], samples - half_taps, 1)[channel : channel + 1, :]
        shifted = jnp.broadcast_to(centred, (samples, samples))
        shift = 1
        while shift < samples:
            shifted = jnp.where((row // shift) % 2 == 1, pltpu.roll(shifted, shift, 1), shifted)
            shift *= 2
        operator[:, channel * samples : (channel + 1) * samples] = jnp.where(
            inside, shifted, 0.0
        ).astype(operator.dtype)
    total[...] = jnp.zeros_like(total)

    def tile_at(position, column):
        return jnp.where(low, position, rows_z - 1 - position) * 2 + jnp.where(
            column == 0, x, other
        )

    def arrival(event, side):
        if side == 0:
            late = event >= 12
            end_column = jnp.where(late, 1, 0)
            end_position = jnp.where(late, 3, 1 + event // 4)
            end_quarter = jnp.where(late, event - 10, event % 4)
            end_x = event < 10
            end_in = event < 0
        else:
            end_column = 1
            end_position = event // 4
            end_quarter = jnp.where(event < 4, (event + 2) % 4, event % 4)
            end_x = event < 0
            end_in = event < 4
        number = 2 * event + side
        turn = number < 24
        stream = jnp.where(turn, number % 3, 1 + number % 2)
        index = jnp.where(turn, number // 3, number // 2 - 4)
        from_end = stream == 0
        from_middle = stream == 1
        from_x = stream == 2
        relayed = (from_end & (index >= 4)) | (from_middle & (index >= 8))
        column = jnp.where(from_x | relayed, 1, 0)
        position = jnp.where(
            from_end, 0, jnp.where(from_middle, jnp.where(relayed, 3, 2 + index // 4), 1 + index // 4)
        )
        quarter = jnp.where(relayed, (index + 2) % 4, index % 4)
        mid_x = from_middle & (index < 6)
        mid_in = from_end & (index < 6)
        mid_out = from_middle
        origin = tile_at(
            jnp.where(end, end_position, position), jnp.where(end, end_column, column)
        )
        ways = {
            "x": (end & end_x) | (middle & mid_x),
            "in": (end & end_in) | (middle & mid_in),
            "out": middle & mid_out,
        }
        return origin, jnp.where(end, end_quarter, quarter), ways

    def give(way, origin, quarter):
        return pltpu.make_async_remote_copy(
            src_ref=gathered.at[origin, quarter],
            dst_ref=gift.at[("out", "x").index(way)],
            send_sem=send_sem.at[("x", "in", "out").index(way), origin, quarter],
            recv_sem=gift_recv_sem.at[("out", "x").index(way)],
            device_id=(neighbours[way], peers[2]),
            device_id_type=MESH,
        )

    def each_way(event, side, act, before_gift):
        origin, quarter, ways = arrival(event, side)
        gifts = {"in": False, "out": False, "x": False}
        if side == 0:
            gifts["out"] = middle & (core == 0) & (event == 13)
            gifts["x"] = end & (core == 0) & (event == 9)
        for way in ("out", "in", "x"):
            given = gifts[way]

            @pl.when(ways[way] & jnp.logical_not(given))
            def _():
                act(send(way, origin, quarter))

            if given is not False:

                @pl.when(given)
                def _():
                    before_gift()
                    act(give(way, origin, quarter))

    def take(event):
        for side in range(2):
            origin, quarter, _ = arrival(event, side)
            wait_arrival(origin, quarter)
            each_way(
                event,
                side,
                lambda copy: copy.start(),
                lambda: pl.semaphore_wait(near_sem, 1),
            )

    lanes = lax.broadcasted_iota(jnp.int32, (1, 2 * chunk_rows), 1)
    member = (lanes // block_rows) % chunk_blocks

    def migrate(rows, groups):
        filtered = jnp.dot(rows, operator[...], preferred_element_type=jnp.float32).astype(
            jnp.bfloat16
        )
        image = None
        for at, (stacked, columns, gains) in enumerate(groups):
            first = at * chunk_rows
            blocks = jnp.concatenate(
                [
                    filtered[first : first + chunk_rows, 0:samples],
                    filtered[first : first + chunk_rows, samples : 2 * samples],
                ],
                axis=0,
            )
            product = lax.dot_general(
                stacked, blocks, (((1,), (1,)), ((), ())), preferred_element_type=jnp.float32
            )
            interp = product[0:taus]
            for index in range(1, chunk_blocks):
                interp = jnp.where(
                    member == index, product[index * taus : (index + 1) * taus], interp
                )
            if gains is not None:
                alive = jnp.full((1, 2 * chunk_rows), gains[0], jnp.float32)
                for index in range(1, chunk_blocks):
                    alive = jnp.where(member == index, gains[index], alive)
                interp = interp * alive
            interp = interp.astype(jnp.bfloat16)
            part = jnp.dot(interp, columns, preferred_element_type=jnp.float32)
            image = part if image is None else image + part
        total[...] += image

    def look_up(origin, quarter):
        base = origin * block_count + quarter * chunk_blocks
        found = [slot_of[0, base + index] for index in range(chunk_blocks)]
        picks = [jnp.maximum(value, 0) for value in found]
        gains = [jnp.where(value >= 0, 1.0, 0.0) for value in found]
        return picks, gains

    def compute(chunks):
        rows = jnp.concatenate([gathered[origin, quarter] for origin, quarter in chunks], axis=0)
        groups = []
        for origin, quarter in chunks:
            picks, gains = look_up(origin, quarter)
            stacked = jnp.concatenate([weights[pick] for pick in picks], axis=0)
            columns = jnp.concatenate(
                [spread[pick, channel] for channel in range(2) for pick in picks], axis=0
            )
            groups.append((stacked, columns, gains))
        migrate(rows, groups)

    lending = [
        pltpu.make_async_remote_copy(
            src_ref=src,
            dst_ref=dst,
            send_sem=lend_sem.at[at],
            recv_sem=lent_sem.at[at],
            device_id=(tile, peers[2]),
            device_id_type=MESH,
        )
        for at, (src, dst) in enumerate(
            ((staged_weights, lent_weights), (staged_spread, lent_spread))
        )
    ]

    def lend():
        for at, quarter in enumerate((3, 1)):
            picks, gains = look_up(tile_at(3, 1), quarter)
            for index, (pick, gain) in enumerate(zip(picks, gains, strict=True)):
                staged_weights[at * chunk_blocks + index] = weights[pick]
                staged_spread[at * chunk_blocks + index] = (
                    spread[pick].astype(jnp.float32) * gain
                ).astype(staged_spread.dtype)
        for copy in lending:
            copy.start()

    def work_on_gift():
        for copy in lending:
            copy.wait_recv()
        for way in ("out", "x"):
            give(way, 0, 0).wait_recv()
        groups = []
        for at in range(2):
            mine = range(at * chunk_blocks, (at + 1) * chunk_blocks)
            stacked = jnp.concatenate([lent_weights[index] for index in mine], axis=0)
            columns = jnp.concatenate(
                [lent_spread[index, channel] for channel in range(2) for index in mine], axis=0
            )
            groups.append((stacked, columns, None))
        migrate(jnp.concatenate([gift[0], gift[1]], axis=0), groups)

    take(0)

    @pl.when(middle)
    def _():
        take(1)

    load_weights.wait()
    load_spread.wait()
    publish.wait()

    def step(number, carry):
        pl.when(giver & (number == 8))(lend)
        caught_up = number >= 6
        end_takes = (number == 1) | (number == 3) | (number == 5) | caught_up
        middle_takes = number + 2 < events
        end_event = jnp.where(caught_up, number - 2, (number + 1) // 2)

        @pl.when((end & end_takes) | (middle & middle_takes))
        def _():
            take(jnp.where(end, end_event, number + 2))

        chunks = []
        for side in range(2):
            origin, quarter, _ = arrival(jnp.maximum(number - 2, 0), side)
            own = number < 2
            chunks.append(
                (jnp.where(own, tile, origin), jnp.where(own, 2 * number + side, quarter))
            )
        compute(chunks)
        return carry

    lax.fori_loop(0, events + 2 - jnp.where(giver, 1, 0), step, 0)
    pl.when(taker)(work_on_gift)

    pl.semaphore_wait(far_sem, 1)
    exchanges = []
    for at, peer in enumerate(peers):
        outgoing[at] = total[pl.ds(pl.multiple_of(peer * share, share), share), :].astype(
            outgoing.dtype
        )
        copy = pltpu.make_async_remote_copy(
            src_ref=outgoing.at[at],
            dst_ref=parts.at[at],
            send_sem=part_send_sem.at[at],
            recv_sem=part_recv_sem.at[at],
            device_id=(tile, peer),
            device_id_type=MESH,
        )
        copy.start()
        exchanges.append(copy)

    for quarter in range(quarters):
        send("in", tile, quarter).wait_send()

        @pl.when(middle)
        def _():
            send("out", tile, quarter).wait_send()

        send("x", tile, quarter).wait_send()

    def sent(event, carry):
        for side in range(2):
            each_way(event, side, lambda copy: copy.wait_send(), lambda: None)
        return carry

    lax.fori_loop(0, events, sent, 0)

    result = total[pl.ds(pl.multiple_of(subset * share, share), share), :]
    for at, copy in enumerate(exchanges):
        copy.wait_recv()
        result = result + parts[at].astype(jnp.float32)
    out_ref[...] = result
    for copy in exchanges:
        copy.wait_send()

    @pl.when(giver)
    def _():
        for copy in lending:
            copy.wait_send()


def keep(array):
    return pltpu.with_memory_space_constraint(array, pltpu.HBM)


def gather_per_device(traces, taps, aperture, counts, time_weights, amplitudes):
    tiles = lax.axis_size("tile")
    subsets = lax.axis_size("trace")
    _, block_count, block_rows, samples = traces.shape
    slots, taus = time_weights.shape[2:4]
    columns = amplitudes.shape[-1]
    chunk_rows = block_count * block_rows // quarters
    share = taus // subsets
    lent_blocks = 2 * block_count // quarters
    vmem = pl.BlockSpec(memory_space=pltpu.VMEM)
    hbm = pl.BlockSpec(memory_space=pl.ANY)
    image = pl.pallas_call(
        migrate_kernel,
        out_shape=jax.ShapeDtypeStruct((share, columns), jnp.float32),
        in_specs=[hbm] * 6,
        out_specs=vmem,
        scratch_shapes=[
            pltpu.VMEM((tiles, quarters, chunk_rows, samples), jnp.bfloat16),
            pltpu.VMEM((slots, taus, samples), jnp.bfloat16),
            pltpu.VMEM((slots, 2, block_rows, columns), jnp.bfloat16),
            pltpu.VMEM((samples, 2 * samples), jnp.bfloat16),
            pltpu.VMEM((taus, columns), jnp.float32),
            pltpu.VMEM((subsets - 1, share, columns), jnp.bfloat16),
            pltpu.VMEM((subsets - 1, share, columns), jnp.bfloat16),
            pltpu.SMEM(counts.shape, jnp.int32),
            pltpu.VMEM(aperture.shape, jnp.int32),
            pltpu.VMEM(taps.shape, taps.dtype),
            pltpu.VMEM((8, samples), jnp.float32),
            pltpu.VMEM((8, slots), jnp.int32),
            pltpu.SMEM((8, slots), jnp.int32),
            pltpu.SemaphoreType.DMA((tiles, quarters)),
            pltpu.SemaphoreType.DMA((3, tiles, quarters)),
            pltpu.SemaphoreType.DMA((7,)),
            pltpu.SemaphoreType.DMA((subsets - 1,)),
            pltpu.SemaphoreType.DMA((subsets - 1,)),
            pltpu.SemaphoreType.REGULAR,
            pltpu.SemaphoreType.REGULAR,
            pltpu.VMEM((2, chunk_rows, samples), jnp.bfloat16),
            pltpu.SemaphoreType.DMA((2,)),
            pltpu.VMEM((lent_blocks, taus, samples), jnp.bfloat16),
            pltpu.VMEM((lent_blocks, 2, block_rows, columns), jnp.bfloat16),
            pltpu.VMEM((lent_blocks, taus, samples), jnp.bfloat16),
            pltpu.VMEM((lent_blocks, 2, block_rows, columns), jnp.bfloat16),
            pltpu.SemaphoreType.DMA((2,)),
            pltpu.SemaphoreType.DMA((2,)),
        ],
        compiler_params=pltpu.CompilerParams(
            collective_id=0, has_side_effects=True, vmem_limit_bytes=48 * 1024 * 1024
        ),
    )(
        keep(counts),
        keep(aperture),
        keep(taps),
        keep(traces.reshape(quarters, chunk_rows, samples)),
        keep(time_weights[0, 0]),
        keep(amplitudes[0, 0]),
    )
    return image[None]


def filter_matrix(taps, samples):
    width = taps.shape[1]
    center = (width - 1) // 2
    offset = jnp.arange(samples)[:, None] - jnp.arange(samples)[None, :] + center
    table = (offset[:, :, None] == jnp.arange(width)[None, None, :]).astype(jnp.bfloat16)
    return jnp.einsum("ct,nmt->cnm", taps, table, preferred_element_type=jnp.float32).astype(
        jnp.bfloat16
    )


def exchange_per_device(traces, taps, aperture, counts, time_weights, amplitudes):
    tiles = lax.axis_size("tile")
    myself = lax.axis_index("tile")
    block_count = traces.shape[1]
    samples = traces.shape[3]
    slots = aperture.shape[2]
    capacity = max(2, slots // tiles)
    listing = aperture[0]
    filled = counts[0]
    owners = listing // block_count
    within = listing - owners * block_count
    order = jnp.arange(slots)
    earlier = order[None, :] < order[:, None]
    rank = jnp.sum((owners[:, :, None] == owners[:, None, :]) & earlier[None], axis=2)
    alive_slots = order[None, :] < filled[:, None]
    mine = (owners == myself) & alive_slots
    rank_onehot = (
        (rank[:, :, None] == jnp.arange(capacity)[None, None, :]) & mine[:, :, None]
    ).astype(jnp.bfloat16)
    local_onehot = (within[:, :, None] == jnp.arange(block_count)[None, None, :]).astype(
        jnp.bfloat16
    )
    select = jnp.einsum(
        "ksc,ksl->kcl", rank_onehot, local_onehot, preferred_element_type=jnp.float32
    ).astype(jnp.bfloat16)
    operator = filter_matrix(taps, samples)
    own_owner = lax.dynamic_index_in_dim(owners, myself, 0, keepdims=False)
    own_rank = lax.dynamic_index_in_dim(rank, myself, 0, keepdims=False)
    own_fill = lax.dynamic_index_in_dim(filled, myself, 0, keepdims=False)
    source_slot = own_owner * capacity + own_rank
    arrived_rows = tiles * capacity

    def pick_rows(positions):
        return (positions[:, None] == jnp.arange(arrived_rows)[None, :]).astype(jnp.bfloat16)

    filtered = jnp.einsum(
        "cnm,kbm->kcbn", operator, traces[0], preferred_element_type=jnp.float32
    ).astype(jnp.bfloat16)
    outgoing = jnp.einsum(
        "kcl,lqbn->kcqbn", select, filtered, preferred_element_type=jnp.float32
    ).astype(jnp.bfloat16)
    arrived = lax.all_to_all(outgoing, "tile", split_axis=0, concat_axis=0, tiled=True)
    arrived = arrived.reshape((arrived_rows,) + arrived.shape[2:])

    def fetch(positions):
        return jnp.einsum(
            "gq,qcbn->gcbn", pick_rows(positions), arrived, preferred_element_type=jnp.float32
        ).astype(jnp.bfloat16)

    weights = time_weights[0, 0]
    spread = amplitudes[0, 0]

    def add_group(index, total):
        start = index * group_slots
        positions = lax.dynamic_slice_in_dim(source_slot, start, group_slots, 0)
        blocks = fetch(positions)
        part_weights = lax.dynamic_slice_in_dim(weights, start, group_slots, 0)
        part_spread = lax.dynamic_slice_in_dim(spread, start, group_slots, 0)
        alive = (start + jnp.arange(group_slots) < own_fill).astype(jnp.float32)
        interp = jnp.einsum(
            "gtn,gcbn->gcbt", part_weights, blocks, preferred_element_type=jnp.float32
        )
        interp = (interp * alive[:, None, None, None]).astype(jnp.bfloat16)
        return total + jnp.einsum(
            "gcbt,gcbp->tp", interp, part_spread, preferred_element_type=jnp.float32
        )

    rounds = (own_fill + group_slots - 1) // group_slots
    partial_value = lax.fori_loop(
        0, rounds, add_group, jnp.zeros((weights.shape[1], spread.shape[-1]), jnp.float32)
    )
    image = lax.psum_scatter(partial_value, "trace", scatter_dimension=0, tiled=True)
    return image[None]


def per_device(traces, taps, aperture, counts, time_weights, amplitudes):
    tiles = lax.axis_size("tile")
    every_block = traces.shape[1] * tiles
    quarter = traces.shape[1] // quarters
    gathers = (
        every_block == aperture.shape[2]
        and tiles == 2 * rows_z
        and lax.axis_size("trace") == 4
        and quarter * quarters == traces.shape[1]
    )
    form = gather_per_device if gathers else exchange_per_device
    return form(traces, taps, aperture, counts, time_weights, amplitudes)


def solution(mesh):
    placed = (
        P("trace", "tile", None, None),
        P(),
        P("trace", None, None),
        P("trace", None),
        P("trace", "tile", None, None, None),
        P("trace", "tile", None, None, None, None),
    )
    return jax.shard_map(
        per_device, mesh=mesh, in_specs=placed, out_specs=P("tile", "trace", None), check_vma=False
    )
```

```python
import jax
import jax.numpy as jnp
from jax import lax
from jax.experimental import pallas as pl
from jax.experimental.pallas import tpu as pltpu
from jax.sharding import PartitionSpec as P

group_slots = 8
quarters = 4
rows_z = 4
events = 14
MESH = pl.DeviceIdType.MESH


def migrate_kernel(
    counts_hbm,
    aperture_hbm,
    taps_hbm,
    traces_ref,
    weights_ref,
    spread_ref,
    out_ref,
    gathered,
    weights,
    spread,
    operator,
    total,
    outgoing,
    parts,
    counts_ref,
    aperture_ref,
    taps_ref,
    band,
    lookup,
    slot_of,
    recv_sem,
    send_sem,
    load_sem,
    part_send_sem,
    part_recv_sem,
    far_sem,
    near_sem,
    gift,
    gift_recv_sem,
    staged_weights,
    staged_spread,
    lent_weights,
    lent_spread,
    lend_sem,
    lent_sem,
    kept,
):
    tile = lax.axis_index("tile")
    subset = lax.axis_index("trace")
    z = tile // 2
    x = tile % 2
    other = 1 - x
    low = z < rows_z // 2
    inward = jnp.where(low, 1, -1)
    place = jnp.where(low, z, rows_z - 1 - z)
    end = place == 0
    middle = place == 1
    samples = operator.shape[0]
    taus = weights.shape[1]
    block_rows = spread.shape[2]
    chunk_rows = gathered.shape[2]
    chunk_blocks = chunk_rows // block_rows
    block_count = chunk_blocks * quarters
    share = out_ref.shape[0]

    load_small = [
        pltpu.make_async_copy(src, dst, load_sem.at[4 + at])
        for at, (src, dst) in enumerate(
            ((counts_hbm, counts_ref), (aperture_hbm, aperture_ref), (taps_hbm, taps_ref))
        )
    ]
    load_own = pltpu.make_async_copy(traces_ref, gathered.at[tile], load_sem.at[0])
    load_weights = pltpu.make_async_copy(weights_ref, weights, load_sem.at[1])
    load_spread = pltpu.make_async_copy(spread_ref, spread, load_sem.at[2])

    row_y = subset // 2
    core = subset % 2
    across_y = (1 - row_y) * 2
    giver = end & (core == 0)
    taker = end & (core == 1)
    peers = (across_y + core, across_y + 1 - core, row_y * 2 + 1 - core)

    barrier = pltpu.get_barrier_semaphore()
    neighbours = {
        "x": z * 2 + other,
        "in": tile + 2 * inward,
        "out": tile - 2 * inward,
    }

    def greet(to_tile, to_subset):
        pl.semaphore_signal(barrier, inc=1, device_id=(to_tile, to_subset), device_id_type=MESH)

    greet(neighbours["in"], subset)
    greet(neighbours["x"], subset)

    @pl.when(middle)
    def _():
        greet(neighbours["out"], subset)

    for peer in (peers[0], peers[2]):
        greet(tile, peer)
    load_own.start()
    for load in load_small:
        load.start()
    load_own.wait()
    load_weights.start()
    load_spread.start()
    pl.semaphore_wait(barrier, 4 + jnp.where(middle, 1, 0))

    def send(way, origin, quarter):
        return pltpu.make_async_remote_copy(
            src_ref=gathered.at[origin, quarter],
            dst_ref=gathered.at[origin, quarter],
            send_sem=send_sem.at[("x", "in", "out").index(way), origin, quarter],
            recv_sem=recv_sem.at[origin, quarter],
            device_id=(neighbours[way], subset),
            device_id_type=MESH,
        )

    def wait_arrival(origin, quarter):
        pltpu.make_async_remote_copy(
            src_ref=gathered.at[origin, quarter],
            dst_ref=gathered.at[origin, quarter],
            send_sem=send_sem.at[0, 0, 0],
            recv_sem=recv_sem.at[origin, quarter],
            device_id=(neighbours["x"], subset),
            device_id_type=MESH,
        ).wait_recv()

    for quarter in range(quarters):
        send("in", tile, quarter).start()

        @pl.when(middle)
        def _():
            send("out", tile, quarter).start()

        send("x", tile, (quarter + jnp.where(end, 2, 0)) % quarters).start()

    @pl.when(giver)
    def _():
        for neighbour in ("in", "x"):
            pl.semaphore_signal(
                near_sem,
                inc=1,
                device_id=(neighbours[neighbour], subset),
                device_id_type=MESH,
            )

    pl.semaphore_signal(far_sem, inc=1, device_id=(tile, peers[0]), device_id_type=MESH)
    for load in load_small:
        load.wait()
    slots = weights.shape[0]
    listing = aperture_ref[0, pl.ds(tile, 1), :]
    slot = lax.broadcasted_iota(jnp.int32, (slots, slots), 0)
    block = lax.broadcasted_iota(jnp.int32, (slots, slots), 1)
    named = jnp.broadcast_to(listing, (slots, slots)).T
    match = (named == block) & (slot < counts_ref[0, tile])
    lookup[...] = jnp.broadcast_to(
        jnp.sum(jnp.where(match, slot + 1, 0), axis=0, keepdims=True) - 1, lookup.shape
    )
    publish = pltpu.make_async_copy(lookup, slot_of, load_sem.at[3])
    publish.start()

    half_taps = (taps_ref.shape[1] - 1) // 2
    band[...] = jnp.zeros_like(band)
    band[0:2, 0 : taps_ref.shape[1]] = taps_ref[...].astype(jnp.float32)
    row = lax.broadcasted_iota(jnp.int32, (samples, samples), 0)
    gap = lax.broadcasted_iota(jnp.int32, (samples, samples), 1) - row
    inside = (gap <= half_taps) & (gap >= -half_taps)
    for channel in range(2):
        centred = pltpu.roll(band[...], samples - half_taps, 1)[channel : channel + 1, :]
        shifted = jnp.broadcast_to(centred, (samples, samples))
        shift = 1
        while shift < samples:
            shifted = jnp.where((row // shift) % 2 == 1, pltpu.roll(shifted, shift, 1), shifted)
            shift *= 2
        operator[:, channel * samples : (channel + 1) * samples] = jnp.where(
            inside, shifted, 0.0
        ).astype(operator.dtype)
    total[...] = jnp.zeros_like(total)

    def tile_at(position, column):
        return jnp.where(low, position, rows_z - 1 - position) * 2 + jnp.where(
            column == 0, x, other
        )

    def arrival(event, side):
        if side == 0:
            late = event >= 12
            end_column = jnp.where(late, 1, 0)
            end_position = jnp.where(late, 3, 1 + event // 4)
            end_quarter = jnp.where(late, event - 10, event % 4)
            end_x = event < 10
            end_in = event < 0
        else:
            end_column = 1
            end_position = event // 4
            end_quarter = jnp.where(event < 4, (event + 2) % 4, event % 4)
            end_x = event < 0
            end_in = event < 4
        number = 2 * event + side
        turn = number < 24
        stream = jnp.where(turn, number % 3, 1 + number % 2)
        index = jnp.where(turn, number // 3, number // 2 - 4)
        from_end = stream == 0
        from_middle = stream == 1
        from_x = stream == 2
        relayed = (from_end & (index >= 4)) | (from_middle & (index >= 8))
        column = jnp.where(from_x | relayed, 1, 0)
        position = jnp.where(
            from_end, 0, jnp.where(from_middle, jnp.where(relayed, 3, 2 + index // 4), 1 + index // 4)
        )
        quarter = jnp.where(relayed, (index + 2) % 4, index % 4)
        mid_x = from_middle & (index < 6)
        mid_in = from_end & (index < 6)
        mid_out = from_middle
        origin = tile_at(
            jnp.where(end, end_position, position), jnp.where(end, end_column, column)
        )
        ways = {
            "x": (end & end_x) | (middle & mid_x),
            "in": (end & end_in) | (middle & mid_in),
            "out": middle & mid_out,
        }
        return origin, jnp.where(end, end_quarter, quarter), ways

    def give(way, origin, quarter):
        return pltpu.make_async_remote_copy(
            src_ref=gathered.at[origin, quarter],
            dst_ref=gift.at[("out", "x").index(way)],
            send_sem=send_sem.at[("x", "in", "out").index(way), origin, quarter],
            recv_sem=gift_recv_sem.at[("out", "x").index(way)],
            device_id=(neighbours[way], peers[2]),
            device_id_type=MESH,
        )

    def each_way(event, side, act, before_gift):
        origin, quarter, ways = arrival(event, side)
        gifts = {"in": False, "out": False, "x": False}
        if side == 0:
            gifts["out"] = middle & (core == 0) & (event == 13)
            gifts["x"] = end & (core == 0) & (event == 9)
        for way in ("out", "in", "x"):
            given = gifts[way]

            @pl.when(ways[way] & jnp.logical_not(given))
            def _():
                act(send(way, origin, quarter))

            if given is not False:

                @pl.when(given)
                def _():
                    before_gift()
                    act(give(way, origin, quarter))

    def take(event):
        for side in range(2):
            origin, quarter, _ = arrival(event, side)
            wait_arrival(origin, quarter)
            each_way(
                event,
                side,
                lambda copy: copy.start(),
                lambda: pl.semaphore_wait(near_sem, 1),
            )

    lanes = lax.broadcasted_iota(jnp.int32, (1, 2 * chunk_rows), 1)
    member = (lanes // block_rows) % chunk_blocks

    def migrate(rows, groups):
        filtered = jnp.dot(rows, operator[...], preferred_element_type=jnp.float32).astype(
            jnp.bfloat16
        )
        image = None
        for at, (stacked, columns, gains) in enumerate(groups):
            first = at * chunk_rows
            blocks = jnp.concatenate(
                [
                    filtered[first : first + chunk_rows, 0:samples],
                    filtered[first : first + chunk_rows, samples : 2 * samples],
                ],
                axis=0,
            )
            product = lax.dot_general(
                stacked, blocks, (((1,), (1,)), ((), ())), preferred_element_type=jnp.float32
            )
            interp = product[0:taus]
            for index in range(1, chunk_blocks):
                interp = jnp.where(
                    member == index, product[index * taus : (index + 1) * taus], interp
                )
            if gains is not None:
                alive = jnp.full((1, 2 * chunk_rows), gains[0], jnp.float32)
                for index in range(1, chunk_blocks):
                    alive = jnp.where(member == index, gains[index], alive)
                interp = interp * alive
            interp = interp.astype(jnp.bfloat16)
            part = jnp.dot(interp, columns, preferred_element_type=jnp.float32)
            image = part if image is None else image + part
        total[...] += image

    def look_up(origin, quarter):
        base = origin * block_count + quarter * chunk_blocks
        found = [slot_of[0, base + index] for index in range(chunk_blocks)]
        picks = [jnp.maximum(value, 0) for value in found]
        gains = [jnp.where(value >= 0, 1.0, 0.0) for value in found]
        return picks, gains

    def compute(chunks):
        rows = jnp.concatenate([gathered[origin, quarter] for origin, quarter in chunks], axis=0)
        groups = []
        for origin, quarter in chunks:
            picks, gains = look_up(origin, quarter)
            stacked = jnp.concatenate([weights[pick] for pick in picks], axis=0)
            columns = jnp.concatenate(
                [spread[pick, channel] for channel in range(2) for pick in picks], axis=0
            )
            groups.append((stacked, columns, gains))
        migrate(rows, groups)

    lending = [
        pltpu.make_async_remote_copy(
            src_ref=src,
            dst_ref=dst,
            send_sem=lend_sem.at[at],
            recv_sem=lent_sem.at[at],
            device_id=(tile, peers[2]),
            device_id_type=MESH,
        )
        for at, (src, dst) in enumerate(
            ((staged_weights, lent_weights), (staged_spread, lent_spread))
        )
    ]

    def lend():
        for at, quarter in enumerate((3, 1)):
            picks, gains = look_up(tile_at(3, 1), quarter)
            for index, (pick, gain) in enumerate(zip(picks, gains, strict=True)):
                staged_weights[at * chunk_blocks + index] = weights[pick]
                staged_spread[at * chunk_blocks + index] = (
                    spread[pick].astype(jnp.float32) * gain
                ).astype(staged_spread.dtype)
        for copy in lending:
            copy.start()

    half_taus = 2 * share

    def keep_filtered(rows):
        filtered = jnp.dot(rows, operator[...], preferred_element_type=jnp.float32).astype(
            jnp.bfloat16
        )
        for at in range(2):
            first = at * chunk_rows
            for channel in range(2):
                kept[at, channel * chunk_rows : (channel + 1) * chunk_rows, :] = filtered[
                    first : first + chunk_rows, channel * samples : (channel + 1) * samples
                ]

    def add_half(at_rows, groups):
        image = None
        for at, (stacked, columns, gains) in enumerate(groups):
            product = lax.dot_general(
                stacked, kept[at], (((1,), (1,)), ((), ())), preferred_element_type=jnp.float32
            )
            interp = product[0:half_taus]
            alive = jnp.full((1, 2 * chunk_rows), gains[0], jnp.float32)
            for index in range(1, chunk_blocks):
                here = member == index
                interp = jnp.where(
                    here, product[index * half_taus : (index + 1) * half_taus], interp
                )
                alive = jnp.where(here, gains[index], alive)
            part = jnp.dot(
                (interp * alive).astype(jnp.bfloat16), columns, preferred_element_type=jnp.float32
            )
            image = part if image is None else image + part
        total[pl.ds(at_rows, half_taus), :] += image

    last_own = [arrival(12, side)[0:2] for side in range(2)]

    def giver_half(at_rows):
        groups = []
        for origin, quarter in last_own:
            picks, gains = look_up(origin, quarter)
            stacked = jnp.concatenate(
                [weights[pick, pl.ds(at_rows, half_taus), :] for pick in picks], axis=0
            )
            columns = jnp.concatenate(
                [spread[pick, channel] for channel in range(2) for pick in picks], axis=0
            )
            groups.append((stacked, columns, gains))
        add_half(at_rows, groups)

    def taker_half(at_rows):
        groups = []
        for at in range(2):
            mine = range(at * chunk_blocks, (at + 1) * chunk_blocks)
            stacked = jnp.concatenate(
                [lent_weights[index, pl.ds(at_rows, half_taus), :] for index in mine], axis=0
            )
            columns = jnp.concatenate(
                [lent_spread[index, channel] for channel in range(2) for index in mine], axis=0
            )
            groups.append((stacked, columns, [1.0] * chunk_blocks))
        add_half(at_rows, groups)

    far_rows = pl.multiple_of(across_y * share, half_taus)
    near_rows = pl.multiple_of(row_y * 2 * share, half_taus)

    def giver_first():
        take(12)
        keep_filtered(
            jnp.concatenate([gathered[origin, quarter] for origin, quarter in last_own], axis=0)
        )
        giver_half(far_rows)

    def taker_first():
        for copy in lending:
            copy.wait_recv()
        for way in ("out", "x"):
            give(way, 0, 0).wait_recv()
        keep_filtered(jnp.concatenate([gift[0], gift[1]], axis=0))
        taker_half(far_rows)

    take(0)

    @pl.when(middle)
    def _():
        take(1)

    load_weights.wait()
    load_spread.wait()
    publish.wait()

    def step(number, carry):
        pl.when(giver & (number == 8))(lend)
        caught_up = number >= 6
        end_takes = (number == 1) | (number == 3) | (number == 5) | caught_up
        middle_takes = number + 2 < events
        end_event = jnp.where(caught_up, number - 2, (number + 1) // 2)

        @pl.when((end & end_takes) | (middle & middle_takes))
        def _():
            take(jnp.where(end, end_event, number + 2))

        chunks = []
        for side in range(2):
            origin, quarter, _ = arrival(jnp.maximum(number - 2, 0), side)
            own = number < 2
            chunks.append(
                (jnp.where(own, tile, origin), jnp.where(own, 2 * number + side, quarter))
            )
        compute(chunks)
        return carry

    lax.fori_loop(0, events + 2 - jnp.where(giver, 2, 0), step, 0)
    pl.when(giver)(giver_first)
    pl.when(taker)(taker_first)
    pl.semaphore_wait(far_sem, 1)

    def exchange(at, peer):
        return pltpu.make_async_remote_copy(
            src_ref=outgoing.at[at],
            dst_ref=parts.at[at],
            send_sem=part_send_sem.at[at],
            recv_sem=part_recv_sem.at[at],
            device_id=(tile, peer),
            device_id_type=MESH,
        )

    def ship(at, peer):
        outgoing[at] = total[pl.ds(pl.multiple_of(peer * share, share), share), :].astype(
            outgoing.dtype
        )
        exchange(at, peer).start()

    ship(core, across_y)
    ship(1 - core, across_y + 1)
    pl.when(giver)(lambda: giver_half(near_rows))
    pl.when(taker)(lambda: taker_half(near_rows))
    ship(2, peers[2])
    exchanges = [exchange(at, peer) for at, peer in enumerate(peers)]

    for quarter in range(quarters):
        send("in", tile, quarter).wait_send()

        @pl.when(middle)
        def _():
            send("out", tile, quarter).wait_send()

        send("x", tile, quarter).wait_send()

    def sent(event, carry):
        for side in range(2):
            each_way(event, side, lambda copy: copy.wait_send(), lambda: None)
        return carry

    lax.fori_loop(0, events, sent, 0)

    result = total[pl.ds(pl.multiple_of(subset * share, share), share), :]
    for at, copy in enumerate(exchanges):
        copy.wait_recv()
        result = result + parts[at].astype(jnp.float32)
    out_ref[...] = result
    for copy in exchanges:
        copy.wait_send()

    @pl.when(giver)
    def _():
        for copy in lending:
            copy.wait_send()


def keep(array):
    return pltpu.with_memory_space_constraint(array, pltpu.HBM)


def gather_per_device(traces, taps, aperture, counts, time_weights, amplitudes):
    tiles = lax.axis_size("tile")
    subsets = lax.axis_size("trace")
    _, block_count, block_rows, samples = traces.shape
    slots, taus = time_weights.shape[2:4]
    columns = amplitudes.shape[-1]
    chunk_rows = block_count * block_rows // quarters
    share = taus // subsets
    lent_blocks = 2 * block_count // quarters
    vmem = pl.BlockSpec(memory_space=pltpu.VMEM)
    hbm = pl.BlockSpec(memory_space=pl.ANY)
    image = pl.pallas_call(
        migrate_kernel,
        out_shape=jax.ShapeDtypeStruct((share, columns), jnp.float32),
        in_specs=[hbm] * 6,
        out_specs=vmem,
        scratch_shapes=[
            pltpu.VMEM((tiles, quarters, chunk_rows, samples), jnp.bfloat16),
            pltpu.VMEM((slots, taus, samples), jnp.bfloat16),
            pltpu.VMEM((slots, 2, block_rows, columns), jnp.bfloat16),
            pltpu.VMEM((samples, 2 * samples), jnp.bfloat16),
            pltpu.VMEM((taus, columns), jnp.float32),
            pltpu.VMEM((subsets - 1, share, columns), jnp.bfloat16),
            pltpu.VMEM((subsets - 1, share, columns), jnp.bfloat16),
            pltpu.SMEM(counts.shape, jnp.int32),
            pltpu.VMEM(aperture.shape, jnp.int32),
            pltpu.VMEM(taps.shape, taps.dtype),
            pltpu.VMEM((8, samples), jnp.float32),
            pltpu.VMEM((8, slots), jnp.int32),
            pltpu.SMEM((8, slots), jnp.int32),
            pltpu.SemaphoreType.DMA((tiles, quarters)),
            pltpu.SemaphoreType.DMA((3, tiles, quarters)),
            pltpu.SemaphoreType.DMA((7,)),
            pltpu.SemaphoreType.DMA((subsets - 1,)),
            pltpu.SemaphoreType.DMA((subsets - 1,)),
            pltpu.SemaphoreType.REGULAR,
            pltpu.SemaphoreType.REGULAR,
            pltpu.VMEM((2, chunk_rows, samples), jnp.bfloat16),
            pltpu.SemaphoreType.DMA((2,)),
            pltpu.VMEM((lent_blocks, taus, samples), jnp.bfloat16),
            pltpu.VMEM((lent_blocks, 2, block_rows, columns), jnp.bfloat16),
            pltpu.VMEM((lent_blocks, taus, samples), jnp.bfloat16),
            pltpu.VMEM((lent_blocks, 2, block_rows, columns), jnp.bfloat16),
            pltpu.SemaphoreType.DMA((2,)),
            pltpu.SemaphoreType.DMA((2,)),
            pltpu.VMEM((2, 2 * chunk_rows, samples), jnp.bfloat16),
        ],
        compiler_params=pltpu.CompilerParams(
            collective_id=0, has_side_effects=True, vmem_limit_bytes=48 * 1024 * 1024
        ),
    )(
        keep(counts),
        keep(aperture),
        keep(taps),
        keep(traces.reshape(quarters, chunk_rows, samples)),
        keep(time_weights[0, 0]),
        keep(amplitudes[0, 0]),
    )
    return image[None]


def filter_matrix(taps, samples):
    width = taps.shape[1]
    center = (width - 1) // 2
    offset = jnp.arange(samples)[:, None] - jnp.arange(samples)[None, :] + center
    table = (offset[:, :, None] == jnp.arange(width)[None, None, :]).astype(jnp.bfloat16)
    return jnp.einsum("ct,nmt->cnm", taps, table, preferred_element_type=jnp.float32).astype(
        jnp.bfloat16
    )


def exchange_per_device(traces, taps, aperture, counts, time_weights, amplitudes):
    tiles = lax.axis_size("tile")
    myself = lax.axis_index("tile")
    block_count = traces.shape[1]
    samples = traces.shape[3]
    slots = aperture.shape[2]
    capacity = max(2, slots // tiles)
    listing = aperture[0]
    filled = counts[0]
    owners = listing // block_count
    within = listing - owners * block_count
    order = jnp.arange(slots)
    earlier = order[None, :] < order[:, None]
    rank = jnp.sum((owners[:, :, None] == owners[:, None, :]) & earlier[None], axis=2)
    alive_slots = order[None, :] < filled[:, None]
    mine = (owners == myself) & alive_slots
    rank_onehot = (
        (rank[:, :, None] == jnp.arange(capacity)[None, None, :]) & mine[:, :, None]
    ).astype(jnp.bfloat16)
    local_onehot = (within[:, :, None] == jnp.arange(block_count)[None, None, :]).astype(
        jnp.bfloat16
    )
    select = jnp.einsum(
        "ksc,ksl->kcl", rank_onehot, local_onehot, preferred_element_type=jnp.float32
    ).astype(jnp.bfloat16)
    operator = filter_matrix(taps, samples)
    own_owner = lax.dynamic_index_in_dim(owners, myself, 0, keepdims=False)
    own_rank = lax.dynamic_index_in_dim(rank, myself, 0, keepdims=False)
    own_fill = lax.dynamic_index_in_dim(filled, myself, 0, keepdims=False)
    source_slot = own_owner * capacity + own_rank
    arrived_rows = tiles * capacity

    def pick_rows(positions):
        return (positions[:, None] == jnp.arange(arrived_rows)[None, :]).astype(jnp.bfloat16)

    filtered = jnp.einsum(
        "cnm,kbm->kcbn", operator, traces[0], preferred_element_type=jnp.float32
    ).astype(jnp.bfloat16)
    outgoing = jnp.einsum(
        "kcl,lqbn->kcqbn", select, filtered, preferred_element_type=jnp.float32
    ).astype(jnp.bfloat16)
    arrived = lax.all_to_all(outgoing, "tile", split_axis=0, concat_axis=0, tiled=True)
    arrived = arrived.reshape((arrived_rows,) + arrived.shape[2:])

    def fetch(positions):
        return jnp.einsum(
            "gq,qcbn->gcbn", pick_rows(positions), arrived, preferred_element_type=jnp.float32
        ).astype(jnp.bfloat16)

    weights = time_weights[0, 0]
    spread = amplitudes[0, 0]

    def add_group(index, total):
        start = index * group_slots
        positions = lax.dynamic_slice_in_dim(source_slot, start, group_slots, 0)
        blocks = fetch(positions)
        part_weights = lax.dynamic_slice_in_dim(weights, start, group_slots, 0)
        part_spread = lax.dynamic_slice_in_dim(spread, start, group_slots, 0)
        alive = (start + jnp.arange(group_slots) < own_fill).astype(jnp.float32)
        interp = jnp.einsum(
            "gtn,gcbn->gcbt", part_weights, blocks, preferred_element_type=jnp.float32
        )
        interp = (interp * alive[:, None, None, None]).astype(jnp.bfloat16)
        return total + jnp.einsum(
            "gcbt,gcbp->tp", interp, part_spread, preferred_element_type=jnp.float32
        )

    rounds = (own_fill + group_slots - 1) // group_slots
    partial_value = lax.fori_loop(
        0, rounds, add_group, jnp.zeros((weights.shape[1], spread.shape[-1]), jnp.float32)
    )
    image = lax.psum_scatter(partial_value, "trace", scatter_dimension=0, tiled=True)
    return image[None]


def per_device(traces, taps, aperture, counts, time_weights, amplitudes):
    tiles = lax.axis_size("tile")
    every_block = traces.shape[1] * tiles
    quarter = traces.shape[1] // quarters
    gathers = (
        every_block == aperture.shape[2]
        and tiles == 2 * rows_z
        and lax.axis_size("trace") == 4
        and quarter * quarters == traces.shape[1]
    )
    form = gather_per_device if gathers else exchange_per_device
    return form(traces, taps, aperture, counts, time_weights, amplitudes)


def solution(mesh):
    placed = (
        P("trace", "tile", None, None),
        P(),
        P("trace", None, None),
        P("trace", None),
        P("trace", "tile", None, None, None),
        P("trace", "tile", None, None, None, None),
    )
    return jax.shard_map(
        per_device, mesh=mesh, in_specs=placed, out_specs=P("tile", "trace", None), check_vma=False
    )
```

```python
import jax
import jax.numpy as jnp
from jax import lax
from jax.experimental import pallas as pl
from jax.experimental.pallas import tpu as pltpu
from jax.sharding import PartitionSpec as P

group_slots = 8
quarters = 4
rows_z = 4
events = 14
MESH = pl.DeviceIdType.MESH


def migrate_kernel(
    counts_hbm,
    aperture_hbm,
    taps_hbm,
    traces_ref,
    weights_ref,
    spread_ref,
    out_ref,
    gathered,
    weights,
    spread,
    operator,
    total,
    outgoing,
    parts,
    counts_ref,
    aperture_ref,
    taps_ref,
    band,
    lookup,
    slot_of,
    recv_sem,
    send_sem,
    load_sem,
    part_send_sem,
    part_recv_sem,
    far_sem,
    near_sem,
    gift,
    gift_recv_sem,
    staged_weights,
    staged_spread,
    lent_weights,
    lent_spread,
    lend_sem,
    lent_sem,
    kept,
):
    tile = lax.axis_index("tile")
    subset = lax.axis_index("trace")
    z = tile // 2
    x = tile % 2
    other = 1 - x
    low = z < rows_z // 2
    inward = jnp.where(low, 1, -1)
    place = jnp.where(low, z, rows_z - 1 - z)
    end = place == 0
    middle = place == 1
    samples = operator.shape[0]
    taus = weights.shape[1]
    block_rows = spread.shape[2]
    chunk_rows = gathered.shape[2]
    chunk_blocks = chunk_rows // block_rows
    block_count = chunk_blocks * quarters
    share = out_ref.shape[0]

    load_small = [
        pltpu.make_async_copy(src, dst, load_sem.at[4 + at])
        for at, (src, dst) in enumerate(
            ((counts_hbm, counts_ref), (aperture_hbm, aperture_ref), (taps_hbm, taps_ref))
        )
    ]
    load_own = pltpu.make_async_copy(traces_ref, gathered.at[tile], load_sem.at[0])
    load_weights = pltpu.make_async_copy(weights_ref, weights, load_sem.at[1])
    load_spread = pltpu.make_async_copy(spread_ref, spread, load_sem.at[2])

    row_y = subset // 2
    core = subset % 2
    across_y = (1 - row_y) * 2
    giver = end & (core == 0)
    taker = end & (core == 1)
    peers = (across_y + core, across_y + 1 - core, row_y * 2 + 1 - core)

    barrier = pltpu.get_barrier_semaphore()
    neighbours = {
        "x": z * 2 + other,
        "in": tile + 2 * inward,
        "out": tile - 2 * inward,
    }

    def greet(to_tile, to_subset):
        pl.semaphore_signal(barrier, inc=1, device_id=(to_tile, to_subset), device_id_type=MESH)

    greet(neighbours["in"], subset)
    greet(neighbours["x"], subset)

    @pl.when(middle)
    def _():
        greet(neighbours["out"], subset)

    for peer in (peers[0], peers[2]):
        greet(tile, peer)
    load_own.start()
    for load in load_small:
        load.start()
    load_own.wait()
    load_weights.start()
    load_spread.start()
    pl.semaphore_wait(barrier, 4 + jnp.where(middle, 1, 0))

    def send(way, origin, quarter):
        return pltpu.make_async_remote_copy(
            src_ref=gathered.at[origin, quarter],
            dst_ref=gathered.at[origin, quarter],
            send_sem=send_sem.at[("x", "in", "out").index(way), origin, quarter],
            recv_sem=recv_sem.at[origin, quarter],
            device_id=(neighbours[way], subset),
            device_id_type=MESH,
        )

    def wait_arrival(origin, quarter):
        pltpu.make_async_remote_copy(
            src_ref=gathered.at[origin, quarter],
            dst_ref=gathered.at[origin, quarter],
            send_sem=send_sem.at[0, 0, 0],
            recv_sem=recv_sem.at[origin, quarter],
            device_id=(neighbours["x"], subset),
            device_id_type=MESH,
        ).wait_recv()

    for quarter in range(quarters):
        send("in", tile, quarter).start()

        @pl.when(middle)
        def _():
            send("out", tile, quarter).start()

        send("x", tile, (quarter + jnp.where(end, 2, 0)) % quarters).start()

    @pl.when(giver)
    def _():
        for neighbour in ("in", "x"):
            pl.semaphore_signal(
                near_sem,
                inc=1,
                device_id=(neighbours[neighbour], subset),
                device_id_type=MESH,
            )

    pl.semaphore_signal(far_sem, inc=1, device_id=(tile, peers[0]), device_id_type=MESH)
    for load in load_small:
        load.wait()
    slots = weights.shape[0]
    listing = aperture_ref[0, pl.ds(tile, 1), :]
    slot = lax.broadcasted_iota(jnp.int32, (slots, slots), 0)
    block = lax.broadcasted_iota(jnp.int32, (slots, slots), 1)
    named = jnp.broadcast_to(listing, (slots, slots)).T
    match = (named == block) & (slot < counts_ref[0, tile])
    lookup[...] = jnp.broadcast_to(
        jnp.sum(jnp.where(match, slot + 1, 0), axis=0, keepdims=True) - 1, lookup.shape
    )
    publish = pltpu.make_async_copy(lookup, slot_of, load_sem.at[3])
    publish.start()

    half_taps = (taps_ref.shape[1] - 1) // 2
    band[...] = jnp.zeros_like(band)
    band[0:2, 0 : taps_ref.shape[1]] = taps_ref[...].astype(jnp.float32)
    row = lax.broadcasted_iota(jnp.int32, (samples, samples), 0)
    gap = lax.broadcasted_iota(jnp.int32, (samples, samples), 1) - row
    inside = (gap <= half_taps) & (gap >= -half_taps)
    for channel in range(2):
        centred = pltpu.roll(band[...], samples - half_taps, 1)[channel : channel + 1, :]
        shifted = jnp.broadcast_to(centred, (samples, samples))
        shift = 1
        while shift < samples:
            shifted = jnp.where((row // shift) % 2 == 1, pltpu.roll(shifted, shift, 1), shifted)
            shift *= 2
        operator[:, channel * samples : (channel + 1) * samples] = jnp.where(
            inside, shifted, 0.0
        ).astype(operator.dtype)
    total[...] = jnp.zeros_like(total)

    def tile_at(position, column):
        return jnp.where(low, position, rows_z - 1 - position) * 2 + jnp.where(
            column == 0, x, other
        )

    def arrival(event, side):
        if side == 0:
            late = event >= 12
            end_column = jnp.where(late, 1, 0)
            end_position = jnp.where(late, 3, 1 + event // 4)
            end_quarter = jnp.where(late, event - 10, event % 4)
            end_x = event < 10
            end_in = event < 0
        else:
            end_column = 1
            end_position = event // 4
            end_quarter = jnp.where(event < 4, (event + 2) % 4, event % 4)
            end_x = event < 0
            end_in = event < 4
        number = 2 * event + side
        turn = number < 24
        stream = jnp.where(turn, number % 3, 1 + number % 2)
        index = jnp.where(turn, number // 3, number // 2 - 4)
        from_end = stream == 0
        from_middle = stream == 1
        from_x = stream == 2
        relayed = (from_end & (index >= 4)) | (from_middle & (index >= 8))
        column = jnp.where(from_x | relayed, 1, 0)
        position = jnp.where(
            from_end, 0, jnp.where(from_middle, jnp.where(relayed, 3, 2 + index // 4), 1 + index // 4)
        )
        quarter = jnp.where(relayed, (index + 2) % 4, index % 4)
        mid_x = from_middle & (index < 6)
        mid_in = from_end & (index < 6)
        mid_out = from_middle
        origin = tile_at(
            jnp.where(end, end_position, position), jnp.where(end, end_column, column)
        )
        ways = {
            "x": (end & end_x) | (middle & mid_x),
            "in": (end & end_in) | (middle & mid_in),
            "out": middle & mid_out,
        }
        return origin, jnp.where(end, end_quarter, quarter), ways

    def give(way, origin, quarter, pair):
        return pltpu.make_async_remote_copy(
            src_ref=gathered.at[origin, quarter],
            dst_ref=gift.at[pair, ("out", "x").index(way)],
            send_sem=send_sem.at[("x", "in", "out").index(way), origin, quarter],
            recv_sem=gift_recv_sem.at[pair, ("out", "x").index(way)],
            device_id=(neighbours[way], peers[2]),
            device_id_type=MESH,
        )

    def each_way(event, side, act, before_gift):
        origin, quarter, ways = arrival(event, side)
        gifts = {"in": False, "out": False, "x": False}
        if side == 0:
            gifts["out"] = middle & (core == 0) & (event >= 12)
            gifts["x"] = end & (core == 0) & ((event == 8) | (event == 9))
        for way in ("out", "in", "x"):
            given = gifts[way]

            @pl.when(ways[way] & jnp.logical_not(given))
            def _():
                act(send(way, origin, quarter))

            if given is not False:

                @pl.when(given)
                def _():
                    first = 12 if way == "out" else 8
                    pl.when(jnp.int32(event) == first)(before_gift)
                    act(give(way, origin, quarter, event - first))

    def take(event):
        for side in range(2):
            origin, quarter, _ = arrival(event, side)
            wait_arrival(origin, quarter)
            each_way(
                event,
                side,
                lambda copy: copy.start(),
                lambda: pl.semaphore_wait(near_sem, 1),
            )

    lanes = lax.broadcasted_iota(jnp.int32, (1, 2 * chunk_rows), 1)
    member = (lanes // block_rows) % chunk_blocks

    def migrate(rows, groups):
        filtered = jnp.dot(rows, operator[...], preferred_element_type=jnp.float32).astype(
            jnp.bfloat16
        )
        image = None
        for at, (stacked, columns, gains) in enumerate(groups):
            first = at * chunk_rows
            blocks = jnp.concatenate(
                [
                    filtered[first : first + chunk_rows, 0:samples],
                    filtered[first : first + chunk_rows, samples : 2 * samples],
                ],
                axis=0,
            )
            product = lax.dot_general(
                stacked, blocks, (((1,), (1,)), ((), ())), preferred_element_type=jnp.float32
            )
            interp = product[0:taus]
            for index in range(1, chunk_blocks):
                interp = jnp.where(
                    member == index, product[index * taus : (index + 1) * taus], interp
                )
            if gains is not None:
                alive = jnp.full((1, 2 * chunk_rows), gains[0], jnp.float32)
                for index in range(1, chunk_blocks):
                    alive = jnp.where(member == index, gains[index], alive)
                interp = interp * alive
            interp = interp.astype(jnp.bfloat16)
            part = jnp.dot(interp, columns, preferred_element_type=jnp.float32)
            image = part if image is None else image + part
        total[...] += image

    def look_up(origin, quarter):
        base = origin * block_count + quarter * chunk_blocks
        found = [slot_of[0, base + index] for index in range(chunk_blocks)]
        picks = [jnp.maximum(value, 0) for value in found]
        gains = [jnp.where(value >= 0, 1.0, 0.0) for value in found]
        return picks, gains

    def compute(chunks):
        rows = jnp.concatenate([gathered[origin, quarter] for origin, quarter in chunks], axis=0)
        groups = []
        for origin, quarter in chunks:
            picks, gains = look_up(origin, quarter)
            stacked = jnp.concatenate([weights[pick] for pick in picks], axis=0)
            columns = jnp.concatenate(
                [spread[pick, channel] for channel in range(2) for pick in picks], axis=0
            )
            groups.append((stacked, columns, gains))
        migrate(rows, groups)

    lending = [
        pltpu.make_async_remote_copy(
            src_ref=src,
            dst_ref=dst,
            send_sem=lend_sem.at[at],
            recv_sem=lent_sem.at[at],
            device_id=(tile, peers[2]),
            device_id_type=MESH,
        )
        for at, (src, dst) in enumerate(
            ((staged_weights, lent_weights), (staged_spread, lent_spread))
        )
    ]

    def lend():
        for at, quarter in enumerate((2, 0, 3, 1)):
            picks, gains = look_up(tile_at(3, 1), quarter)
            for index, (pick, gain) in enumerate(zip(picks, gains, strict=True)):
                staged_weights[at * chunk_blocks + index] = weights[pick]
                staged_spread[at * chunk_blocks + index] = (
                    spread[pick].astype(jnp.float32) * gain
                ).astype(staged_spread.dtype)
        for copy in lending:
            copy.start()

    half_taus = 2 * share

    def keep_filtered(rows):
        filtered = jnp.dot(rows, operator[...], preferred_element_type=jnp.float32).astype(
            jnp.bfloat16
        )
        for at in range(2):
            first = at * chunk_rows
            for channel in range(2):
                kept[at, channel * chunk_rows : (channel + 1) * chunk_rows, :] = filtered[
                    first : first + chunk_rows, channel * samples : (channel + 1) * samples
                ]

    def add_half(at_rows, groups):
        image = None
        for at, (stacked, columns, gains) in enumerate(groups):
            product = lax.dot_general(
                stacked, kept[at], (((1,), (1,)), ((), ())), preferred_element_type=jnp.float32
            )
            interp = product[0:half_taus]
            alive = jnp.full((1, 2 * chunk_rows), gains[0], jnp.float32)
            for index in range(1, chunk_blocks):
                here = member == index
                interp = jnp.where(
                    here, product[index * half_taus : (index + 1) * half_taus], interp
                )
                alive = jnp.where(here, gains[index], alive)
            part = jnp.dot(
                (interp * alive).astype(jnp.bfloat16), columns, preferred_element_type=jnp.float32
            )
            image = part if image is None else image + part
        total[pl.ds(at_rows, half_taus), :] += image

    last_own = [arrival(11, side)[0:2] for side in range(2)]

    def giver_half(at_rows):
        groups = []
        for origin, quarter in last_own:
            picks, gains = look_up(origin, quarter)
            stacked = jnp.concatenate(
                [weights[pick, pl.ds(at_rows, half_taus), :] for pick in picks], axis=0
            )
            columns = jnp.concatenate(
                [spread[pick, channel] for channel in range(2) for pick in picks], axis=0
            )
            groups.append((stacked, columns, gains))
        add_half(at_rows, groups)

    def taker_half(at_rows):
        groups = []
        for at in range(2):
            mine = range((2 + at) * chunk_blocks, (3 + at) * chunk_blocks)
            stacked = jnp.concatenate(
                [lent_weights[index, pl.ds(at_rows, half_taus), :] for index in mine], axis=0
            )
            columns = jnp.concatenate(
                [lent_spread[index, channel] for channel in range(2) for index in mine], axis=0
            )
            groups.append((stacked, columns, [1.0] * chunk_blocks))
        add_half(at_rows, groups)

    far_rows = pl.multiple_of(across_y * share, half_taus)
    near_rows = pl.multiple_of(row_y * 2 * share, half_taus)

    def giver_first():
        take(11)
        keep_filtered(
            jnp.concatenate([gathered[origin, quarter] for origin, quarter in last_own], axis=0)
        )
        giver_half(far_rows)

    def first_gift():
        for copy in lending:
            copy.wait_recv()
        for way in ("out", "x"):
            give(way, 0, 0, 0).wait_recv()
        groups = []
        for at in range(2):
            mine = range(at * chunk_blocks, (at + 1) * chunk_blocks)
            stacked = jnp.concatenate([lent_weights[index] for index in mine], axis=0)
            columns = jnp.concatenate(
                [lent_spread[index, channel] for channel in range(2) for index in mine], axis=0
            )
            groups.append((stacked, columns, None))
        migrate(jnp.concatenate([gift[0, 0], gift[0, 1]], axis=0), groups)

    def taker_first():
        for way in ("out", "x"):
            give(way, 0, 0, 1).wait_recv()
        keep_filtered(jnp.concatenate([gift[1, 0], gift[1, 1]], axis=0))
        taker_half(far_rows)

    take(0)

    @pl.when(middle)
    def _():
        take(1)

    load_weights.wait()
    load_spread.wait()
    publish.wait()

    def step(number, carry):
        pl.when(giver & (number == 8))(lend)
        caught_up = number >= 6
        end_takes = (number == 1) | (number == 3) | (number == 5) | caught_up
        middle_takes = number + 2 < events
        end_event = jnp.where(caught_up, number - 2, (number + 1) // 2)

        @pl.when((end & end_takes) | (middle & middle_takes))
        def _():
            take(jnp.where(end, end_event, number + 2))

        chunks = []
        for side in range(2):
            origin, quarter, _ = arrival(jnp.maximum(number - 2, 0), side)
            own = number < 2
            chunks.append(
                (jnp.where(own, tile, origin), jnp.where(own, 2 * number + side, quarter))
            )
        compute(chunks)
        return carry

    lax.fori_loop(0, events + 2 - jnp.where(giver, 3, 0), step, 0)
    pl.when(taker)(first_gift)
    pl.when(giver)(giver_first)
    pl.when(taker)(taker_first)
    pl.semaphore_wait(far_sem, 1)

    def exchange(at, peer):
        return pltpu.make_async_remote_copy(
            src_ref=outgoing.at[at],
            dst_ref=parts.at[at],
            send_sem=part_send_sem.at[at],
            recv_sem=part_recv_sem.at[at],
            device_id=(tile, peer),
            device_id_type=MESH,
        )

    def ship(at, peer):
        outgoing[at] = total[pl.ds(pl.multiple_of(peer * share, share), share), :].astype(
            outgoing.dtype
        )
        exchange(at, peer).start()

    ship(core, across_y)
    ship(1 - core, across_y + 1)
    pl.when(giver)(lambda: giver_half(near_rows))
    pl.when(taker)(lambda: taker_half(near_rows))
    ship(2, peers[2])
    exchanges = [exchange(at, peer) for at, peer in enumerate(peers)]

    for quarter in range(quarters):
        send("in", tile, quarter).wait_send()

        @pl.when(middle)
        def _():
            send("out", tile, quarter).wait_send()

        send("x", tile, quarter).wait_send()

    def sent(event, carry):
        for side in range(2):
            each_way(event, side, lambda copy: copy.wait_send(), lambda: None)
        return carry

    lax.fori_loop(0, events, sent, 0)

    result = total[pl.ds(pl.multiple_of(subset * share, share), share), :]
    for at, copy in enumerate(exchanges):
        copy.wait_recv()
        result = result + parts[at].astype(jnp.float32)
    out_ref[...] = result
    for copy in exchanges:
        copy.wait_send()

    @pl.when(giver)
    def _():
        for copy in lending:
            copy.wait_send()


def keep(array):
    return pltpu.with_memory_space_constraint(array, pltpu.HBM)


def gather_per_device(traces, taps, aperture, counts, time_weights, amplitudes):
    tiles = lax.axis_size("tile")
    subsets = lax.axis_size("trace")
    _, block_count, block_rows, samples = traces.shape
    slots, taus = time_weights.shape[2:4]
    columns = amplitudes.shape[-1]
    chunk_rows = block_count * block_rows // quarters
    share = taus // subsets
    lent_blocks = 4 * block_count // quarters
    vmem = pl.BlockSpec(memory_space=pltpu.VMEM)
    hbm = pl.BlockSpec(memory_space=pl.ANY)
    image = pl.pallas_call(
        migrate_kernel,
        out_shape=jax.ShapeDtypeStruct((share, columns), jnp.float32),
        in_specs=[hbm] * 6,
        out_specs=vmem,
        scratch_shapes=[
            pltpu.VMEM((tiles, quarters, chunk_rows, samples), jnp.bfloat16),
            pltpu.VMEM((slots, taus, samples), jnp.bfloat16),
            pltpu.VMEM((slots, 2, block_rows, columns), jnp.bfloat16),
            pltpu.VMEM((samples, 2 * samples), jnp.bfloat16),
            pltpu.VMEM((taus, columns), jnp.float32),
            pltpu.VMEM((subsets - 1, share, columns), jnp.bfloat16),
            pltpu.VMEM((subsets - 1, share, columns), jnp.bfloat16),
            pltpu.SMEM(counts.shape, jnp.int32),
            pltpu.VMEM(aperture.shape, jnp.int32),
            pltpu.VMEM(taps.shape, taps.dtype),
            pltpu.VMEM((8, samples), jnp.float32),
            pltpu.VMEM((8, slots), jnp.int32),
            pltpu.SMEM((8, slots), jnp.int32),
            pltpu.SemaphoreType.DMA((tiles, quarters)),
            pltpu.SemaphoreType.DMA((3, tiles, quarters)),
            pltpu.SemaphoreType.DMA((7,)),
            pltpu.SemaphoreType.DMA((subsets - 1,)),
            pltpu.SemaphoreType.DMA((subsets - 1,)),
            pltpu.SemaphoreType.REGULAR,
            pltpu.SemaphoreType.REGULAR,
            pltpu.VMEM((2, 2, chunk_rows, samples), jnp.bfloat16),
            pltpu.SemaphoreType.DMA((2, 2)),
            pltpu.VMEM((lent_blocks, taus, samples), jnp.bfloat16),
            pltpu.VMEM((lent_blocks, 2, block_rows, columns), jnp.bfloat16),
            pltpu.VMEM((lent_blocks, taus, samples), jnp.bfloat16),
            pltpu.VMEM((lent_blocks, 2, block_rows, columns), jnp.bfloat16),
            pltpu.SemaphoreType.DMA((2,)),
            pltpu.SemaphoreType.DMA((2,)),
            pltpu.VMEM((2, 2 * chunk_rows, samples), jnp.bfloat16),
        ],
        compiler_params=pltpu.CompilerParams(
            collective_id=0, has_side_effects=True, vmem_limit_bytes=48 * 1024 * 1024
        ),
    )(
        keep(counts),
        keep(aperture),
        keep(taps),
        keep(traces.reshape(quarters, chunk_rows, samples)),
        keep(time_weights[0, 0]),
        keep(amplitudes[0, 0]),
    )
    return image[None]


def filter_matrix(taps, samples):
    width = taps.shape[1]
    center = (width - 1) // 2
    offset = jnp.arange(samples)[:, None] - jnp.arange(samples)[None, :] + center
    table = (offset[:, :, None] == jnp.arange(width)[None, None, :]).astype(jnp.bfloat16)
    return jnp.einsum("ct,nmt->cnm", taps, table, preferred_element_type=jnp.float32).astype(
        jnp.bfloat16
    )


def exchange_per_device(traces, taps, aperture, counts, time_weights, amplitudes):
    tiles = lax.axis_size("tile")
    myself = lax.axis_index("tile")
    block_count = traces.shape[1]
    samples = traces.shape[3]
    slots = aperture.shape[2]
    capacity = max(2, slots // tiles)
    listing = aperture[0]
    filled = counts[0]
    owners = listing // block_count
    within = listing - owners * block_count
    order = jnp.arange(slots)
    earlier = order[None, :] < order[:, None]
    rank = jnp.sum((owners[:, :, None] == owners[:, None, :]) & earlier[None], axis=2)
    alive_slots = order[None, :] < filled[:, None]
    mine = (owners == myself) & alive_slots
    rank_onehot = (
        (rank[:, :, None] == jnp.arange(capacity)[None, None, :]) & mine[:, :, None]
    ).astype(jnp.bfloat16)
    local_onehot = (within[:, :, None] == jnp.arange(block_count)[None, None, :]).astype(
        jnp.bfloat16
    )
    select = jnp.einsum(
        "ksc,ksl->kcl", rank_onehot, local_onehot, preferred_element_type=jnp.float32
    ).astype(jnp.bfloat16)
    operator = filter_matrix(taps, samples)
    own_owner = lax.dynamic_index_in_dim(owners, myself, 0, keepdims=False)
    own_rank = lax.dynamic_index_in_dim(rank, myself, 0, keepdims=False)
    own_fill = lax.dynamic_index_in_dim(filled, myself, 0, keepdims=False)
    source_slot = own_owner * capacity + own_rank
    arrived_rows = tiles * capacity

    def pick_rows(positions):
        return (positions[:, None] == jnp.arange(arrived_rows)[None, :]).astype(jnp.bfloat16)

    filtered = jnp.einsum(
        "cnm,kbm->kcbn", operator, traces[0], preferred_element_type=jnp.float32
    ).astype(jnp.bfloat16)
    outgoing = jnp.einsum(
        "kcl,lqbn->kcqbn", select, filtered, preferred_element_type=jnp.float32
    ).astype(jnp.bfloat16)
    arrived = lax.all_to_all(outgoing, "tile", split_axis=0, concat_axis=0, tiled=True)
    arrived = arrived.reshape((arrived_rows,) + arrived.shape[2:])

    def fetch(positions):
        return jnp.einsum(
            "gq,qcbn->gcbn", pick_rows(positions), arrived, preferred_element_type=jnp.float32
        ).astype(jnp.bfloat16)

    weights = time_weights[0, 0]
    spread = amplitudes[0, 0]

    def add_group(index, total):
        start = index * group_slots
        positions = lax.dynamic_slice_in_dim(source_slot, start, group_slots, 0)
        blocks = fetch(positions)
        part_weights = lax.dynamic_slice_in_dim(weights, start, group_slots, 0)
        part_spread = lax.dynamic_slice_in_dim(spread, start, group_slots, 0)
        alive = (start + jnp.arange(group_slots) < own_fill).astype(jnp.float32)
        interp = jnp.einsum(
            "gtn,gcbn->gcbt", part_weights, blocks, preferred_element_type=jnp.float32
        )
        interp = (interp * alive[:, None, None, None]).astype(jnp.bfloat16)
        return total + jnp.einsum(
            "gcbt,gcbp->tp", interp, part_spread, preferred_element_type=jnp.float32
        )

    rounds = (own_fill + group_slots - 1) // group_slots
    partial_value = lax.fori_loop(
        0, rounds, add_group, jnp.zeros((weights.shape[1], spread.shape[-1]), jnp.float32)
    )
    image = lax.psum_scatter(partial_value, "trace", scatter_dimension=0, tiled=True)
    return image[None]


def per_device(traces, taps, aperture, counts, time_weights, amplitudes):
    tiles = lax.axis_size("tile")
    every_block = traces.shape[1] * tiles
    quarter = traces.shape[1] // quarters
    gathers = (
        every_block == aperture.shape[2]
        and tiles == 2 * rows_z
        and lax.axis_size("trace") == 4
        and quarter * quarters == traces.shape[1]
    )
    form = gather_per_device if gathers else exchange_per_device
    return form(traces, taps, aperture, counts, time_weights, amplitudes)


def solution(mesh):
    placed = (
        P("trace", "tile", None, None),
        P(),
        P("trace", None, None),
        P("trace", None),
        P("trace", "tile", None, None, None),
        P("trace", "tile", None, None, None, None),
    )
    return jax.shard_map(
        per_device, mesh=mesh, in_specs=placed, out_specs=P("tile", "trace", None), check_vma=False
    )
```

```python
import jax
import jax.numpy as jnp
from jax import lax
from jax.experimental import pallas as pl
from jax.experimental.pallas import tpu as pltpu
from jax.sharding import PartitionSpec as P

group_slots = 8
quarters = 4
rows_z = 4
events = 14
MESH = pl.DeviceIdType.MESH


def migrate_kernel(
    counts_hbm,
    aperture_hbm,
    taps_hbm,
    traces_ref,
    weights_ref,
    spread_ref,
    out_ref,
    gathered,
    weights,
    spread,
    operator,
    total,
    outgoing,
    parts,
    counts_ref,
    aperture_ref,
    taps_ref,
    band,
    lookup,
    slot_of,
    recv_sem,
    send_sem,
    load_sem,
    part_send_sem,
    part_recv_sem,
    far_sem,
    near_sem,
    turn_sem,
    gift,
    gift_recv_sem,
    staged_weights,
    staged_spread,
    lent_weights,
    lent_spread,
    lend_sem,
    lent_sem,
    kept,
):
    tile = lax.axis_index("tile")
    subset = lax.axis_index("trace")
    z = tile // 2
    x = tile % 2
    other = 1 - x
    low = z < rows_z // 2
    inward = jnp.where(low, 1, -1)
    place = jnp.where(low, z, rows_z - 1 - z)
    end = place == 0
    middle = place == 1
    samples = operator.shape[0]
    taus = weights.shape[1]
    block_rows = spread.shape[2]
    chunk_rows = gathered.shape[2]
    chunk_blocks = chunk_rows // block_rows
    block_count = chunk_blocks * quarters
    share = out_ref.shape[0]

    load_small = [
        pltpu.make_async_copy(src, dst, load_sem.at[4 + at])
        for at, (src, dst) in enumerate(
            ((counts_hbm, counts_ref), (aperture_hbm, aperture_ref), (taps_hbm, taps_ref))
        )
    ]
    load_own = pltpu.make_async_copy(traces_ref, gathered.at[tile], load_sem.at[0])
    load_weights = pltpu.make_async_copy(weights_ref, weights, load_sem.at[1])
    load_spread = pltpu.make_async_copy(spread_ref, spread, load_sem.at[2])

    row_y = subset // 2
    core = subset % 2
    across_y = (1 - row_y) * 2
    giver = end & (core == 0)
    taker = end & (core == 1)
    peers = (across_y + core, across_y + 1 - core, row_y * 2 + 1 - core)

    barrier = pltpu.get_barrier_semaphore()
    neighbours = {
        "x": z * 2 + other,
        "in": tile + 2 * inward,
        "out": tile - 2 * inward,
    }

    def greet(to_tile, to_subset):
        pl.semaphore_signal(barrier, inc=1, device_id=(to_tile, to_subset), device_id_type=MESH)

    greet(neighbours["in"], subset)
    greet(neighbours["x"], subset)

    @pl.when(middle)
    def _():
        greet(neighbours["out"], subset)

    for peer in (peers[0], peers[2]):
        greet(tile, peer)
    load_own.start()
    for load in load_small:
        load.start()
    load_own.wait()
    load_weights.start()
    load_spread.start()
    pl.semaphore_wait(barrier, 4 + jnp.where(middle, 1, 0))

    def send(way, origin, quarter):
        return pltpu.make_async_remote_copy(
            src_ref=gathered.at[origin, quarter],
            dst_ref=gathered.at[origin, quarter],
            send_sem=send_sem.at[("x", "in", "out").index(way), origin, quarter],
            recv_sem=recv_sem.at[origin, quarter],
            device_id=(neighbours[way], subset),
            device_id_type=MESH,
        )

    def wait_arrival(origin, quarter):
        pltpu.make_async_remote_copy(
            src_ref=gathered.at[origin, quarter],
            dst_ref=gathered.at[origin, quarter],
            send_sem=send_sem.at[0, 0, 0],
            recv_sem=recv_sem.at[origin, quarter],
            device_id=(neighbours["x"], subset),
            device_id_type=MESH,
        ).wait_recv()

    def send_own(quarters_now):
        for quarter in quarters_now:
            @pl.when(middle)
            def _():
                send("out", tile, quarter).start()

            send("x", tile, (quarter + jnp.where(end, 2, 0)) % quarters).start()
            send("in", tile, quarter).start()

    send_own(range(3))

    @pl.when(core == 0)
    def _():
        send_own(range(3, quarters))
        pl.semaphore_signal(turn_sem, inc=1, device_id=(tile, peers[2]), device_id_type=MESH)

    @pl.when(core == 1)
    def _():
        pl.semaphore_wait(turn_sem, 1)
        send_own(range(3, quarters))

    @pl.when(giver)
    def _():
        for neighbour in ("in", "x"):
            pl.semaphore_signal(
                near_sem,
                inc=1,
                device_id=(neighbours[neighbour], subset),
                device_id_type=MESH,
            )

    pl.semaphore_signal(far_sem, inc=1, device_id=(tile, peers[0]), device_id_type=MESH)
    for load in load_small:
        load.wait()
    slots = weights.shape[0]
    listing = aperture_ref[0, pl.ds(tile, 1), :]
    slot = lax.broadcasted_iota(jnp.int32, (slots, slots), 0)
    block = lax.broadcasted_iota(jnp.int32, (slots, slots), 1)
    named = jnp.broadcast_to(listing, (slots, slots)).T
    match = (named == block) & (slot < counts_ref[0, tile])
    lookup[...] = jnp.broadcast_to(
        jnp.sum(jnp.where(match, slot + 1, 0), axis=0, keepdims=True) - 1, lookup.shape
    )
    publish = pltpu.make_async_copy(lookup, slot_of, load_sem.at[3])
    publish.start()

    half_taps = (taps_ref.shape[1] - 1) // 2
    band[...] = jnp.zeros_like(band)
    band[0:2, 0 : taps_ref.shape[1]] = taps_ref[...].astype(jnp.float32)
    row = lax.broadcasted_iota(jnp.int32, (samples, samples), 0)
    gap = lax.broadcasted_iota(jnp.int32, (samples, samples), 1) - row
    inside = (gap <= half_taps) & (gap >= -half_taps)
    for channel in range(2):
        centred = pltpu.roll(band[...], samples - half_taps, 1)[channel : channel + 1, :]
        shifted = jnp.broadcast_to(centred, (samples, samples))
        shift = 1
        while shift < samples:
            shifted = jnp.where((row // shift) % 2 == 1, pltpu.roll(shifted, shift, 1), shifted)
            shift *= 2
        operator[:, channel * samples : (channel + 1) * samples] = jnp.where(
            inside, shifted, 0.0
        ).astype(operator.dtype)
    total[...] = jnp.zeros_like(total)

    def tile_at(position, column):
        return jnp.where(low, position, rows_z - 1 - position) * 2 + jnp.where(
            column == 0, x, other
        )

    def arrival(event, side):
        if side == 0:
            late = event >= 12
            end_column = jnp.where(late, 1, 0)
            end_position = jnp.where(late, 3, 1 + event // 4)
            end_quarter = jnp.where(late, event - 10, event % 4)
            end_x = event < 10
            end_in = event < 0
        else:
            end_column = 1
            end_position = event // 4
            end_quarter = jnp.where(event < 4, (event + 2) % 4, event % 4)
            end_x = event < 0
            end_in = event < 4
        number = 2 * event + side
        turn = number < 24
        stream = jnp.where(turn, number % 3, 1 + number % 2)
        index = jnp.where(turn, number // 3, number // 2 - 4)
        from_end = stream == 0
        from_middle = stream == 1
        from_x = stream == 2
        relayed = (from_end & (index >= 4)) | (from_middle & (index >= 8))
        column = jnp.where(from_x | relayed, 1, 0)
        position = jnp.where(
            from_end, 0, jnp.where(from_middle, jnp.where(relayed, 3, 2 + index // 4), 1 + index // 4)
        )
        quarter = jnp.where(relayed, (index + 2) % 4, index % 4)
        mid_x = from_middle & (index < 6)
        mid_in = from_end & (index < 6)
        mid_out = from_middle
        origin = tile_at(
            jnp.where(end, end_position, position), jnp.where(end, end_column, column)
        )
        ways = {
            "x": (end & end_x) | (middle & mid_x),
            "in": (end & end_in) | (middle & mid_in),
            "out": middle & mid_out,
        }
        return origin, jnp.where(end, end_quarter, quarter), ways

    def give(way, origin, quarter, pair):
        return pltpu.make_async_remote_copy(
            src_ref=gathered.at[origin, quarter],
            dst_ref=gift.at[pair, ("out", "x").index(way)],
            send_sem=send_sem.at[("x", "in", "out").index(way), origin, quarter],
            recv_sem=gift_recv_sem.at[pair, ("out", "x").index(way)],
            device_id=(neighbours[way], peers[2]),
            device_id_type=MESH,
        )

    def each_way(event, side, act, before_gift):
        origin, quarter, ways = arrival(event, side)
        gifts = {"in": False, "out": False, "x": False}
        if side == 0:
            gifts["out"] = middle & (core == 0) & (event >= 12)
            gifts["x"] = end & (core == 0) & ((event == 8) | (event == 9))
        for way in ("out", "x", "in"):
            given = gifts[way]

            @pl.when(ways[way] & jnp.logical_not(given))
            def _():
                act(send(way, origin, quarter))

            if given is not False:

                @pl.when(given)
                def _():
                    first = 12 if way == "out" else 8
                    pl.when(jnp.int32(event) == first)(before_gift)
                    act(give(way, origin, quarter, event - first))

    def take(event):
        for side in range(2):
            origin, quarter, _ = arrival(event, side)
            wait_arrival(origin, quarter)
            each_way(
                event,
                side,
                lambda copy: copy.start(),
                lambda: pl.semaphore_wait(near_sem, 1),
            )

    lanes = lax.broadcasted_iota(jnp.int32, (1, 2 * chunk_rows), 1)
    member = (lanes // block_rows) % chunk_blocks

    def migrate(rows, groups):
        filtered = jnp.dot(rows, operator[...], preferred_element_type=jnp.float32).astype(
            jnp.bfloat16
        )
        image = None
        for at, (stacked, columns, gains) in enumerate(groups):
            first = at * chunk_rows
            blocks = jnp.concatenate(
                [
                    filtered[first : first + chunk_rows, 0:samples],
                    filtered[first : first + chunk_rows, samples : 2 * samples],
                ],
                axis=0,
            )
            product = lax.dot_general(
                stacked, blocks, (((1,), (1,)), ((), ())), preferred_element_type=jnp.float32
            )
            interp = product[0:taus]
            for index in range(1, chunk_blocks):
                interp = jnp.where(
                    member == index, product[index * taus : (index + 1) * taus], interp
                )
            if gains is not None:
                alive = jnp.full((1, 2 * chunk_rows), gains[0], jnp.float32)
                for index in range(1, chunk_blocks):
                    alive = jnp.where(member == index, gains[index], alive)
                interp = interp * alive
            interp = interp.astype(jnp.bfloat16)
            part = jnp.dot(interp, columns, preferred_element_type=jnp.float32)
            image = part if image is None else image + part
        total[...] += image

    def look_up(origin, quarter):
        base = origin * block_count + quarter * chunk_blocks
        found = [slot_of[0, base + index] for index in range(chunk_blocks)]
        picks = [jnp.maximum(value, 0) for value in found]
        gains = [jnp.where(value >= 0, 1.0, 0.0) for value in found]
        return picks, gains

    def compute(chunks):
        rows = jnp.concatenate([gathered[origin, quarter] for origin, quarter in chunks], axis=0)
        groups = []
        for origin, quarter in chunks:
            picks, gains = look_up(origin, quarter)
            stacked = jnp.concatenate([weights[pick] for pick in picks], axis=0)
            columns = jnp.concatenate(
                [spread[pick, channel] for channel in range(2) for pick in picks], axis=0
            )
            groups.append((stacked, columns, gains))
        migrate(rows, groups)

    lending = [
        pltpu.make_async_remote_copy(
            src_ref=src,
            dst_ref=dst,
            send_sem=lend_sem.at[at],
            recv_sem=lent_sem.at[at],
            device_id=(tile, peers[2]),
            device_id_type=MESH,
        )
        for at, (src, dst) in enumerate(
            ((staged_weights, lent_weights), (staged_spread, lent_spread))
        )
    ]

    def lend():
        for at, quarter in enumerate((2, 0, 3, 1)):
            picks, gains = look_up(tile_at(3, 1), quarter)
            for index, (pick, gain) in enumerate(zip(picks, gains, strict=True)):
                staged_weights[at * chunk_blocks + index] = weights[pick]
                staged_spread[at * chunk_blocks + index] = (
                    spread[pick].astype(jnp.float32) * gain
                ).astype(staged_spread.dtype)
        for copy in lending:
            copy.start()

    half_taus = 2 * share

    def keep_filtered(rows):
        filtered = jnp.dot(rows, operator[...], preferred_element_type=jnp.float32).astype(
            jnp.bfloat16
        )
        for at in range(2):
            first = at * chunk_rows
            for channel in range(2):
                kept[at, channel * chunk_rows : (channel + 1) * chunk_rows, :] = filtered[
                    first : first + chunk_rows, channel * samples : (channel + 1) * samples
                ]

    def add_half(at_rows, groups):
        image = None
        for at, (stacked, columns, gains) in enumerate(groups):
            product = lax.dot_general(
                stacked, kept[at], (((1,), (1,)), ((), ())), preferred_element_type=jnp.float32
            )
            interp = product[0:half_taus]
            alive = jnp.full((1, 2 * chunk_rows), gains[0], jnp.float32)
            for index in range(1, chunk_blocks):
                here = member == index
                interp = jnp.where(
                    here, product[index * half_taus : (index + 1) * half_taus], interp
                )
                alive = jnp.where(here, gains[index], alive)
            part = jnp.dot(
                (interp * alive).astype(jnp.bfloat16), columns, preferred_element_type=jnp.float32
            )
            image = part if image is None else image + part
        total[pl.ds(at_rows, half_taus), :] += image

    last_own = [arrival(11, side)[0:2] for side in range(2)]

    def giver_half(at_rows):
        groups = []
        for origin, quarter in last_own:
            picks, gains = look_up(origin, quarter)
            stacked = jnp.concatenate(
                [weights[pick, pl.ds(at_rows, half_taus), :] for pick in picks], axis=0
            )
            columns = jnp.concatenate(
                [spread[pick, channel] for channel in range(2) for pick in picks], axis=0
            )
            groups.append((stacked, columns, gains))
        add_half(at_rows, groups)

    def taker_half(at_rows):
        groups = []
        for at in range(2):
            mine = range((2 + at) * chunk_blocks, (3 + at) * chunk_blocks)
            stacked = jnp.concatenate(
                [lent_weights[index, pl.ds(at_rows, half_taus), :] for index in mine], axis=0
            )
            columns = jnp.concatenate(
                [lent_spread[index, channel] for channel in range(2) for index in mine], axis=0
            )
            groups.append((stacked, columns, [1.0] * chunk_blocks))
        add_half(at_rows, groups)

    far_rows = pl.multiple_of(across_y * share, half_taus)
    near_rows = pl.multiple_of(row_y * 2 * share, half_taus)

    def giver_first():
        take(11)
        keep_filtered(
            jnp.concatenate([gathered[origin, quarter] for origin, quarter in last_own], axis=0)
        )
        giver_half(far_rows)

    def first_gift():
        for copy in lending:
            copy.wait_recv()
        for way in ("out", "x"):
            give(way, 0, 0, 0).wait_recv()
        groups = []
        for at in range(2):
            mine = range(at * chunk_blocks, (at + 1) * chunk_blocks)
            stacked = jnp.concatenate([lent_weights[index] for index in mine], axis=0)
            columns = jnp.concatenate(
                [lent_spread[index, channel] for channel in range(2) for index in mine], axis=0
            )
            groups.append((stacked, columns, None))
        migrate(jnp.concatenate([gift[0, 0], gift[0, 1]], axis=0), groups)

    def taker_first():
        for way in ("out", "x"):
            give(way, 0, 0, 1).wait_recv()
        keep_filtered(jnp.concatenate([gift[1, 0], gift[1, 1]], axis=0))
        taker_half(far_rows)

    take(0)

    @pl.when(middle)
    def _():
        take(1)

    load_weights.wait()
    load_spread.wait()
    publish.wait()

    def step(number, carry):
        pl.when(giver & (number == 8))(lend)
        caught_up = number >= 6
        end_takes = (number == 1) | (number == 3) | (number == 5) | caught_up
        middle_takes = number + 2 < events
        end_event = jnp.where(caught_up, number - 2, (number + 1) // 2)

        @pl.when((end & end_takes) | (middle & middle_takes))
        def _():
            take(jnp.where(end, end_event, number + 2))

        chunks = []
        for side in range(2):
            origin, quarter, _ = arrival(jnp.maximum(number - 2, 0), side)
            own = number < 2
            chunks.append(
                (jnp.where(own, tile, origin), jnp.where(own, 2 * number + side, quarter))
            )
        compute(chunks)
        return carry

    lax.fori_loop(0, events + 2 - jnp.where(giver, 3, 0), step, 0)
    pl.when(taker)(first_gift)
    pl.when(giver)(giver_first)
    pl.when(taker)(taker_first)
    pl.semaphore_wait(far_sem, 1)

    def exchange(at, peer):
        return pltpu.make_async_remote_copy(
            src_ref=outgoing.at[at],
            dst_ref=parts.at[at],
            send_sem=part_send_sem.at[at],
            recv_sem=part_recv_sem.at[at],
            device_id=(tile, peer),
            device_id_type=MESH,
        )

    def ship(at, peer):
        outgoing[at] = total[pl.ds(pl.multiple_of(peer * share, share), share), :].astype(
            outgoing.dtype
        )
        exchange(at, peer).start()

    ship(core, across_y)
    ship(1 - core, across_y + 1)
    pl.when(giver)(lambda: giver_half(near_rows))
    pl.when(taker)(lambda: taker_half(near_rows))
    ship(2, peers[2])
    exchanges = [exchange(at, peer) for at, peer in enumerate(peers)]

    for quarter in range(quarters):
        send("in", tile, quarter).wait_send()

        @pl.when(middle)
        def _():
            send("out", tile, quarter).wait_send()

        send("x", tile, quarter).wait_send()

    def sent(event, carry):
        for side in range(2):
            each_way(event, side, lambda copy: copy.wait_send(), lambda: None)
        return carry

    lax.fori_loop(0, events, sent, 0)

    result = total[pl.ds(pl.multiple_of(subset * share, share), share), :]
    for at, copy in enumerate(exchanges):
        copy.wait_recv()
        result = result + parts[at].astype(jnp.float32)
    out_ref[...] = result
    for copy in exchanges:
        copy.wait_send()

    @pl.when(giver)
    def _():
        for copy in lending:
            copy.wait_send()


def keep(array):
    return pltpu.with_memory_space_constraint(array, pltpu.HBM)


def gather_per_device(traces, taps, aperture, counts, time_weights, amplitudes):
    tiles = lax.axis_size("tile")
    subsets = lax.axis_size("trace")
    _, block_count, block_rows, samples = traces.shape
    slots, taus = time_weights.shape[2:4]
    columns = amplitudes.shape[-1]
    chunk_rows = block_count * block_rows // quarters
    share = taus // subsets
    lent_blocks = 4 * block_count // quarters
    vmem = pl.BlockSpec(memory_space=pltpu.VMEM)
    hbm = pl.BlockSpec(memory_space=pl.ANY)
    image = pl.pallas_call(
        migrate_kernel,
        out_shape=jax.ShapeDtypeStruct((share, columns), jnp.float32),
        in_specs=[hbm] * 6,
        out_specs=vmem,
        scratch_shapes=[
            pltpu.VMEM((tiles, quarters, chunk_rows, samples), jnp.bfloat16),
            pltpu.VMEM((slots, taus, samples), jnp.bfloat16),
            pltpu.VMEM((slots, 2, block_rows, columns), jnp.bfloat16),
            pltpu.VMEM((samples, 2 * samples), jnp.bfloat16),
            pltpu.VMEM((taus, columns), jnp.float32),
            pltpu.VMEM((subsets - 1, share, columns), jnp.bfloat16),
            pltpu.VMEM((subsets - 1, share, columns), jnp.bfloat16),
            pltpu.SMEM(counts.shape, jnp.int32),
            pltpu.VMEM(aperture.shape, jnp.int32),
            pltpu.VMEM(taps.shape, taps.dtype),
            pltpu.VMEM((8, samples), jnp.float32),
            pltpu.VMEM((8, slots), jnp.int32),
            pltpu.SMEM((8, slots), jnp.int32),
            pltpu.SemaphoreType.DMA((tiles, quarters)),
            pltpu.SemaphoreType.DMA((3, tiles, quarters)),
            pltpu.SemaphoreType.DMA((7,)),
            pltpu.SemaphoreType.DMA((subsets - 1,)),
            pltpu.SemaphoreType.DMA((subsets - 1,)),
            pltpu.SemaphoreType.REGULAR,
            pltpu.SemaphoreType.REGULAR,
            pltpu.SemaphoreType.REGULAR,
            pltpu.VMEM((2, 2, chunk_rows, samples), jnp.bfloat16),
            pltpu.SemaphoreType.DMA((2, 2)),
            pltpu.VMEM((lent_blocks, taus, samples), jnp.bfloat16),
            pltpu.VMEM((lent_blocks, 2, block_rows, columns), jnp.bfloat16),
            pltpu.VMEM((lent_blocks, taus, samples), jnp.bfloat16),
            pltpu.VMEM((lent_blocks, 2, block_rows, columns), jnp.bfloat16),
            pltpu.SemaphoreType.DMA((2,)),
            pltpu.SemaphoreType.DMA((2,)),
            pltpu.VMEM((2, 2 * chunk_rows, samples), jnp.bfloat16),
        ],
        compiler_params=pltpu.CompilerParams(
            collective_id=0, has_side_effects=True, vmem_limit_bytes=48 * 1024 * 1024
        ),
    )(
        keep(counts),
        keep(aperture),
        keep(taps),
        keep(traces.reshape(quarters, chunk_rows, samples)),
        keep(time_weights[0, 0]),
        keep(amplitudes[0, 0]),
    )
    return image[None]


def filter_matrix(taps, samples):
    width = taps.shape[1]
    center = (width - 1) // 2
    offset = jnp.arange(samples)[:, None] - jnp.arange(samples)[None, :] + center
    table = (offset[:, :, None] == jnp.arange(width)[None, None, :]).astype(jnp.bfloat16)
    return jnp.einsum("ct,nmt->cnm", taps, table, preferred_element_type=jnp.float32).astype(
        jnp.bfloat16
    )


def exchange_per_device(traces, taps, aperture, counts, time_weights, amplitudes):
    tiles = lax.axis_size("tile")
    myself = lax.axis_index("tile")
    block_count = traces.shape[1]
    samples = traces.shape[3]
    slots = aperture.shape[2]
    capacity = max(2, slots // tiles)
    listing = aperture[0]
    filled = counts[0]
    owners = listing // block_count
    within = listing - owners * block_count
    order = jnp.arange(slots)
    earlier = order[None, :] < order[:, None]
    rank = jnp.sum((owners[:, :, None] == owners[:, None, :]) & earlier[None], axis=2)
    alive_slots = order[None, :] < filled[:, None]
    mine = (owners == myself) & alive_slots
    rank_onehot = (
        (rank[:, :, None] == jnp.arange(capacity)[None, None, :]) & mine[:, :, None]
    ).astype(jnp.bfloat16)
    local_onehot = (within[:, :, None] == jnp.arange(block_count)[None, None, :]).astype(
        jnp.bfloat16
    )
    select = jnp.einsum(
        "ksc,ksl->kcl", rank_onehot, local_onehot, preferred_element_type=jnp.float32
    ).astype(jnp.bfloat16)
    operator = filter_matrix(taps, samples)
    own_owner = lax.dynamic_index_in_dim(owners, myself, 0, keepdims=False)
    own_rank = lax.dynamic_index_in_dim(rank, myself, 0, keepdims=False)
    own_fill = lax.dynamic_index_in_dim(filled, myself, 0, keepdims=False)
    source_slot = own_owner * capacity + own_rank
    arrived_rows = tiles * capacity

    def pick_rows(positions):
        return (positions[:, None] == jnp.arange(arrived_rows)[None, :]).astype(jnp.bfloat16)

    filtered = jnp.einsum(
        "cnm,kbm->kcbn", operator, traces[0], preferred_element_type=jnp.float32
    ).astype(jnp.bfloat16)
    outgoing = jnp.einsum(
        "kcl,lqbn->kcqbn", select, filtered, preferred_element_type=jnp.float32
    ).astype(jnp.bfloat16)
    arrived = lax.all_to_all(outgoing, "tile", split_axis=0, concat_axis=0, tiled=True)
    arrived = arrived.reshape((arrived_rows,) + arrived.shape[2:])

    def fetch(positions):
        return jnp.einsum(
            "gq,qcbn->gcbn", pick_rows(positions), arrived, preferred_element_type=jnp.float32
        ).astype(jnp.bfloat16)

    weights = time_weights[0, 0]
    spread = amplitudes[0, 0]

    def add_group(index, total):
        start = index * group_slots
        positions = lax.dynamic_slice_in_dim(source_slot, start, group_slots, 0)
        blocks = fetch(positions)
        part_weights = lax.dynamic_slice_in_dim(weights, start, group_slots, 0)
        part_spread = lax.dynamic_slice_in_dim(spread, start, group_slots, 0)
        alive = (start + jnp.arange(group_slots) < own_fill).astype(jnp.float32)
        interp = jnp.einsum(
            "gtn,gcbn->gcbt", part_weights, blocks, preferred_element_type=jnp.float32
        )
        interp = (interp * alive[:, None, None, None]).astype(jnp.bfloat16)
        return total + jnp.einsum(
            "gcbt,gcbp->tp", interp, part_spread, preferred_element_type=jnp.float32
        )

    rounds = (own_fill + group_slots - 1) // group_slots
    partial_value = lax.fori_loop(
        0, rounds, add_group, jnp.zeros((weights.shape[1], spread.shape[-1]), jnp.float32)
    )
    image = lax.psum_scatter(partial_value, "trace", scatter_dimension=0, tiled=True)
    return image[None]


def per_device(traces, taps, aperture, counts, time_weights, amplitudes):
    tiles = lax.axis_size("tile")
    every_block = traces.shape[1] * tiles
    quarter = traces.shape[1] // quarters
    gathers = (
        every_block == aperture.shape[2]
        and tiles == 2 * rows_z
        and lax.axis_size("trace") == 4
        and quarter * quarters == traces.shape[1]
    )
    form = gather_per_device if gathers else exchange_per_device
    return form(traces, taps, aperture, counts, time_weights, amplitudes)


def solution(mesh):
    placed = (
        P("trace", "tile", None, None),
        P(),
        P("trace", None, None),
        P("trace", None),
        P("trace", "tile", None, None, None),
        P("trace", "tile", None, None, None, None),
    )
    return jax.shard_map(
        per_device, mesh=mesh, in_specs=placed, out_specs=P("tile", "trace", None), check_vma=False
    )
```

```python
import jax
import jax.numpy as jnp
from jax import lax
from jax.experimental import pallas as pl
from jax.experimental.pallas import tpu as pltpu
from jax.sharding import PartitionSpec as P

group_slots = 8
quarters = 4
rows_z = 4
events = 14
MESH = pl.DeviceIdType.MESH


def migrate_kernel(
    counts_hbm,
    aperture_hbm,
    taps_hbm,
    traces_ref,
    weights_ref,
    spread_ref,
    out_ref,
    parts,
    gathered,
    weights,
    spread,
    operator,
    total,
    outgoing,
    counts_ref,
    aperture_ref,
    taps_ref,
    band,
    lookup,
    slot_of,
    recv_sem,
    send_sem,
    load_sem,
    part_send_sem,
    part_recv_sem,
    far_sem,
    near_sem,
    gift,
    gift_recv_sem,
    staged_weights,
    staged_spread,
    lent_weights,
    lent_spread,
    lend_sem,
    lent_sem,
    kept,
):
    tile = lax.axis_index("tile")
    subset = lax.axis_index("trace")
    z = tile // 2
    x = tile % 2
    other = 1 - x
    low = z < rows_z // 2
    inward = jnp.where(low, 1, -1)
    place = jnp.where(low, z, rows_z - 1 - z)
    end = place == 0
    middle = place == 1
    samples = operator.shape[0]
    taus = weights.shape[1]
    block_rows = spread.shape[2]
    chunk_rows = gathered.shape[2]
    chunk_blocks = chunk_rows // block_rows
    block_count = chunk_blocks * quarters
    share = out_ref.shape[0]

    load_small = [
        pltpu.make_async_copy(src, dst, load_sem.at[4 + at])
        for at, (src, dst) in enumerate(
            ((counts_hbm, counts_ref), (aperture_hbm, aperture_ref), (taps_hbm, taps_ref))
        )
    ]
    load_own = pltpu.make_async_copy(traces_ref, gathered.at[tile], load_sem.at[0])
    load_weights = pltpu.make_async_copy(weights_ref, weights, load_sem.at[1])
    load_spread = pltpu.make_async_copy(spread_ref, spread, load_sem.at[2])

    row_y = subset // 2
    core = subset % 2
    across_y = (1 - row_y) * 2
    giver = end & (core == 0)
    taker = end & (core == 1)
    peers = (across_y + core, across_y + 1 - core, row_y * 2 + 1 - core)

    barrier = pltpu.get_barrier_semaphore()
    neighbours = {
        "x": z * 2 + other,
        "in": tile + 2 * inward,
        "out": tile - 2 * inward,
    }

    def greet(to_tile, to_subset):
        pl.semaphore_signal(barrier, inc=1, device_id=(to_tile, to_subset), device_id_type=MESH)

    greet(neighbours["in"], subset)
    greet(neighbours["x"], subset)

    @pl.when(middle)
    def _():
        greet(neighbours["out"], subset)

    for peer in (peers[0], peers[2]):
        greet(tile, peer)
    load_own.start()
    for load in load_small:
        load.start()
    load_own.wait()
    load_weights.start()
    load_spread.start()
    pl.semaphore_wait(barrier, 4 + jnp.where(middle, 1, 0))

    def send(way, origin, quarter):
        return pltpu.make_async_remote_copy(
            src_ref=gathered.at[origin, quarter],
            dst_ref=gathered.at[origin, quarter],
            send_sem=send_sem.at[("x", "in", "out").index(way), origin, quarter],
            recv_sem=recv_sem.at[origin, quarter],
            device_id=(neighbours[way], subset),
            device_id_type=MESH,
        )

    def wait_arrival(origin, quarter):
        pltpu.make_async_remote_copy(
            src_ref=gathered.at[origin, quarter],
            dst_ref=gathered.at[origin, quarter],
            send_sem=send_sem.at[0, 0, 0],
            recv_sem=recv_sem.at[origin, quarter],
            device_id=(neighbours["x"], subset),
            device_id_type=MESH,
        ).wait_recv()

    for quarter in range(quarters):
        send("in", tile, quarter).start()

        @pl.when(middle)
        def _():
            send("out", tile, quarter).start()

        send("x", tile, (quarter + jnp.where(end, 2, 0)) % quarters).start()

    @pl.when(giver)
    def _():
        for neighbour in ("in", "x"):
            pl.semaphore_signal(
                near_sem,
                inc=1,
                device_id=(neighbours[neighbour], subset),
                device_id_type=MESH,
            )

    pl.semaphore_signal(far_sem, inc=1, device_id=(tile, peers[0]), device_id_type=MESH)
    for load in load_small:
        load.wait()
    slots = weights.shape[0]
    listing = aperture_ref[0, pl.ds(tile, 1), :]
    slot = lax.broadcasted_iota(jnp.int32, (slots, slots), 0)
    block = lax.broadcasted_iota(jnp.int32, (slots, slots), 1)
    named = jnp.broadcast_to(listing, (slots, slots)).T
    match = (named == block) & (slot < counts_ref[0, tile])
    lookup[...] = jnp.broadcast_to(
        jnp.sum(jnp.where(match, slot + 1, 0), axis=0, keepdims=True) - 1, lookup.shape
    )
    publish = pltpu.make_async_copy(lookup, slot_of, load_sem.at[3])
    publish.start()

    half_taps = (taps_ref.shape[1] - 1) // 2
    band[...] = jnp.zeros_like(band)
    band[0:2, 0 : taps_ref.shape[1]] = taps_ref[...].astype(jnp.float32)
    row = lax.broadcasted_iota(jnp.int32, (samples, samples), 0)
    gap = lax.broadcasted_iota(jnp.int32, (samples, samples), 1) - row
    inside = (gap <= half_taps) & (gap >= -half_taps)
    for channel in range(2):
        centred = pltpu.roll(band[...], samples - half_taps, 1)[channel : channel + 1, :]
        shifted = jnp.broadcast_to(centred, (samples, samples))
        shift = 1
        while shift < samples:
            shifted = jnp.where((row // shift) % 2 == 1, pltpu.roll(shifted, shift, 1), shifted)
            shift *= 2
        operator[:, channel * samples : (channel + 1) * samples] = jnp.where(
            inside, shifted, 0.0
        ).astype(operator.dtype)
    total[...] = jnp.zeros_like(total)

    def tile_at(position, column):
        return jnp.where(low, position, rows_z - 1 - position) * 2 + jnp.where(
            column == 0, x, other
        )

    def arrival(event, side):
        if side == 0:
            late = event >= 12
            end_column = jnp.where(late, 1, 0)
            end_position = jnp.where(late, 3, 1 + event // 4)
            end_quarter = jnp.where(late, event - 10, event % 4)
            end_x = event < 10
            end_in = event < 0
        else:
            end_column = 1
            end_position = event // 4
            end_quarter = jnp.where(event < 4, (event + 2) % 4, event % 4)
            end_x = event < 0
            end_in = event < 4
        number = 2 * event + side
        turn = number < 24
        stream = jnp.where(turn, number % 3, 1 + number % 2)
        index = jnp.where(turn, number // 3, number // 2 - 4)
        from_end = stream == 0
        from_middle = stream == 1
        from_x = stream == 2
        relayed = (from_end & (index >= 4)) | (from_middle & (index >= 8))
        column = jnp.where(from_x | relayed, 1, 0)
        position = jnp.where(
            from_end, 0, jnp.where(from_middle, jnp.where(relayed, 3, 2 + index // 4), 1 + index // 4)
        )
        quarter = jnp.where(relayed, (index + 2) % 4, index % 4)
        mid_x = from_middle & (index < 6)
        mid_in = from_end & (index < 6)
        mid_out = from_middle
        origin = tile_at(
            jnp.where(end, end_position, position), jnp.where(end, end_column, column)
        )
        ways = {
            "x": (end & end_x) | (middle & mid_x),
            "in": (end & end_in) | (middle & mid_in),
            "out": middle & mid_out,
        }
        return origin, jnp.where(end, end_quarter, quarter), ways

    def give(way, origin, quarter, pair):
        return pltpu.make_async_remote_copy(
            src_ref=gathered.at[origin, quarter],
            dst_ref=gift.at[pair, ("out", "x").index(way)],
            send_sem=send_sem.at[("x", "in", "out").index(way), origin, quarter],
            recv_sem=gift_recv_sem.at[pair, ("out", "x").index(way)],
            device_id=(neighbours[way], peers[2]),
            device_id_type=MESH,
        )

    def each_way(event, side, act, before_gift):
        origin, quarter, ways = arrival(event, side)
        gifts = {"in": False, "out": False, "x": False}
        if side == 0:
            gifts["out"] = middle & (core == 0) & (event >= 12)
            gifts["x"] = end & (core == 0) & ((event == 8) | (event == 9))
        for way in ("out", "in", "x"):
            given = gifts[way]

            @pl.when(ways[way] & jnp.logical_not(given))
            def _():
                act(send(way, origin, quarter))

            if given is not False:

                @pl.when(given)
                def _():
                    first = 12 if way == "out" else 8
                    pl.when(jnp.int32(event) == first)(before_gift)
                    act(give(way, origin, quarter, event - first))

    def take(event):
        for side in range(2):
            origin, quarter, _ = arrival(event, side)
            wait_arrival(origin, quarter)
            each_way(
                event,
                side,
                lambda copy: copy.start(),
                lambda: pl.semaphore_wait(near_sem, 1),
            )

    lanes = lax.broadcasted_iota(jnp.int32, (1, 2 * chunk_rows), 1)
    member = (lanes // block_rows) % chunk_blocks

    def migrate(rows, groups):
        filtered = jnp.dot(rows, operator[...], preferred_element_type=jnp.float32).astype(
            jnp.bfloat16
        )
        image = None
        for at, (stacked, columns, gains) in enumerate(groups):
            first = at * chunk_rows
            blocks = jnp.concatenate(
                [
                    filtered[first : first + chunk_rows, 0:samples],
                    filtered[first : first + chunk_rows, samples : 2 * samples],
                ],
                axis=0,
            )
            product = lax.dot_general(
                stacked, blocks, (((1,), (1,)), ((), ())), preferred_element_type=jnp.float32
            )
            interp = product[0:taus]
            for index in range(1, chunk_blocks):
                interp = jnp.where(
                    member == index, product[index * taus : (index + 1) * taus], interp
                )
            if gains is not None:
                alive = jnp.full((1, 2 * chunk_rows), gains[0], jnp.float32)
                for index in range(1, chunk_blocks):
                    alive = jnp.where(member == index, gains[index], alive)
                interp = interp * alive
            interp = interp.astype(jnp.bfloat16)
            part = jnp.dot(interp, columns, preferred_element_type=jnp.float32)
            image = part if image is None else image + part
        total[...] += image

    def look_up(origin, quarter):
        base = origin * block_count + quarter * chunk_blocks
        found = [slot_of[0, base + index] for index in range(chunk_blocks)]
        picks = [jnp.maximum(value, 0) for value in found]
        gains = [jnp.where(value >= 0, 1.0, 0.0) for value in found]
        return picks, gains

    def compute(chunks):
        rows = jnp.concatenate([gathered[origin, quarter] for origin, quarter in chunks], axis=0)
        groups = []
        for origin, quarter in chunks:
            picks, gains = look_up(origin, quarter)
            stacked = jnp.concatenate([weights[pick] for pick in picks], axis=0)
            columns = jnp.concatenate(
                [spread[pick, channel] for channel in range(2) for pick in picks], axis=0
            )
            groups.append((stacked, columns, gains))
        migrate(rows, groups)

    lending = [
        pltpu.make_async_remote_copy(
            src_ref=src,
            dst_ref=dst,
            send_sem=lend_sem.at[at],
            recv_sem=lent_sem.at[at],
            device_id=(tile, peers[2]),
            device_id_type=MESH,
        )
        for at, (src, dst) in enumerate(
            ((staged_weights, lent_weights), (staged_spread, lent_spread))
        )
    ]

    def lend():
        for at, quarter in enumerate((2, 0, 3, 1)):
            picks, gains = look_up(tile_at(3, 1), quarter)
            for index, (pick, gain) in enumerate(zip(picks, gains, strict=True)):
                staged_weights[at * chunk_blocks + index] = weights[pick]
                staged_spread[at * chunk_blocks + index] = (
                    spread[pick].astype(jnp.float32) * gain
                ).astype(staged_spread.dtype)
        for copy in lending:
            copy.start()

    half_taus = 2 * share

    def keep_filtered(rows):
        filtered = jnp.dot(rows, operator[...], preferred_element_type=jnp.float32).astype(
            jnp.bfloat16
        )
        for at in range(2):
            first = at * chunk_rows
            for channel in range(2):
                kept[at, channel * chunk_rows : (channel + 1) * chunk_rows, :] = filtered[
                    first : first + chunk_rows, channel * samples : (channel + 1) * samples
                ]

    def add_half(at_rows, groups):
        image = None
        for at, (stacked, columns, gains) in enumerate(groups):
            product = lax.dot_general(
                stacked, kept[at], (((1,), (1,)), ((), ())), preferred_element_type=jnp.float32
            )
            interp = product[0:half_taus]
            alive = jnp.full((1, 2 * chunk_rows), gains[0], jnp.float32)
            for index in range(1, chunk_blocks):
                here = member == index
                interp = jnp.where(
                    here, product[index * half_taus : (index + 1) * half_taus], interp
                )
                alive = jnp.where(here, gains[index], alive)
            part = jnp.dot(
                (interp * alive).astype(jnp.bfloat16), columns, preferred_element_type=jnp.float32
            )
            image = part if image is None else image + part
        total[pl.ds(at_rows, half_taus), :] += image

    last_own = [arrival(11, side)[0:2] for side in range(2)]

    def giver_half(at_rows):
        groups = []
        for origin, quarter in last_own:
            picks, gains = look_up(origin, quarter)
            stacked = jnp.concatenate(
                [weights[pick, pl.ds(at_rows, half_taus), :] for pick in picks], axis=0
            )
            columns = jnp.concatenate(
                [spread[pick, channel] for channel in range(2) for pick in picks], axis=0
            )
            groups.append((stacked, columns, gains))
        add_half(at_rows, groups)

    def taker_half(at_rows):
        groups = []
        for at in range(2):
            mine = range((2 + at) * chunk_blocks, (3 + at) * chunk_blocks)
            stacked = jnp.concatenate(
                [lent_weights[index, pl.ds(at_rows, half_taus), :] for index in mine], axis=0
            )
            columns = jnp.concatenate(
                [lent_spread[index, channel] for channel in range(2) for index in mine], axis=0
            )
            groups.append((stacked, columns, [1.0] * chunk_blocks))
        add_half(at_rows, groups)

    far_rows = pl.multiple_of(across_y * share, half_taus)
    near_rows = pl.multiple_of(row_y * 2 * share, half_taus)

    def giver_first():
        take(11)
        keep_filtered(
            jnp.concatenate([gathered[origin, quarter] for origin, quarter in last_own], axis=0)
        )
        giver_half(far_rows)

    def first_gift():
        for copy in lending:
            copy.wait_recv()
        for way in ("out", "x"):
            give(way, 0, 0, 0).wait_recv()
        groups = []
        for at in range(2):
            mine = range(at * chunk_blocks, (at + 1) * chunk_blocks)
            stacked = jnp.concatenate([lent_weights[index] for index in mine], axis=0)
            columns = jnp.concatenate(
                [lent_spread[index, channel] for channel in range(2) for index in mine], axis=0
            )
            groups.append((stacked, columns, None))
        migrate(jnp.concatenate([gift[0, 0], gift[0, 1]], axis=0), groups)

    def taker_first():
        for way in ("out", "x"):
            give(way, 0, 0, 1).wait_recv()
        keep_filtered(jnp.concatenate([gift[1, 0], gift[1, 1]], axis=0))
        taker_half(far_rows)

    take(0)

    @pl.when(middle)
    def _():
        take(1)

    load_weights.wait()
    load_spread.wait()
    publish.wait()

    def step(number, carry):
        pl.when(giver & (number == 8))(lend)
        caught_up = number >= 6
        end_takes = (number == 1) | (number == 3) | (number == 5) | caught_up
        middle_takes = number + 2 < events
        end_event = jnp.where(caught_up, number - 2, (number + 1) // 2)

        @pl.when((end & end_takes) | (middle & middle_takes))
        def _():
            take(jnp.where(end, end_event, number + 2))

        chunks = []
        for side in range(2):
            origin, quarter, _ = arrival(jnp.maximum(number - 2, 0), side)
            own = number < 2
            chunks.append(
                (jnp.where(own, tile, origin), jnp.where(own, 2 * number + side, quarter))
            )
        compute(chunks)
        return carry

    lax.fori_loop(0, events + 2 - jnp.where(giver, 3, 0), step, 0)
    pl.when(taker)(first_gift)
    pl.when(giver)(giver_first)
    pl.when(taker)(taker_first)
    pl.semaphore_wait(far_sem, 1)

    def exchange(at, peer):
        return pltpu.make_async_remote_copy(
            src_ref=outgoing.at[at],
            dst_ref=parts.at[at],
            send_sem=part_send_sem.at[at],
            recv_sem=part_recv_sem.at[at],
            device_id=(tile, peer),
            device_id_type=MESH,
        )

    def ship(at, peer):
        outgoing[at] = total[pl.ds(pl.multiple_of(peer * share, share), share), :].astype(
            outgoing.dtype
        )
        exchange(at, peer).start()

    ship(core, across_y)
    ship(1 - core, across_y + 1)
    pl.when(giver)(lambda: giver_half(near_rows))
    pl.when(taker)(lambda: taker_half(near_rows))
    ship(2, peers[2])
    out_ref[...] = total[pl.ds(pl.multiple_of(subset * share, share), share), :]
    exchanges = [exchange(at, peer) for at, peer in enumerate(peers)]

    for quarter in range(quarters):
        send("in", tile, quarter).wait_send()

        @pl.when(middle)
        def _():
            send("out", tile, quarter).wait_send()

        send("x", tile, quarter).wait_send()

    def sent(event, carry):
        for side in range(2):
            each_way(event, side, lambda copy: copy.wait_send(), lambda: None)
        return carry

    lax.fori_loop(0, events, sent, 0)

    for copy in exchanges:
        copy.wait_recv()
    for copy in exchanges:
        copy.wait_send()

    @pl.when(giver)
    def _():
        for copy in lending:
            copy.wait_send()


def keep(array):
    return pltpu.with_memory_space_constraint(array, pltpu.HBM)


def gather_per_device(traces, taps, aperture, counts, time_weights, amplitudes):
    tiles = lax.axis_size("tile")
    subsets = lax.axis_size("trace")
    _, block_count, block_rows, samples = traces.shape
    slots, taus = time_weights.shape[2:4]
    columns = amplitudes.shape[-1]
    chunk_rows = block_count * block_rows // quarters
    share = taus // subsets
    lent_blocks = 4 * block_count // quarters
    vmem = pl.BlockSpec(memory_space=pltpu.VMEM)
    hbm = pl.BlockSpec(memory_space=pl.ANY)
    image, parts = pl.pallas_call(
        migrate_kernel,
        out_shape=(
            jax.ShapeDtypeStruct((share, columns), jnp.float32),
            jax.ShapeDtypeStruct((subsets - 1, share, columns), jnp.bfloat16),
        ),
        in_specs=[hbm] * 6,
        out_specs=(vmem, vmem),
        scratch_shapes=[
            pltpu.VMEM((tiles, quarters, chunk_rows, samples), jnp.bfloat16),
            pltpu.VMEM((slots, taus, samples), jnp.bfloat16),
            pltpu.VMEM((slots, 2, block_rows, columns), jnp.bfloat16),
            pltpu.VMEM((samples, 2 * samples), jnp.bfloat16),
            pltpu.VMEM((taus, columns), jnp.float32),
            pltpu.VMEM((subsets - 1, share, columns), jnp.bfloat16),
            pltpu.SMEM(counts.shape, jnp.int32),
            pltpu.VMEM(aperture.shape, jnp.int32),
            pltpu.VMEM(taps.shape, taps.dtype),
            pltpu.VMEM((8, samples), jnp.float32),
            pltpu.VMEM((8, slots), jnp.int32),
            pltpu.SMEM((8, slots), jnp.int32),
            pltpu.SemaphoreType.DMA((tiles, quarters)),
            pltpu.SemaphoreType.DMA((3, tiles, quarters)),
            pltpu.SemaphoreType.DMA((7,)),
            pltpu.SemaphoreType.DMA((subsets - 1,)),
            pltpu.SemaphoreType.DMA((subsets - 1,)),
            pltpu.SemaphoreType.REGULAR,
            pltpu.SemaphoreType.REGULAR,
            pltpu.VMEM((2, 2, chunk_rows, samples), jnp.bfloat16),
            pltpu.SemaphoreType.DMA((2, 2)),
            pltpu.VMEM((lent_blocks, taus, samples), jnp.bfloat16),
            pltpu.VMEM((lent_blocks, 2, block_rows, columns), jnp.bfloat16),
            pltpu.VMEM((lent_blocks, taus, samples), jnp.bfloat16),
            pltpu.VMEM((lent_blocks, 2, block_rows, columns), jnp.bfloat16),
            pltpu.SemaphoreType.DMA((2,)),
            pltpu.SemaphoreType.DMA((2,)),
            pltpu.VMEM((2, 2 * chunk_rows, samples), jnp.bfloat16),
        ],
        compiler_params=pltpu.CompilerParams(
            collective_id=0, has_side_effects=True, vmem_limit_bytes=48 * 1024 * 1024
        ),
    )(
        keep(counts),
        keep(aperture),
        keep(taps),
        keep(traces.reshape(quarters, chunk_rows, samples)),
        keep(time_weights[0, 0]),
        keep(amplitudes[0, 0]),
    )
    for part in range(subsets - 1):
        image = image + parts[part].astype(jnp.float32)
    return image[None]


def filter_matrix(taps, samples):
    width = taps.shape[1]
    center = (width - 1) // 2
    offset = jnp.arange(samples)[:, None] - jnp.arange(samples)[None, :] + center
    table = (offset[:, :, None] == jnp.arange(width)[None, None, :]).astype(jnp.bfloat16)
    return jnp.einsum("ct,nmt->cnm", taps, table, preferred_element_type=jnp.float32).astype(
        jnp.bfloat16
    )


def exchange_per_device(traces, taps, aperture, counts, time_weights, amplitudes):
    tiles = lax.axis_size("tile")
    myself = lax.axis_index("tile")
    block_count = traces.shape[1]
    samples = traces.shape[3]
    slots = aperture.shape[2]
    capacity = max(2, slots // tiles)
    listing = aperture[0]
    filled = counts[0]
    owners = listing // block_count
    within = listing - owners * block_count
    order = jnp.arange(slots)
    earlier = order[None, :] < order[:, None]
    rank = jnp.sum((owners[:, :, None] == owners[:, None, :]) & earlier[None], axis=2)
    alive_slots = order[None, :] < filled[:, None]
    mine = (owners == myself) & alive_slots
    rank_onehot = (
        (rank[:, :, None] == jnp.arange(capacity)[None, None, :]) & mine[:, :, None]
    ).astype(jnp.bfloat16)
    local_onehot = (within[:, :, None] == jnp.arange(block_count)[None, None, :]).astype(
        jnp.bfloat16
    )
    select = jnp.einsum(
        "ksc,ksl->kcl", rank_onehot, local_onehot, preferred_element_type=jnp.float32
    ).astype(jnp.bfloat16)
    operator = filter_matrix(taps, samples)
    own_owner = lax.dynamic_index_in_dim(owners, myself, 0, keepdims=False)
    own_rank = lax.dynamic_index_in_dim(rank, myself, 0, keepdims=False)
    own_fill = lax.dynamic_index_in_dim(filled, myself, 0, keepdims=False)
    source_slot = own_owner * capacity + own_rank
    arrived_rows = tiles * capacity

    def pick_rows(positions):
        return (positions[:, None] == jnp.arange(arrived_rows)[None, :]).astype(jnp.bfloat16)

    filtered = jnp.einsum(
        "cnm,kbm->kcbn", operator, traces[0], preferred_element_type=jnp.float32
    ).astype(jnp.bfloat16)
    outgoing = jnp.einsum(
        "kcl,lqbn->kcqbn", select, filtered, preferred_element_type=jnp.float32
    ).astype(jnp.bfloat16)
    arrived = lax.all_to_all(outgoing, "tile", split_axis=0, concat_axis=0, tiled=True)
    arrived = arrived.reshape((arrived_rows,) + arrived.shape[2:])

    def fetch(positions):
        return jnp.einsum(
            "gq,qcbn->gcbn", pick_rows(positions), arrived, preferred_element_type=jnp.float32
        ).astype(jnp.bfloat16)

    weights = time_weights[0, 0]
    spread = amplitudes[0, 0]

    def add_group(index, total):
        start = index * group_slots
        positions = lax.dynamic_slice_in_dim(source_slot, start, group_slots, 0)
        blocks = fetch(positions)
        part_weights = lax.dynamic_slice_in_dim(weights, start, group_slots, 0)
        part_spread = lax.dynamic_slice_in_dim(spread, start, group_slots, 0)
        alive = (start + jnp.arange(group_slots) < own_fill).astype(jnp.float32)
        interp = jnp.einsum(
            "gtn,gcbn->gcbt", part_weights, blocks, preferred_element_type=jnp.float32
        )
        interp = (interp * alive[:, None, None, None]).astype(jnp.bfloat16)
        return total + jnp.einsum(
            "gcbt,gcbp->tp", interp, part_spread, preferred_element_type=jnp.float32
        )

    rounds = (own_fill + group_slots - 1) // group_slots
    partial_value = lax.fori_loop(
        0, rounds, add_group, jnp.zeros((weights.shape[1], spread.shape[-1]), jnp.float32)
    )
    image = lax.psum_scatter(partial_value, "trace", scatter_dimension=0, tiled=True)
    return image[None]


def per_device(traces, taps, aperture, counts, time_weights, amplitudes):
    tiles = lax.axis_size("tile")
    every_block = traces.shape[1] * tiles
    quarter = traces.shape[1] // quarters
    gathers = (
        every_block == aperture.shape[2]
        and tiles == 2 * rows_z
        and lax.axis_size("trace") == 4
        and quarter * quarters == traces.shape[1]
    )
    form = gather_per_device if gathers else exchange_per_device
    return form(traces, taps, aperture, counts, time_weights, amplitudes)


def solution(mesh):
    placed = (
        P("trace", "tile", None, None),
        P(),
        P("trace", None, None),
        P("trace", None),
        P("trace", "tile", None, None, None),
        P("trace", "tile", None, None, None, None),
    )
    return jax.shard_map(
        per_device, mesh=mesh, in_specs=placed, out_specs=P("tile", "trace", None), check_vma=False
    )
```
